32 devices in a mesh: rep: 2 (over x), seq: 2 (over y), ctx: 8 (over z, core).
Axes of the slice: x: 2, y: 2, z: 4, core: 2. Of those that a mesh axis runs over, the one named last changes fastest.
Arguments:
- tokens: bfloat16 [4, 1024, 768], P(('rep', 'seq'), 'ctx'), may hold values from -6 to 6
- segments: int32 [4, 1024], P(('rep', 'seq')), may hold values from 0 to 7, never falling along the last dimension, each value on 1 to 768 neighbouring positions
- joined_weight: bfloat16 [768, 2304], P(('seq', 'ctx')), may hold values from -0.21875 to 0.21875
- query_bias: bfloat16 [768], P(('seq', 'ctx')), may hold values from -3 to 3
- value_bias: bfloat16 [768], P(('seq', 'ctx')), may hold values from -0.59765625 to 0.59765625
- output_weight: bfloat16 [768, 768], P(('seq', 'ctx')), may hold values from -0.875 to 0.875
- output_bias: bfloat16 [768], P(('seq', 'ctx')), may hold values from -2 to 2
- first_gain: bfloat16 [768], P(('seq', 'ctx')), may hold values from 0.5 to 1.5
- first_shift: bfloat16 [768], P(('seq', 'ctx')), may hold values from -2 to 2
- widen_weight: bfloat16 [768, 6144], P(('seq', 'ctx')), may hold values from -0.21875 to 0.21875
- widen_bias: bfloat16 [6144], P(('seq', 'ctx')), may hold values from -2 to 2
- narrow_weight: bfloat16 [3072, 768], P(('seq', 'ctx')), may hold values from -0.15625 to 0.15625
- narrow_bias: bfloat16 [768], P(('seq', 'ctx')), may hold values from -2 to 2
- final_gain: bfloat16 [768], P(('seq', 'ctx')), may hold values from 0.5 to 1.5
- final_shift: bfloat16 [768], P(('seq', 'ctx')), may hold values from -2 to 2
- cotangent: bfloat16 [4, 1024, 768], P(('rep', 'seq'), 'ctx'), may hold values from -6 to 6
Outputs:
- layer_output: bfloat16 [4, 1024, 768], P(('rep', 'seq'), 'ctx')
- tokens_grad: float32 [4, 1024, 768], P(('rep', 'seq'), 'ctx')
- joined_weight_grad: float32 [768, 2304], P(('seq', 'ctx'))
- query_bias_grad: float32 [768], P(('seq', 'ctx'))
- value_bias_grad: float32 [768], P(('seq', 'ctx'))
- output_weight_grad: float32 [768, 768], P(('seq', 'ctx'))
- output_bias_grad: float32 [768], P(('seq', 'ctx'))
- first_gain_grad: float32 [768], P(('seq', 'ctx'))
- first_shift_grad: float32 [768], P(('seq', 'ctx'))
- widen_weight_grad: float32 [768, 6144], P(('seq', 'ctx'))
- widen_bias_grad: float32 [6144], P(('seq', 'ctx'))
- narrow_weight_grad: float32 [3072, 768], P(('seq', 'ctx'))
- narrow_bias_grad: float32 [768], P(('seq', 'ctx'))
- final_gain_grad: float32 [768], P(('seq', 'ctx'))
- final_shift_grad: float32 [768], P(('seq', 'ctx'))
The draws below stay inside these ranges and needn't reach their ends.
Inputs may be any that keep to these rules, and one draw needn't show every extreme that they name: `segments`: in each sequence the document ids never fall, each of the 8 documents holds 1 to 768 tokens, and one holds exactly 768.
All inputs are finite; a program needn't handle non-finite values.
Results may differ from the reference program's by a relative error of at most 0.03.
Values may be sent and summed in bfloat16 or wider, within the bound.
No kernel may reach another device: no remote copies, remote signals or barrier semaphores. Data moves between devices by JAX's collectives and lax.ppermute only.
A program may use at most 256 MiB of HBM per device.

```python
import math
import jax
import jax.numpy as jnp
import numpy as np
from jax import lax

D = 768
HEAD_DIM = 64
FF = 3072
DOCS = 8
SEQ_LEN = 1024
SEQS = 4
MOST_DOC = 768


def block_scale(key, shape, cuts, smallest, high):
    level, own = 1.0, jax.random.fold_in(key, 6)
    for axis_at, parts in cuts:
        heights = jnp.exp(jax.random.uniform(jax.random.fold_in(own, axis_at), (parts,), jnp.float32, smallest / len(cuts), high / len(cuts)))
        level = level * jnp.repeat(heights, shape[axis_at] // parts).reshape([-1 if axis == axis_at else 1 for axis in range(len(shape))])
    return level


def length_profile(count, total, limit, slope):
    loads = [(1 << 20) // math.isqrt(standing ** slope) + 1 for standing in range(2, count + 1)]
    spare, given = total - limit - (count - 1), [1] * (count - 1)
    while spare > 0:
        candidates = [i for i in range(count - 1) if given[i] < limit]
        mass, remaining = sum([loads[i] for i in candidates]), spare
        for i in candidates:
            addition = min(limit - given[i], max(1, remaining * loads[i] // mass), spare)
            given[i] = given[i] + addition
            spare = spare - addition
    return np.array([limit] + given)


def ragged_sizes(stream_key, count, total, limit, slope):
    if count == 2:
        one = jax.random.randint(stream_key, (), max(1, total - limit), min(limit, total - 1) + 1)
        return jnp.stack([one, total - one])
    sizes = jnp.asarray(length_profile(count, total, limit, slope), jnp.int32)
    pairs = (count - 1) // 2
    source_of, receiver = sizes[1:1 + 2 * pairs:2], sizes[2:2 + 2 * pairs:2]
    slack = jnp.minimum(source_of - 1, limit - receiver)
    passed = jax.random.randint(jax.random.fold_in(stream_key, 1), (pairs,), 0, 1 << 20) % (slack + 1)
    sizes = sizes.at[1:1 + 2 * pairs:2].set(source_of - passed).at[2:2 + 2 * pairs:2].set(receiver + passed)
    return sizes[jax.random.permutation(jax.random.fold_in(stream_key, 2), count)]


def normal_values(key, extent, scale, most, split=(), kind=jnp.bfloat16):
    entries = jax.random.normal(key, extent, jnp.float32) * scale
    if len(split) > 0:
        entries = block_scale(key, extent, split, -0.22, 0.18) * entries
    return jnp.clip(entries, min=-most, max=most).astype(kind)


def setup_inputs(seed: int = 0) -> dict:
    seeds = jax.random.split(jax.random.key(seed), 17)
    return {
        "tokens": normal_values(seeds[0], (SEQS, SEQ_LEN, D), 1.0, 6.0, ((0, 4), (1, 8))),
        "segments": jax.vmap(lambda own: jnp.searchsorted(jnp.cumsum(ragged_sizes(own, DOCS, SEQ_LEN, MOST_DOC, 2)), jnp.arange(SEQ_LEN), side="right"))(jax.random.split(seeds[1], SEQS)).reshape((SEQS, SEQ_LEN)).astype(jnp.int32),
        "joined_weight": normal_values(seeds[2], (D, 3 * D), D ** -0.5, 0.21875, ((0, 16),)),
        "query_bias": normal_values(seeds[3], (D,), 0.5, 3.0, ((0, 16),)),
        "value_bias": normal_values(seeds[4], (D,), 0.1, 0.59765625, ((0, 16),)),
        "output_weight": normal_values(seeds[5], (D, D), (D // 16) ** -0.5, 0.875, ((0, 16),)),
        "output_bias": normal_values(seeds[6], (D,), 0.3, 2.0, ((0, 16),)),
        "first_gain": jnp.clip(1.0 + 0.1 * jax.random.normal(seeds[7], (D,), jnp.float32), 0.5, 1.5).astype(jnp.bfloat16),
        "first_shift": normal_values(seeds[8], (D,), 0.3, 2.0, ((0, 16),)),
        "widen_weight": normal_values(seeds[9], (D, 2 * FF), D ** -0.5, 0.21875, ((0, 16),)),
        "widen_bias": normal_values(seeds[10], (2 * FF,), 0.3, 2.0, ((0, 16),)),
        "narrow_weight": normal_values(seeds[11], (FF, D), (FF // 2) ** -0.5, 0.15625, ((0, 16),)),
        "narrow_bias": normal_values(seeds[12], (D,), 0.3, 2.0, ((0, 16),)),
        "final_gain": jnp.clip(1.0 + 0.1 * jax.random.normal(seeds[13], (D,), jnp.float32), 0.5, 1.5).astype(jnp.bfloat16),
        "final_shift": normal_values(seeds[14], (D,), 0.3, 2.0, ((0, 16),)),
        "cotangent": normal_values(seeds[15], (SEQS, SEQ_LEN, D), 1.0, 6.0, ((0, 4), (1, 8))),
    }


@jax.custom_vjp
def low(v):
    return lax.optimization_barrier(v.astype(jnp.bfloat16)).astype(jnp.float32)

@jax.custom_vjp
def low_back(v):
    return v

def low_keep(v):
    return (low(v), None)

def low_pass(kept, grad):
    return (grad,)

def back_keep(v):
    return (v, None)

def back_low(kept, grad):
    return (low(grad),)
low.defvjp(low_keep, low_pass)
low_back.defvjp(back_keep, back_low)

def matmul(left, right):
    return jnp.dot(left, right, precision=lax.Precision.HIGHEST, preferred_element_type=jnp.float32)

def normalize(value, gain, shift):
    centre = lax.optimization_barrier(jnp.mean(value, axis=-1, keepdims=True))
    centred = value - centre
    spread = lax.optimization_barrier(jnp.mean(centred * centred, axis=-1, keepdims=True))
    return centred * lax.rsqrt(spread + 1e-06) * gain + shift

def attend(queries, keys, values, segment_row):
    length = keys.shape[0]
    heads = queries.shape[1]
    block = math.gcd(length, 512)
    order = jnp.arange(heads, dtype=jnp.float32) + 1.0
    slopes = jnp.power(2.0, -8.0 * order / heads) * (512.0 / length)
    positions = jnp.arange(length, dtype=jnp.int32)

    def one_block(index):
        begin = (index * block).astype(jnp.int32)
        query_rows = lax.dynamic_slice_in_dim(queries, begin, block, 0)
        query_pos = lax.dynamic_slice_in_dim(positions, begin, block, 0)
        query_seg = lax.dynamic_slice_in_dim(segment_row, begin, block, 0)
        raw = low_back(jnp.einsum('qhd,khd->hqk', query_rows, keys, precision=lax.Precision.HIGHEST))
        distance = jnp.abs(query_pos[:, None] - positions[None, :]).astype(jnp.float32)
        scores = raw - slopes[:, None, None] * distance[None]
        same = (query_seg[:, None] == segment_row[None, :])[None]
        scores = jnp.where(same, scores, -jnp.inf)
        raised = jnp.exp(scores)
        probs = raised / lax.optimization_barrier(jnp.sum(raised, axis=-1, keepdims=True))
        probs = low(probs)
        return jnp.einsum('hqk,khd->qhd', probs, values, precision=lax.Precision.HIGHEST)
    blocks = lax.map(jax.checkpoint(one_block), jnp.arange(length // block, dtype=jnp.int32))
    return blocks.reshape(length, heads * queries.shape[2])

def layer(inputs, segment_row, joined_weight, query_bias, value_bias, output_weight, output_bias, first_gain, first_shift, widen_weight, widen_bias, narrow_weight, narrow_bias, final_gain, final_shift):
    width = inputs.shape[1]
    heads = width // HEAD_DIM
    length = inputs.shape[0]
    joined = matmul(inputs, joined_weight)
    scale = 1.0 / math.sqrt(HEAD_DIM)
    queries = low_back(low((joined[:, :width] + query_bias) * scale))
    keys = low_back(low(joined[:, width:2 * width]))
    values = low_back(low(joined[:, 2 * width:] + value_bias))
    layout = (length, heads, HEAD_DIM)
    mixed = attend(queries.reshape(layout), keys.reshape(layout), values.reshape(layout), segment_row)
    mixed = low_back(low(mixed))
    branch = low_back(matmul(mixed, output_weight) + output_bias)
    first = normalize(inputs + branch, first_gain, first_shift)
    gate_up = low_back(matmul(low(first), widen_weight) + widen_bias)
    hidden = low(jax.nn.gelu(gate_up[:, :FF], approximate=False) * gate_up[:, FF:])
    branch_two = low_back(matmul(hidden, narrow_weight) + narrow_bias)
    return normalize(first + branch_two, final_gain, final_shift)

def reference(tokens, segments, joined_weight, query_bias, value_bias, output_weight, output_bias, first_gain, first_shift, widen_weight, widen_bias, narrow_weight, narrow_bias, final_gain, final_shift, cotangent):
    weights = tuple((w.astype(jnp.float32) for w in (joined_weight, query_bias, value_bias, output_weight, output_bias, first_gain, first_shift, widen_weight, widen_bias, narrow_weight, narrow_bias, final_gain, final_shift)))

    def one_sequence(totals, item):
        inputs, segment_row, upstream = item

        def forward(inputs_full, *params):
            return layer(inputs_full, segment_row, *params)
        result, pull = jax.vjp(forward, inputs.astype(jnp.float32), *weights)
        grads = pull(upstream.astype(jnp.float32))
        totals = tuple((a + b for a, b in zip(totals, grads[1:])))
        return (totals, (result.astype(jnp.bfloat16), grads[0]))
    zeros = tuple((jnp.zeros(w.shape, jnp.float32) for w in weights))
    totals, stacked = lax.scan(one_sequence, zeros, (tokens, segments, cotangent))
    return (stacked[0], stacked[1], totals[0], totals[1], totals[2], totals[3], totals[4], totals[5], totals[6], totals[7], totals[8], totals[9], totals[10], totals[11], totals[12])
```

```python
import math

import jax
import jax.numpy as jnp
from jax import lax
from jax.experimental import pallas as pl
from jax.experimental.pallas import tpu as pltpu
from jax.sharding import PartitionSpec as P

HEAD_DIM = 64
GROUPS = 4
FAR = 1e30
BF = jnp.bfloat16
F32 = jnp.float32


def dot_nn(left, right):
    return lax.dot_general(left, right, (((1,), (0,)), ((), ())), preferred_element_type=F32)


def dot_tn(left, right):
    return lax.dot_general(left, right, (((0,), (0,)), ((), ())), preferred_element_type=F32)


def dot_nt(left, right):
    return lax.dot_general(left, right, (((1,), (1,)), ((), ())), preferred_element_type=F32)


def head_mask(head, cols):
    lane = lax.broadcasted_iota(jnp.int32, (1, cols), 1)
    return (lane >= head * HEAD_DIM) & (lane < (head + 1) * HEAD_DIM)


def only_head(value, head):
    return jnp.where(head_mask(head, value.shape[1]), value, jnp.zeros_like(value))


def each_chunk(count, body):
    if count <= 4:
        for index in range(count):
            body(index)
    else:
        lax.fori_loop(0, count, lambda index, carry: (body(index), carry)[1], 0)


def forward_kernel(slope_ref, q_ref, kv_ref, qinfo_ref, kinfo_ref, out_ref, inv_ref, acc_ref, sum_ref, *, chunk):
    rows, cols = q_ref.shape
    heads = cols // HEAD_DIM
    count = kv_ref.shape[0] // chunk
    acc_ref[...] = jnp.zeros_like(acc_ref)
    sum_ref[...] = jnp.zeros_like(sum_ref)
    q = q_ref[...]
    qpos = qinfo_ref[:, 0:1]
    qseg = qinfo_ref[:, 1:2]
    ones = jnp.ones((8, chunk), BF)

    def step(index):
        begin = index * chunk
        here = pl.ds(begin, chunk)
        keys = kv_ref[here, :cols]
        values = kv_ref[here, cols:]
        kpos = kinfo_ref[0:1, here]
        kseg = kinfo_ref[1:2, here]
        far = jnp.where(qseg == kseg, jnp.abs(qpos - kpos), FAR)
        for head in range(heads):
            scores = dot_nt(only_head(q, head), keys) - slope_ref[head] * far
            raised = jnp.exp(scores).astype(BF)
            sum_ref[head] += dot_nt(ones, raised)
            acc_ref[head] += dot_nn(raised, values)

    each_chunk(count, step)
    total = jnp.zeros((rows, cols), F32)
    for head in range(heads):
        inv = 1.0 / sum_ref[head]
        inv_ref[head] = inv
        column = jnp.transpose(inv)[:, 0:1]
        total = total + only_head(acc_ref[head] * column, head)
    out_ref[...] = total


def attend_forward(slopes, queries, key_value, qinfo, kinfo, interpret=False):
    count, cols = queries.shape
    heads = cols // HEAD_DIM
    keys = key_value.shape[0]
    chunk = math.gcd(keys, 512)
    rows = math.gcd(count, 128)
    whole = lambda shape: pl.BlockSpec(shape, lambda i: tuple(0 for _ in shape))
    return pl.pallas_call(
        lambda *refs: forward_kernel(*refs, chunk=chunk),
        grid=(count // rows,),
        in_specs=[
            pl.BlockSpec(memory_space=pltpu.SMEM),
            pl.BlockSpec((rows, cols), lambda i: (i, 0)),
            whole((keys, 2 * cols)),
            pl.BlockSpec((rows, 2), lambda i: (i, 0)),
            whole((2, keys)),
        ],
        out_specs=[
            pl.BlockSpec((rows, cols), lambda i: (i, 0)),
            pl.BlockSpec((heads, 8, rows), lambda i: (0, 0, i)),
        ],
        out_shape=[
            jax.ShapeDtypeStruct((count, cols), F32),
            jax.ShapeDtypeStruct((heads, 8, count), F32),
        ],
        scratch_shapes=[pltpu.VMEM((heads, rows, cols), F32), pltpu.VMEM((heads, 8, rows), F32)],
        name="attend_forward",
        interpret=interpret,
    )(slopes, queries, key_value, qinfo, kinfo)


def backward_kernel(
    slope_ref, q_ref, do_ref, out_ref, inv_ref, kv_ref, qinfo_ref, kinfo_ref, dq_ref, dkv_ref, acc_ref, *, chunk
):
    rows, cols = q_ref.shape
    heads = cols // HEAD_DIM
    count = kv_ref.shape[0] // chunk
    q = q_ref[...]
    back = do_ref[...]
    product = back.astype(F32) * out_ref[...]
    qpos = qinfo_ref[0:1, :]
    qseg = qinfo_ref[1:2, :]
    acc_ref[...] = jnp.zeros_like(acc_ref)
    row_dots = []
    for head in range(heads):
        chosen = jnp.broadcast_to(head_mask(head, cols), (8, cols)).astype(F32)
        row_dots.append(
            lax.dot_general(
                chosen,
                product,
                (((1,), (1,)), ((), ())),
                precision=lax.Precision.HIGHEST,
                preferred_element_type=F32,
            )[0:1]
        )

    @pl.when(pl.program_id(0) == 0)
    def _():
        dkv_ref[...] = jnp.zeros_like(dkv_ref)

    def step(index):
        begin = index * chunk
        here = pl.ds(begin, chunk)
        keys = kv_ref[here, :cols]
        values = kv_ref[here, cols:]
        kpos = kinfo_ref[here, 0:1]
        kseg = kinfo_ref[here, 1:2]
        far = jnp.where(qseg == kseg, jnp.abs(qpos - kpos), FAR)
        key_part = jnp.zeros((chunk, cols), F32)
        value_part = jnp.zeros((chunk, cols), F32)
        for head in range(heads):
            q_head = only_head(q, head)
            back_head = only_head(back, head)
            scores = dot_nt(keys, q_head) - slope_ref[head] * far
            probs = jnp.exp(scores) * inv_ref[head, 0:1, :]
            prob_back = dot_nt(values, back_head)
            score_back = (probs * (prob_back - row_dots[head])).astype(BF)
            key_part = key_part + dot_nn(score_back, q_head)
            value_part = value_part + dot_nn(probs.astype(BF), back_head)
            acc_ref[head] += dot_tn(score_back, keys)
        dkv_ref[here, :cols] += key_part
        dkv_ref[here, cols:] += value_part

    each_chunk(count, step)
    total = jnp.zeros((rows, cols), F32)
    for head in range(heads):
        total = total + only_head(acc_ref[head], head)
    dq_ref[...] = total


def attend_backward(slopes, queries, back, mixed, inv, key_value, qinfo, kinfo, interpret=False):
    count, cols = queries.shape
    heads = cols // HEAD_DIM
    keys = key_value.shape[0]
    chunk = math.gcd(keys, 512)
    rows = math.gcd(count, 128)
    whole = lambda shape: pl.BlockSpec(shape, lambda i: tuple(0 for _ in shape))
    by_row = pl.BlockSpec((rows, cols), lambda i: (i, 0))
    return pl.pallas_call(
        lambda *refs: backward_kernel(*refs, chunk=chunk),
        grid=(count // rows,),
        in_specs=[
            pl.BlockSpec(memory_space=pltpu.SMEM),
            by_row,
            by_row,
            by_row,
            pl.BlockSpec((heads, 8, rows), lambda i: (0, 0, i)),
            whole((keys, 2 * cols)),
            pl.BlockSpec((2, rows), lambda i: (0, i)),
            whole((keys, 2)),
        ],
        out_specs=[by_row, whole((keys, 2 * cols))],
        out_shape=[
            jax.ShapeDtypeStruct((count, cols), F32),
            jax.ShapeDtypeStruct((keys, 2 * cols), F32),
        ],
        scratch_shapes=[pltpu.VMEM((heads, rows, cols), F32)],
        name="attend_backward",
        interpret=interpret,
    )(slopes, queries, back, mixed, inv, key_value, qinfo, kinfo)


def norm_stats(value):
    centre = jnp.mean(value, axis=-1, keepdims=True)
    centred = value - centre
    spread = jnp.mean(centred * centred, axis=-1, keepdims=True)
    root = lax.rsqrt(spread + 1e-06)
    return centred * root, root


def norm_back(unit, root, gain, back):
    scaled = back * gain
    return root * (
        scaled
        - jnp.mean(scaled, axis=-1, keepdims=True)
        - unit * jnp.mean(scaled * unit, axis=-1, keepdims=True)
    )


def after(value, *others):
    return lax.optimization_barrier((value,) + others)[0]


class Layout:
    def __init__(self):
        self.size = lax.axis_size("ctx")
        self.members = self.size // GROUPS
        index = lax.axis_index("ctx")
        self.group = index // self.members
        self.member = index % self.members
        self.seq = lax.axis_index("seq")
        self.inner = [
            [g * self.members + m for m in range(self.members)] for g in range(GROUPS)
        ]

    def shift(self, value, steps):
        n, r = self.size, self.members
        return lax.ppermute(value, "ctx", [(i, (i + steps * r) % n) for i in range(n)])

    def swap(self, value, axis):
        return lax.ppermute(value, axis, [(0, 1), (1, 0)])

    def gather(self, value):
        return [value] + [self.shift(value, k) for k in range(1, GROUPS)]

    def scatter_sum(self, parts):
        total = parts[0]
        for k in range(1, GROUPS):
            total = total + self.shift(parts[k].astype(BF), -k).astype(F32)
        return total

    def exchange(self, pieces):
        own = lax.dynamic_index_in_dim(pieces, self.group, 0, keepdims=False)
        out = [own]
        for k in range(1, GROUPS):
            target = (self.group + k) % GROUPS
            out.append(
                self.shift(lax.dynamic_index_in_dim(pieces, target, 0, keepdims=False), k)
            )
        return out

    def ordered(self, relative):
        line = [relative[0], relative[3], relative[2], relative[1]]
        twice = jnp.stack(line + line[:3])
        return lax.dynamic_slice_in_dim(twice, (GROUPS - self.group) % GROUPS, GROUPS, 0)

    def both_seq(self, value):
        other = self.swap(value, "seq")
        first = self.seq == 0
        return jnp.stack([jnp.where(first, value, other), jnp.where(first, other, value)])

    def partner(self, value):
        return lax.ppermute(
            value, "ctx", [(i, i ^ 1) for i in range(self.size)]
        )

    def all_members(self, value, axis):
        if self.members == 2:
            other = self.partner(value)
            first = self.member == 0
            return jnp.stack(
                [jnp.where(first, value, other), jnp.where(first, other, value)], axis
            )
        out = lax.all_gather(value, "ctx", axis_index_groups=self.inner)
        return jnp.moveaxis(out, 0, axis)

    def member_sum(self, pieces):
        if self.members == 2:
            keep = lax.dynamic_index_in_dim(pieces, self.member, 0, keepdims=False)
            give = lax.dynamic_index_in_dim(pieces, 1 - self.member, 0, keepdims=False)
            return keep + self.partner(give.astype(BF)).astype(F32)
        got = lax.all_to_all(
            pieces.astype(BF), "ctx", 0, 0, axis_index_groups=self.inner, tiled=True
        )
        return jnp.sum(got.astype(F32), axis=0)

    def seq_sum(self, pieces):
        keep = lax.dynamic_index_in_dim(pieces, self.seq, 0, keepdims=False)
        give = lax.dynamic_index_in_dim(pieces, 1 - self.seq, 0, keepdims=False)
        return keep + self.swap(give.astype(BF), "seq").astype(F32)

    def rep_sum(self, value):
        low = value.astype(BF)
        return low.astype(F32) + self.swap(low, "rep").astype(F32)


def on_device(
    tokens,
    segments,
    joined_weight,
    query_bias,
    value_bias,
    output_weight,
    output_bias,
    first_gain,
    first_shift,
    widen_weight,
    widen_bias,
    narrow_weight,
    narrow_bias,
    final_gain,
    final_shift,
    cotangent,
):
    at = Layout()
    n, r = at.size, at.members
    rows, width = tokens.shape[1:]
    heads = width // HEAD_DIM
    near_heads = heads // GROUPS
    cols = near_heads * HEAD_DIM
    kb = joined_weight.shape[0]
    ff_own = narrow_weight.shape[0]
    ff = ff_own * 2 * n
    quarter = ff // GROUPS
    span = r * ff_own
    seg_row = segments[0]
    length = seg_row.shape[0]
    scale = 1.0 / math.sqrt(HEAD_DIM)
    inputs = tokens[0]

    x_rel = at.gather(inputs)
    x_four = jnp.concatenate(x_rel, axis=0)

    small = jnp.concatenate(
        [
            query_bias,
            value_bias,
            output_bias,
            first_gain,
            first_shift,
            narrow_bias,
            final_gain,
            final_shift,
            widen_bias,
        ]
    )[None]
    small_all = at.all_members(at.both_seq(at.ordered(at.gather(small))), 2)
    small_all = small_all.reshape(2 * n, -1).astype(F32)

    def vector(place):
        return small_all[:, place * kb : (place + 1) * kb].reshape(width)

    b_query, b_value, b_output, g_first, s_first, b_narrow, g_final, s_final = (
        vector(place) for place in range(8)
    )
    b_widen = lax.dynamic_index_in_dim(
        small_all[:, 8 * kb :].reshape(2, 2, GROUPS, span), at.group, 2, keepdims=False
    ).reshape(2 * quarter)
    b_query = lax.dynamic_index_in_dim(b_query.reshape(GROUPS, cols), at.group, 0, keepdims=False)
    b_value = lax.dynamic_index_in_dim(b_value.reshape(GROUPS, cols), at.group, 0, keepdims=False)

    joined_cut = jnp.transpose(joined_weight.reshape(kb, 3, GROUPS, cols), (2, 0, 1, 3)).reshape(
        GROUPS, kb, 3 * cols
    )
    w_joined = at.all_members(at.both_seq(at.ordered(at.exchange(joined_cut))), 2).reshape(
        width, 3 * cols
    )

    output_low = after(output_weight, x_four)
    out_rel = at.ordered(at.gather(output_low)).reshape(GROUPS * kb, width)
    both = at.both_seq(jnp.concatenate([out_rel, narrow_weight], axis=0))
    both = at.all_members(both, 1)
    w_output = jnp.transpose(
        both[:, :, : GROUPS * kb].reshape(2, r, GROUPS, kb, width), (0, 2, 1, 3, 4)
    ).reshape(width, width)
    w_narrow = both[:, :, GROUPS * kb :].reshape(quarter, width)

    widen_cut = jnp.transpose(
        after(widen_weight, x_four).reshape(kb, 4, GROUPS, span), (2, 0, 1, 3)
    ).reshape(GROUPS, kb, 2 * quarter)
    w_widen = at.all_members(at.both_seq(at.ordered(at.exchange(widen_cut))), 2).reshape(
        width, 2 * quarter
    )

    lanes = jnp.arange(rows, dtype=jnp.int32)
    near = (at.group - jnp.arange(GROUPS, dtype=jnp.int32)) % GROUPS

    def places(member):
        return ((near * r + member)[:, None] * rows + lanes[None]).reshape(-1)

    if r == 2:
        key_members = jnp.stack([at.member, 1 - at.member])
    else:
        key_members = jnp.arange(r, dtype=jnp.int32)
    query_pos = places(at.member)
    key_pos = jnp.concatenate([places(key_members[i]) for i in range(r)])
    query_seg = jnp.take(seg_row, query_pos)
    key_seg = jnp.take(seg_row, key_pos)
    q_info = jnp.stack([query_pos, query_seg]).astype(F32)
    k_info = jnp.stack([key_pos, key_seg]).astype(F32)
    order_heads = at.group * near_heads + jnp.arange(near_heads, dtype=jnp.int32)
    slopes = jnp.power(2.0, -8.0 * (order_heads.astype(F32) + 1.0) / heads) * (512.0 / length)

    joined = dot_nn(x_four, w_joined)
    queries = ((joined[:, :cols] + b_query) * scale).astype(BF)
    kv_own = jnp.concatenate(
        [joined[:, cols : 2 * cols], joined[:, 2 * cols :] + b_value], axis=1
    ).astype(BF)
    if r == 2:
        key_value = jnp.concatenate([kv_own, at.partner(kv_own)], axis=0)
    else:
        key_value = at.all_members(kv_own, 0).reshape(-1, 2 * cols)
    mixed_near, inv = attend_forward(slopes, queries, key_value, jnp.transpose(q_info), k_info)
    mixed_low = mixed_near.astype(BF).reshape(GROUPS, rows, cols)
    mixed_rel = [mixed_low[0]] + [at.shift(mixed_low[k], -k) for k in range(1, GROUPS)]
    mixed_rel = [mixed_rel[0], mixed_rel[3], mixed_rel[2], mixed_rel[1]]
    mixed = jnp.transpose(at.ordered(mixed_rel), (1, 0, 2)).reshape(rows, width)

    first_in = inputs.astype(F32) + dot_nn(mixed, w_output) + b_output
    first_unit, first_root = norm_stats(first_in)
    first = first_unit * g_first + s_first
    first_low = first.astype(BF)

    first_four = jnp.concatenate(at.gather(first_low), axis=0)
    gate_up = dot_nn(first_four, w_widen) + b_widen
    gate, up = gate_up[:, :quarter], gate_up[:, quarter:]
    phi_big = 0.5 * (1.0 + lax.erf(gate * math.sqrt(0.5)))
    gelu = gate * phi_big
    slope_gate = phi_big + gate * jnp.exp(-0.5 * gate * gate) * (1.0 / math.sqrt(2.0 * math.pi))
    hidden = (gelu * up).astype(BF)
    final_part = dot_nn(hidden, w_narrow).reshape(GROUPS, rows, width)
    final_in = first + at.scatter_sum([final_part[k] for k in range(GROUPS)]) + b_narrow
    final_unit, final_root = norm_stats(final_in)
    result = final_unit * g_final + s_final

    upstream = cotangent[0].astype(F32)
    final_back = norm_back(final_unit, final_root, g_final, upstream)
    final_gain_grad = jnp.sum(upstream * final_unit, axis=0)
    final_shift_grad = jnp.sum(upstream, axis=0)
    narrow_back = final_back.astype(BF)
    narrow_bias_grad = jnp.sum(narrow_back.astype(F32), axis=0)
    back_four = jnp.concatenate(at.gather(narrow_back), axis=0)
    hidden_back = dot_nt(back_four, w_narrow)
    widen_back = jnp.concatenate(
        [hidden_back * up * slope_gate, hidden_back * gelu], axis=1
    ).astype(BF)
    first_part = dot_nt(widen_back, w_widen).reshape(GROUPS, rows, width)
    first_back = final_back + at.scatter_sum([first_part[k] for k in range(GROUPS)])
    narrow_grad = dot_tn(hidden, back_four)
    widen_grad = dot_tn(first_four, widen_back)
    widen_bias_grad = jnp.sum(widen_back.astype(F32), axis=0)

    attn_back = norm_back(first_unit, first_root, g_first, first_back)
    first_gain_grad = jnp.sum(first_back * first_unit, axis=0)
    first_shift_grad = jnp.sum(first_back, axis=0)
    output_back = attn_back.astype(BF)
    output_bias_grad = jnp.sum(output_back.astype(F32), axis=0)
    output_grad = dot_tn(mixed, output_back)
    mixed_back = dot_nt(output_back, w_output).astype(BF)
    mixed_back = jnp.transpose(mixed_back.reshape(rows, GROUPS, cols), (1, 0, 2))
    back_near = jnp.concatenate(at.exchange(mixed_back), axis=0)

    query_sum, kv_sum = attend_backward(
        slopes, queries, back_near, mixed_near, inv, key_value, q_info, jnp.transpose(k_info)
    )
    if r == 2:
        half = kv_sum.shape[0] // 2
        kv_back = kv_sum[:half] + at.partner(kv_sum[half:].astype(BF)).astype(F32)
    else:
        kv_back = at.member_sum(kv_sum.reshape(r, -1, 2 * cols))
    query_low = query_sum.astype(BF)
    query_scaled = (query_low.astype(F32) * scale).astype(BF)
    joined_back = jnp.concatenate([query_scaled, kv_back.astype(BF)], axis=1)
    tokens_part = dot_nt(joined_back, w_joined).reshape(GROUPS, rows, width)
    tokens_grad = attn_back + at.scatter_sum([tokens_part[k] for k in range(GROUPS)])
    joined_grad = dot_tn(x_four, joined_back)
    near_bias = jnp.sum(joined_back.astype(F32), axis=0)
    query_bias_grad = near_bias[:cols]
    value_bias_grad = near_bias[2 * cols :]

    narrow_sum = at.member_sum(jnp.transpose(narrow_grad.reshape(2, r, ff_own, width), (1, 0, 2, 3)))
    narrow_total = at.rep_sum(at.seq_sum(narrow_sum))

    def to_rows(grad):
        pieces = jnp.transpose(grad.reshape(2, GROUPS, r, kb, -1), (2, 0, 1, 3, 4))
        mine = at.rep_sum(at.seq_sum(at.member_sum(pieces))).astype(BF)
        return at.ordered(at.exchange(mine))

    widen_total = jnp.transpose(
        to_rows(widen_grad).reshape(GROUPS, kb, 4, span), (1, 2, 0, 3)
    ).reshape(kb, 2 * ff)
    joined_total = jnp.transpose(
        to_rows(joined_grad).reshape(GROUPS, kb, 3, cols), (1, 2, 0, 3)
    ).reshape(kb, 3 * width)

    def spread(vector, parts):
        wide = jnp.zeros((parts, GROUPS, vector.shape[0] // parts), F32)
        return lax.dynamic_update_slice_in_dim(
            wide, vector.reshape(parts, 1, -1), at.group, 1
        ).reshape(-1)

    vectors = [
        spread(query_bias_grad, 1),
        spread(value_bias_grad, 1),
        output_bias_grad,
        first_gain_grad,
        first_shift_grad,
        narrow_bias_grad,
        final_gain_grad,
        final_shift_grad,
    ]
    row = jnp.concatenate(
        [item.reshape(2 * n, kb) for item in vectors]
        + [spread(widen_bias_grad, 4).reshape(2 * n, 8 * kb)],
        axis=1,
    )
    row = jnp.pad(row[:, None, :], ((0, 0), (0, 15), (0, width - 16 * kb)))
    packed = jnp.concatenate([output_grad.reshape(2 * n, kb, width), row], axis=1)
    packed = jnp.transpose(packed.reshape(2, GROUPS, r, kb + 16, width), (2, 0, 1, 3, 4))
    packed = at.seq_sum(at.member_sum(packed)).astype(BF)
    packed = at.exchange(packed)
    packed = sum(item.astype(F32) for item in packed[1:]) + packed[0].astype(F32)
    packed = at.rep_sum(packed)
    output_total = packed[:kb]
    last = packed[kb]

    def owned(place):
        return last[place * kb : (place + 1) * kb]

    return (
        result.astype(BF)[None],
        tokens_grad[None],
        joined_total.astype(F32),
        owned(0),
        owned(1),
        output_total,
        owned(2),
        owned(3),
        owned(4),
        widen_total.astype(F32),
        last[8 * kb : 16 * kb],
        narrow_total,
        owned(5),
        owned(6),
        owned(7),
    )


def solution(mesh):
    tokens = P(("rep", "seq"), "ctx", None)
    matrix = P(("seq", "ctx"), None)
    vector = P(("seq", "ctx"))
    return jax.shard_map(
        on_device,
        mesh=mesh,
        in_specs=(
            tokens,
            P(("rep", "seq"), None),
            matrix,
            vector,
            vector,
            matrix,
            vector,
            vector,
            vector,
            matrix,
            vector,
            matrix,
            vector,
            vector,
            vector,
            tokens,
        ),
        out_specs=(
            tokens,
            tokens,
            matrix,
            vector,
            vector,
            matrix,
            vector,
            vector,
            vector,
            matrix,
            vector,
            matrix,
            vector,
            vector,
            vector,
        ),
        check_vma=False,
    )
```

```python
import math

import jax
import jax.numpy as jnp
from jax import lax
from jax.experimental import pallas as pl
from jax.experimental.pallas import tpu as pltpu
from jax.sharding import PartitionSpec as P

HEAD_DIM = 64
GROUPS = 4
FAR = 1e30
BF = jnp.bfloat16
F32 = jnp.float32


def dot_nn(left, right):
    return lax.dot_general(left, right, (((1,), (0,)), ((), ())), preferred_element_type=F32)


def dot_tn(left, right):
    return lax.dot_general(left, right, (((0,), (0,)), ((), ())), preferred_element_type=F32)


def dot_nt(left, right):
    return lax.dot_general(left, right, (((1,), (1,)), ((), ())), preferred_element_type=F32)


def head_mask(head, cols):
    lane = lax.broadcasted_iota(jnp.int32, (1, cols), 1)
    return (lane >= head * HEAD_DIM) & (lane < (head + 1) * HEAD_DIM)


def only_head(value, head):
    return jnp.where(head_mask(head, value.shape[1]), value, jnp.zeros_like(value))


def each_chunk(count, body):
    if count <= 4:
        for index in range(count):
            body(index)
    else:
        lax.fori_loop(0, count, lambda index, carry: (body(index), carry)[1], 0)


def forward_kernel(slope_ref, q_ref, kv_ref, qinfo_ref, kinfo_ref, out_ref, inv_ref, acc_ref, sum_ref, *, chunk):
    rows, cols = q_ref.shape
    heads = cols // HEAD_DIM
    count = kv_ref.shape[0] // chunk
    acc_ref[...] = jnp.zeros_like(acc_ref)
    sum_ref[...] = jnp.zeros_like(sum_ref)
    q = q_ref[...]
    qpos = qinfo_ref[:, 0:1]
    qseg = qinfo_ref[:, 1:2]
    ones = jnp.ones((8, chunk), BF)

    def step(index):
        begin = index * chunk
        here = pl.ds(begin, chunk)
        keys = kv_ref[here, :cols]
        values = kv_ref[here, cols:]
        kpos = kinfo_ref[0:1, here]
        kseg = kinfo_ref[1:2, here]
        far = jnp.where(qseg == kseg, jnp.abs(qpos - kpos), FAR)
        for head in range(heads):
            scores = dot_nt(only_head(q, head), keys) - slope_ref[head] * far
            raised = jnp.exp(scores).astype(BF)
            sum_ref[head] += dot_nt(ones, raised)
            acc_ref[head] += dot_nn(raised, values)

    each_chunk(count, step)
    total = jnp.zeros((rows, cols), F32)
    for head in range(heads):
        inv = 1.0 / sum_ref[head]
        inv_ref[head] = inv
        column = jnp.transpose(inv)[:, 0:1]
        total = total + only_head(acc_ref[head] * column, head)
    out_ref[...] = total


def attend_forward(slopes, queries, key_value, qinfo, kinfo, interpret=False):
    count, cols = queries.shape
    heads = cols // HEAD_DIM
    keys = key_value.shape[0]
    chunk = math.gcd(keys, 512)
    rows = math.gcd(count, 128)
    whole = lambda shape: pl.BlockSpec(shape, lambda i: tuple(0 for _ in shape))
    return pl.pallas_call(
        lambda *refs: forward_kernel(*refs, chunk=chunk),
        grid=(count // rows,),
        in_specs=[
            pl.BlockSpec(memory_space=pltpu.SMEM),
            pl.BlockSpec((rows, cols), lambda i: (i, 0)),
            whole((keys, 2 * cols)),
            pl.BlockSpec((rows, 2), lambda i: (i, 0)),
            whole((2, keys)),
        ],
        out_specs=[
            pl.BlockSpec((rows, cols), lambda i: (i, 0)),
            pl.BlockSpec((heads, 8, rows), lambda i: (0, 0, i)),
        ],
        out_shape=[
            jax.ShapeDtypeStruct((count, cols), F32),
            jax.ShapeDtypeStruct((heads, 8, count), F32),
        ],
        scratch_shapes=[pltpu.VMEM((heads, rows, cols), F32), pltpu.VMEM((heads, 8, rows), F32)],
        name="attend_forward",
        interpret=interpret,
    )(slopes, queries, key_value, qinfo, kinfo)


def backward_kernel(
    slope_ref, q_ref, do_ref, out_ref, inv_ref, kv_ref, qinfo_ref, kinfo_ref, dq_ref, dkv_ref, acc_ref, *, chunk
):
    rows, cols = q_ref.shape
    heads = cols // HEAD_DIM
    count = kv_ref.shape[0] // chunk
    q = q_ref[...]
    back = do_ref[...]
    product = back.astype(F32) * out_ref[...]
    qpos = qinfo_ref[0:1, :]
    qseg = qinfo_ref[1:2, :]
    acc_ref[...] = jnp.zeros_like(acc_ref)
    row_dots = []
    for head in range(heads):
        chosen = jnp.broadcast_to(head_mask(head, cols), (8, cols)).astype(F32)
        row_dots.append(
            lax.dot_general(
                chosen,
                product,
                (((1,), (1,)), ((), ())),
                precision=lax.Precision.HIGHEST,
                preferred_element_type=F32,
            )[0:1]
        )

    @pl.when(pl.program_id(0) == 0)
    def _():
        dkv_ref[...] = jnp.zeros_like(dkv_ref)

    def step(index):
        begin = index * chunk
        here = pl.ds(begin, chunk)
        keys = kv_ref[here, :cols]
        values = kv_ref[here, cols:]
        kpos = kinfo_ref[here, 0:1]
        kseg = kinfo_ref[here, 1:2]
        far = jnp.where(qseg == kseg, jnp.abs(qpos - kpos), FAR)
        key_part = jnp.zeros((chunk, cols), F32)
        value_part = jnp.zeros((chunk, cols), F32)
        for head in range(heads):
            q_head = only_head(q, head)
            back_head = only_head(back, head)
            scores = dot_nt(keys, q_head) - slope_ref[head] * far
            probs = jnp.exp(scores) * inv_ref[head, 0:1, :]
            prob_back = dot_nt(values, back_head)
            score_back = (probs * (prob_back - row_dots[head])).astype(BF)
            key_part = key_part + dot_nn(score_back, q_head)
            value_part = value_part + dot_nn(probs.astype(BF), back_head)
            acc_ref[head] += dot_tn(score_back, keys)
        dkv_ref[here, :cols] += key_part
        dkv_ref[here, cols:] += value_part

    each_chunk(count, step)
    total = jnp.zeros((rows, cols), F32)
    for head in range(heads):
        total = total + only_head(acc_ref[head], head)
    dq_ref[...] = total


def attend_backward(slopes, queries, back, mixed, inv, key_value, qinfo, kinfo, interpret=False):
    count, cols = queries.shape
    heads = cols // HEAD_DIM
    keys = key_value.shape[0]
    chunk = math.gcd(keys, 512)
    rows = math.gcd(count, 128)
    whole = lambda shape: pl.BlockSpec(shape, lambda i: tuple(0 for _ in shape))
    by_row = pl.BlockSpec((rows, cols), lambda i: (i, 0))
    return pl.pallas_call(
        lambda *refs: backward_kernel(*refs, chunk=chunk),
        grid=(count // rows,),
        in_specs=[
            pl.BlockSpec(memory_space=pltpu.SMEM),
            by_row,
            by_row,
            by_row,
            pl.BlockSpec((heads, 8, rows), lambda i: (0, 0, i)),
            whole((keys, 2 * cols)),
            pl.BlockSpec((2, rows), lambda i: (0, i)),
            whole((keys, 2)),
        ],
        out_specs=[by_row, whole((keys, 2 * cols))],
        out_shape=[
            jax.ShapeDtypeStruct((count, cols), F32),
            jax.ShapeDtypeStruct((keys, 2 * cols), F32),
        ],
        scratch_shapes=[pltpu.VMEM((heads, rows, cols), F32)],
        name="attend_backward",
        interpret=interpret,
    )(slopes, queries, back, mixed, inv, key_value, qinfo, kinfo)


def norm_stats(value):
    centre = jnp.mean(value, axis=-1, keepdims=True)
    centred = value - centre
    spread = jnp.mean(centred * centred, axis=-1, keepdims=True)
    root = lax.rsqrt(spread + 1e-06)
    return centred * root, root


def norm_back(unit, root, gain, back):
    scaled = back * gain
    return root * (
        scaled
        - jnp.mean(scaled, axis=-1, keepdims=True)
        - unit * jnp.mean(scaled * unit, axis=-1, keepdims=True)
    )


def after(value, *others):
    return lax.optimization_barrier((value,) + others)[0]


class Layout:
    def __init__(self):
        self.size = lax.axis_size("ctx")
        self.members = self.size // GROUPS
        index = lax.axis_index("ctx")
        self.group = index // self.members
        self.member = index % self.members
        self.seq = lax.axis_index("seq")
        self.rep = lax.axis_index("rep")
        self.inner = [
            [g * self.members + m for m in range(self.members)] for g in range(GROUPS)
        ]

    def shift(self, value, steps):
        n, r = self.size, self.members
        return lax.ppermute(value, "ctx", [(i, (i + steps * r) % n) for i in range(n)])

    def swap(self, value, axis):
        return lax.ppermute(value, axis, [(0, 1), (1, 0)])

    def gather(self, value):
        return [value] + [self.shift(value, k) for k in range(1, GROUPS)]

    def scatter_sum(self, parts):
        total = parts[0]
        for k in range(1, GROUPS):
            total = total + self.shift(parts[k].astype(BF), -k).astype(F32)
        return total

    def exchange(self, pieces):
        own = lax.dynamic_index_in_dim(pieces, self.group, 0, keepdims=False)
        out = [own]
        for k in range(1, GROUPS):
            target = (self.group + k) % GROUPS
            out.append(
                self.shift(lax.dynamic_index_in_dim(pieces, target, 0, keepdims=False), k)
            )
        return out

    def ordered(self, relative):
        line = [relative[0], relative[3], relative[2], relative[1]]
        twice = jnp.stack(line + line[:3])
        return lax.dynamic_slice_in_dim(twice, (GROUPS - self.group) % GROUPS, GROUPS, 0)

    def both_seq(self, value):
        other = self.swap(value, "seq")
        first = self.seq == 0
        return jnp.stack([jnp.where(first, value, other), jnp.where(first, other, value)])

    def partner(self, value):
        return lax.ppermute(
            value, "ctx", [(i, i ^ 1) for i in range(self.size)]
        )

    def all_members(self, value, axis):
        if self.members == 2:
            other = self.partner(value)
            first = self.member == 0
            return jnp.stack(
                [jnp.where(first, value, other), jnp.where(first, other, value)], axis
            )
        out = lax.all_gather(value, "ctx", axis_index_groups=self.inner)
        return jnp.moveaxis(out, 0, axis)

    def member_sum(self, pieces):
        if self.members == 2:
            keep = lax.dynamic_index_in_dim(pieces, self.member, 0, keepdims=False)
            give = lax.dynamic_index_in_dim(pieces, 1 - self.member, 0, keepdims=False)
            return keep + self.partner(give.astype(BF)).astype(F32)
        got = lax.all_to_all(
            pieces.astype(BF), "ctx", 0, 0, axis_index_groups=self.inner, tiled=True
        )
        return jnp.sum(got.astype(F32), axis=0)

    def seq_sum(self, pieces):
        keep = lax.dynamic_index_in_dim(pieces, self.seq, 0, keepdims=False)
        give = lax.dynamic_index_in_dim(pieces, 1 - self.seq, 0, keepdims=False)
        return keep + self.swap(give.astype(BF), "seq").astype(F32)

    def rep_sum(self, value):
        low = value.astype(BF)
        return low.astype(F32) + self.swap(low, "rep").astype(F32)


def on_device(
    tokens,
    segments,
    joined_weight,
    query_bias,
    value_bias,
    output_weight,
    output_bias,
    first_gain,
    first_shift,
    widen_weight,
    widen_bias,
    narrow_weight,
    narrow_bias,
    final_gain,
    final_shift,
    cotangent,
):
    at = Layout()
    n, r = at.size, at.members
    rows, width = tokens.shape[1:]
    heads = width // HEAD_DIM
    near_heads = heads // GROUPS
    cols = near_heads * HEAD_DIM
    kb = joined_weight.shape[0]
    ff_own = narrow_weight.shape[0]
    ff = ff_own * 2 * n
    quarter = ff // GROUPS
    span = r * ff_own
    seg_row = segments[0]
    length = seg_row.shape[0]
    scale = 1.0 / math.sqrt(HEAD_DIM)
    inputs = tokens[0]

    x_rel = at.gather(inputs)
    x_four = jnp.concatenate(x_rel, axis=0)

    small = jnp.concatenate(
        [
            query_bias,
            value_bias,
            output_bias,
            first_gain,
            first_shift,
            narrow_bias,
            final_gain,
            final_shift,
            widen_bias,
        ]
    )[None]
    small_all = at.all_members(at.both_seq(at.ordered(at.gather(small))), 2)
    small_all = small_all.reshape(2 * n, -1).astype(F32)

    def vector(place):
        return small_all[:, place * kb : (place + 1) * kb].reshape(width)

    b_query, b_value, b_output, g_first, s_first, b_narrow, g_final, s_final = (
        vector(place) for place in range(8)
    )
    b_widen = lax.dynamic_index_in_dim(
        small_all[:, 8 * kb :].reshape(2, 2, GROUPS, span), at.group, 2, keepdims=False
    ).reshape(2 * quarter)
    b_query = lax.dynamic_index_in_dim(b_query.reshape(GROUPS, cols), at.group, 0, keepdims=False)
    b_value = lax.dynamic_index_in_dim(b_value.reshape(GROUPS, cols), at.group, 0, keepdims=False)

    joined_cut = jnp.transpose(joined_weight.reshape(kb, 3, GROUPS, cols), (2, 0, 1, 3)).reshape(
        GROUPS, kb, 3 * cols
    )
    w_joined = at.all_members(at.both_seq(at.ordered(at.exchange(joined_cut))), 2).reshape(
        width, 3 * cols
    )

    output_low = after(output_weight, x_four)
    out_rel = at.ordered(at.gather(output_low)).reshape(GROUPS * kb, width)
    both = at.both_seq(jnp.concatenate([out_rel, narrow_weight], axis=0))
    both = at.all_members(both, 1)
    w_output = jnp.transpose(
        both[:, :, : GROUPS * kb].reshape(2, r, GROUPS, kb, width), (0, 2, 1, 3, 4)
    ).reshape(width, width)
    w_narrow = both[:, :, GROUPS * kb :].reshape(quarter, width)

    widen_cut = jnp.transpose(
        after(widen_weight, x_four).reshape(kb, 4, GROUPS, span), (2, 0, 1, 3)
    ).reshape(GROUPS, kb, 2 * quarter)
    w_widen = at.all_members(at.both_seq(at.ordered(at.exchange(widen_cut))), 2).reshape(
        width, 2 * quarter
    )

    lanes = jnp.arange(rows, dtype=jnp.int32)
    near = (at.group - jnp.arange(GROUPS, dtype=jnp.int32)) % GROUPS

    def places(member):
        return ((near * r + member)[:, None] * rows + lanes[None]).reshape(-1)

    if r == 2:
        key_members = jnp.stack([at.member, 1 - at.member])
    else:
        key_members = jnp.arange(r, dtype=jnp.int32)
    query_pos = places(at.member)
    key_pos = jnp.concatenate([places(key_members[i]) for i in range(r)])
    query_seg = jnp.take(seg_row, query_pos)
    key_seg = jnp.take(seg_row, key_pos)
    q_info = jnp.stack([query_pos, query_seg]).astype(F32)
    k_info = jnp.stack([key_pos, key_seg]).astype(F32)
    order_heads = at.group * near_heads + jnp.arange(near_heads, dtype=jnp.int32)
    slopes = jnp.power(2.0, -8.0 * (order_heads.astype(F32) + 1.0) / heads) * (512.0 / length)

    joined = dot_nn(x_four, w_joined)
    queries = ((joined[:, :cols] + b_query) * scale).astype(BF)
    kv_own = jnp.concatenate(
        [joined[:, cols : 2 * cols], joined[:, 2 * cols :] + b_value], axis=1
    ).astype(BF)
    if r == 2:
        key_value = jnp.concatenate([kv_own, at.partner(kv_own)], axis=0)
    else:
        key_value = at.all_members(kv_own, 0).reshape(-1, 2 * cols)
    mixed_near, inv = attend_forward(slopes, queries, key_value, jnp.transpose(q_info), k_info)
    mixed_low = mixed_near.astype(BF).reshape(GROUPS, rows, cols)
    mixed_rel = [mixed_low[0]] + [at.shift(mixed_low[k], -k) for k in range(1, GROUPS)]
    mixed_rel = [mixed_rel[0], mixed_rel[3], mixed_rel[2], mixed_rel[1]]
    mixed = jnp.transpose(at.ordered(mixed_rel), (1, 0, 2)).reshape(rows, width)

    first_in = inputs.astype(F32) + dot_nn(mixed, w_output) + b_output
    first_unit, first_root = norm_stats(first_in)
    first = first_unit * g_first + s_first
    first_low = first.astype(BF)

    first_four = jnp.concatenate(at.gather(first_low), axis=0)
    gate_up = dot_nn(first_four, w_widen) + b_widen
    gate, up = gate_up[:, :quarter], gate_up[:, quarter:]
    phi_big = 0.5 * (1.0 + lax.erf(gate * math.sqrt(0.5)))
    gelu = gate * phi_big
    slope_gate = phi_big + gate * jnp.exp(-0.5 * gate * gate) * (1.0 / math.sqrt(2.0 * math.pi))
    hidden = (gelu * up).astype(BF)
    final_part = dot_nn(hidden, w_narrow).reshape(GROUPS, rows, width)
    final_in = first + at.scatter_sum([final_part[k] for k in range(GROUPS)]) + b_narrow
    final_unit, final_root = norm_stats(final_in)
    result = final_unit * g_final + s_final

    upstream = cotangent[0].astype(F32)
    final_back = norm_back(final_unit, final_root, g_final, upstream)
    final_gain_grad = jnp.sum(upstream * final_unit, axis=0)
    final_shift_grad = jnp.sum(upstream, axis=0)
    narrow_back = final_back.astype(BF)
    narrow_bias_grad = jnp.sum(narrow_back.astype(F32), axis=0)
    back_four = jnp.concatenate(at.gather(narrow_back), axis=0)
    hidden_back = dot_nt(back_four, w_narrow)
    widen_back = jnp.concatenate(
        [hidden_back * up * slope_gate, hidden_back * gelu], axis=1
    ).astype(BF)
    first_part = dot_nt(widen_back, w_widen).reshape(GROUPS, rows, width)
    first_back = final_back + at.scatter_sum([first_part[k] for k in range(GROUPS)])
    narrow_grad = dot_tn(hidden, back_four)
    widen_grad = dot_tn(first_four, widen_back)
    widen_bias_grad = jnp.sum(widen_back.astype(F32), axis=0)

    attn_back = norm_back(first_unit, first_root, g_first, first_back)
    first_gain_grad = jnp.sum(first_back * first_unit, axis=0)
    first_shift_grad = jnp.sum(first_back, axis=0)
    output_back = attn_back.astype(BF)
    output_bias_grad = jnp.sum(output_back.astype(F32), axis=0)
    output_grad = dot_tn(mixed, output_back)
    mixed_back = dot_nt(output_back, w_output).astype(BF)
    mixed_back = jnp.transpose(mixed_back.reshape(rows, GROUPS, cols), (1, 0, 2))
    back_near = jnp.concatenate(at.exchange(mixed_back), axis=0)

    query_sum, kv_sum = attend_backward(
        slopes, queries, back_near, mixed_near, inv, key_value, q_info, jnp.transpose(k_info)
    )
    if r == 2:
        half = kv_sum.shape[0] // 2
        kv_back = kv_sum[:half] + at.partner(kv_sum[half:].astype(BF)).astype(F32)
    else:
        kv_back = at.member_sum(kv_sum.reshape(r, -1, 2 * cols))
    query_low = query_sum.astype(BF)
    query_scaled = (query_low.astype(F32) * scale).astype(BF)
    joined_back = jnp.concatenate([query_scaled, kv_back.astype(BF)], axis=1)
    tokens_part = dot_nt(joined_back, w_joined).reshape(GROUPS, rows, width)
    tokens_grad = attn_back + at.scatter_sum([tokens_part[k] for k in range(GROUPS)])
    joined_grad = dot_tn(x_four, joined_back)
    near_bias = jnp.sum(joined_back.astype(F32), axis=0)
    query_bias_grad = near_bias[:cols]
    value_bias_grad = near_bias[2 * cols :]

    narrow_sum = at.member_sum(jnp.transpose(narrow_grad.reshape(2, r, ff_own, width), (1, 0, 2, 3)))
    narrow_total = at.rep_sum(at.seq_sum(narrow_sum))

    def to_rows(grad):
        pieces = jnp.transpose(grad.reshape(2, GROUPS, r, kb, -1), (2, 0, 1, 3, 4))
        mine = at.rep_sum(at.seq_sum(at.member_sum(pieces))).astype(BF)
        return at.ordered(at.exchange(mine))

    widen_total = jnp.transpose(
        to_rows(widen_grad).reshape(GROUPS, kb, 4, span), (1, 2, 0, 3)
    ).reshape(kb, 2 * ff)
    joined_total = jnp.transpose(
        to_rows(joined_grad).reshape(GROUPS, kb, 3, cols), (1, 2, 0, 3)
    ).reshape(kb, 3 * width)

    def spread(vector, parts):
        wide = jnp.zeros((parts, GROUPS, vector.shape[0] // parts), F32)
        return lax.dynamic_update_slice_in_dim(
            wide, vector.reshape(parts, 1, -1), at.group, 1
        ).reshape(-1)

    vectors = [
        spread(query_bias_grad, 1),
        spread(value_bias_grad, 1),
        output_bias_grad,
        first_gain_grad,
        first_shift_grad,
        narrow_bias_grad,
        final_gain_grad,
        final_shift_grad,
    ]
    row = jnp.concatenate(
        [item.reshape(2 * n, kb) for item in vectors]
        + [spread(widen_bias_grad, 4).reshape(2 * n, 8 * kb)],
        axis=1,
    )
    row = jnp.pad(row[:, None, :], ((0, 0), (0, 15), (0, width - 16 * kb)))
    packed = jnp.concatenate([output_grad.reshape(2 * n, kb, width), row], axis=1)
    packed = jnp.transpose(packed.reshape(2, GROUPS, r, kb + 16, width), (2, 0, 1, 3, 4))
    packed = at.seq_sum(at.member_sum(packed)).astype(BF)
    packed = at.exchange(packed)
    packed = sum(item.astype(F32) for item in packed[1:]) + packed[0].astype(F32)
    packed = at.rep_sum(packed)
    output_total = packed[:kb]
    last = packed[kb]

    def owned(place):
        return last[place * kb : (place + 1) * kb]

    return (
        result.astype(BF)[None],
        tokens_grad[None],
        joined_total.astype(F32),
        owned(0),
        owned(1),
        output_total,
        owned(2),
        owned(3),
        owned(4),
        widen_total.astype(F32),
        last[8 * kb : 16 * kb],
        narrow_total,
        owned(5),
        owned(6),
        owned(7),
    )


def vmem(shape):
    return pl.BlockSpec(shape, lambda *_: tuple(0 for _ in shape))


SMEM = pl.BlockSpec(memory_space=pltpu.SMEM)


def call(body, name, inputs, outputs, scratch=(), grid=(1,), in_specs=None, out_specs=None, flops=0):
    shapes = [jax.ShapeDtypeStruct(shape, kind) for shape, kind in outputs]
    if in_specs is None:
        in_specs = [SMEM if item.ndim == 1 else vmem(item.shape) for item in inputs]
    if out_specs is None:
        out_specs = [vmem(shape) for shape, kind in outputs]
    moved = sum(item.size * item.dtype.itemsize for item in list(inputs) + shapes)
    return pl.pallas_call(
        body,
        grid=grid,
        in_specs=in_specs,
        out_specs=out_specs,
        out_shape=shapes,
        scratch_shapes=list(scratch),
        name=name,
        cost_estimate=pl.CostEstimate(flops=flops, transcendentals=0, bytes_accessed=moved),
    )(*inputs)


def pack_joined(ids, weight, vectors, widen_bias, cols):
    kb = weight.shape[0]
    vectors = [item[None] for item in vectors]
    shape = (kb + 16, 3 * cols)

    def body(*refs):
        ids_ref, w_ref, wide_ref = refs[0], refs[1], refs[10]
        all_ref = refs[15]
        rows = [ref[...].astype(F32) for ref in refs[2:10]]
        wide = wide_ref[...].astype(F32)
        rows += [wide[:, k * kb : (k + 1) * kb] for k in range(8)]
        small = jnp.concatenate(rows, axis=0).astype(BF)
        for g in range(GROUPS):
            for part in range(3):
                at = (part * GROUPS + g) * cols
                all_ref[g, :kb, part * cols : (part + 1) * cols] = w_ref[:, at : at + cols]
            all_ref[g, kb:, :] = jnp.zeros((16, 3 * cols), BF)
            all_ref[g, kb:, :kb] = small
        for k in range(GROUPS):
            refs[11 + k][...] = all_ref[(ids_ref[0] + k) % GROUPS]

    inputs = [ids, weight] + vectors + [widen_bias[None]]
    return call(
        body,
        "pack_joined",
        inputs,
        [(shape, BF)] * GROUPS,
        scratch=[pltpu.VMEM((GROUPS,) + shape, BF)],
    )


def place_rows(ids_ref, pieces, out_ref, kb, relative=False):
    group, m, y = ids_ref[0], ids_ref[1], ids_ref[2]
    for index, piece in enumerate(pieces):
        row = y if index % 2 == 0 else 1 - y
        member = m if index < 2 else 1 - m
        for g in range(GROUPS):
            source = (group + GROUPS - g) % GROUPS if relative else g
            start = pl.multiple_of((row * GROUPS * 2 + source * 2 + member) * kb, 16)
            out_ref[pl.ds(start, kb), :] = piece[g, :kb, :]


def assemble_joined(ids, pieces, kb):
    cols = pieces[0].shape[2]
    near = cols // 3
    width = 4 * GROUPS * kb
    span = 8 * kb

    def body(ids_ref, a_ref, b_ref, c_ref, d_ref, w_ref, vec_ref, near_ref, wide_ref):
        place_rows(ids_ref, (a_ref, b_ref, c_ref, d_ref), w_ref, kb, True)
        g, m, y = ids_ref[0], ids_ref[1], ids_ref[2]
        blocks = []
        for row in range(2):
            for k in range(GROUPS):
                for member in range(2):
                    turn = (g + GROUPS - k) % GROUPS
                    picks = [ref[turn, kb:, :kb].astype(F32) for ref in (a_ref, b_ref, c_ref, d_ref)]
                    mine = jnp.where(row == y, picks[0], picks[1])
                    theirs = jnp.where(row == y, picks[2], picks[3])
                    blocks.append(jnp.where(member == m, mine, theirs))
        vec = jnp.concatenate(blocks, axis=1)
        vec_ref[...] = vec
        total = jnp.zeros((16, near), F32)
        for k in range(GROUPS):
            total = jnp.where(g == k, vec[:, k * near : (k + 1) * near], total)
        near_ref[...] = total
        lines = []
        for chunk in range(4):
            block = jnp.zeros((8, kb), F32)
            for k in range(GROUPS):
                at = (chunk * GROUPS + k) * kb
                block = jnp.where(g == k, vec[8:16, at : at + kb], block)
            lines += [block[i : i + 1] for i in range(8)]
        wide_ref[...] = jnp.concatenate(lines, axis=1)

    return call(
        body,
        "assemble_joined",
        [ids] + list(pieces),
        [((width, cols), BF), ((16, width), F32), ((16, near), F32), ((1, 4 * span), F32)],
    )


def assemble_rows(ids, pieces, name):
    kb = pieces[0].shape[1]
    cols = pieces[0].shape[2]

    def body(ids_ref, a_ref, b_ref, c_ref, d_ref, w_ref):
        place_rows(ids_ref, (a_ref, b_ref, c_ref, d_ref), w_ref, kb)

    return call(body, name, [ids] + list(pieces), [((4 * GROUPS * kb, cols), BF)])[0]


def assemble_narrow(ids, pieces):
    rows, cols = pieces[0].shape

    def body(ids_ref, a_ref, b_ref, c_ref, d_ref, w_ref):
        m, y = ids_ref[1], ids_ref[2]
        for index, ref in enumerate((a_ref, b_ref, c_ref, d_ref)):
            row = y if index % 2 == 0 else 1 - y
            member = m if index < 2 else 1 - m
            start = pl.multiple_of((row * 2 + member) * rows, 16)
            w_ref[pl.ds(start, rows), :] = ref[...]

    return call(body, "assemble_narrow", [ids] + list(pieces), [((4 * rows, cols), BF)])[0]


def split_joined(x_four, weight, near, scale):
    count, width = x_four.shape
    cols = weight.shape[1] // 3

    def body(x_ref, w_ref, near_ref, q_ref, kv_ref):
        joined = dot_nn(x_ref[...], w_ref[...])
        q_ref[...] = ((joined[:, :cols] + near_ref[0:1, :]) * scale).astype(BF)
        kv_ref[:, :cols] = joined[:, cols : 2 * cols].astype(BF)
        kv_ref[:, cols:] = (joined[:, 2 * cols :] + near_ref[1:2, :]).astype(BF)

    return call(
        body,
        "split_joined",
        [x_four, weight, near],
        [((count, cols), BF), ((count, 2 * cols), BF)],
        flops=2 * count * width * 3 * cols,
    )


def piece_rows(ids_ref, k, rows, sign=1):
    turn = (ids_ref[0] + (k if sign > 0 else GROUPS - k)) % GROUPS
    return pl.ds(pl.multiple_of(turn * rows, 16), rows)


def attend(ids, slopes, queries, kv_own, kv_other, q_col, k_row):
    count, cols = queries.shape
    heads = cols // HEAD_DIM
    rows = count // GROUPS
    chunk = kv_own.shape[0]

    def body(ids_ref, slope_ref, q_ref, own_ref, other_ref, qi_ref, ki_ref, out_ref, inv_ref, *sends):
        q = q_ref[...]
        qpos = qi_ref[:, 0:1]
        qseg = qi_ref[:, 1:2]
        ones = jnp.ones((chunk, 64), BF)
        q_heads = [only_head(q, head) for head in range(heads)]
        accs = [None] * heads
        for side, kv_ref in enumerate((own_ref, other_ref)):
            here = slice(side * chunk, (side + 1) * chunk)
            keys = kv_ref[:, :cols]
            values = jnp.concatenate([kv_ref[:, cols:], ones], axis=1)
            far = jnp.where(qseg == ki_ref[1:2, here], jnp.abs(qpos - ki_ref[0:1, here]), FAR)
            for head in range(heads):
                scores = dot_nt(q_heads[head], keys) - slope_ref[head] * far
                part = dot_nn(jnp.exp(scores).astype(BF), values)
                accs[head] = part if side == 0 else accs[head] + part
        total = jnp.zeros((count, cols), F32)
        for head in range(heads):
            inv = 1.0 / accs[head][:, cols : cols + 1]
            inv_ref[head] = jnp.transpose(jnp.broadcast_to(inv, (count, 128)))[:8]
            total = total + only_head(accs[head][:, :cols] * inv, head)
        out_ref[...] = total
        for k, ref in enumerate(sends):
            ref[...] = out_ref[piece_rows(ids_ref, k, rows), :].astype(BF)

    return call(
        body,
        "attend",
        [ids, slopes, queries, kv_own, kv_other, q_col, k_row],
        [((count, cols), F32), ((heads, 8, count), F32)] + [((rows, cols), BF)] * GROUPS,
        flops=4 * count * 2 * chunk * cols,
    )


def attend_back(ids, slopes, queries, back_rel, mixed, inv, kv_own, kv_other, q_row, k_col, scale):
    count, cols = queries.shape
    heads = cols // HEAD_DIM
    rows = count // GROUPS
    chunk = kv_own.shape[0]

    def body(ids_ref, slope_ref, q_ref, *refs):
        pieces = refs[:GROUPS]
        out_ref, inv_ref, own_ref, other_ref, qi_ref, ki_ref, dq_ref, keep_ref, give_ref, do_ref = refs[GROUPS:]
        for k, ref in enumerate(pieces):
            do_ref[piece_rows(ids_ref, k, rows, -1), :] = ref[...]
        q = q_ref[...]
        back = do_ref[...]
        product = back.astype(F32) * out_ref[...]
        qpos = qi_ref[0:1, :]
        qseg = qi_ref[1:2, :]
        q_heads = [only_head(q, head) for head in range(heads)]
        b_heads = [only_head(back, head) for head in range(heads)]
        place = lax.broadcasted_iota(jnp.int32, (8, cols), 0)
        lane = lax.broadcasted_iota(jnp.int32, (8, cols), 1)
        row_dots = lax.dot_general(
            (lane // HEAD_DIM == place).astype(F32),
            product,
            (((1,), (1,)), ((), ())),
            precision=lax.Precision.HIGHEST,
            preferred_element_type=F32,
        )
        query_parts = [None] * heads
        for side, kv_ref in enumerate((own_ref, other_ref)):
            here = slice(side * chunk, (side + 1) * chunk)
            keys = kv_ref[:, :cols]
            values = kv_ref[:, cols:]
            far = jnp.where(qseg == ki_ref[here, 1:2], jnp.abs(qpos - ki_ref[here, 0:1]), FAR)
            key_part = None
            value_part = None
            for head in range(heads):
                scores = dot_nt(keys, q_heads[head]) - slope_ref[head] * far
                probs = jnp.exp(scores) * inv_ref[head, 0:1, :]
                prob_back = dot_nt(values, b_heads[head])
                score_back = (probs * (prob_back - row_dots[head : head + 1])).astype(BF)
                k_part = dot_nn(score_back, q_heads[head])
                v_part = dot_nn(probs.astype(BF), b_heads[head])
                q_part = dot_tn(score_back, keys)
                key_part = k_part if head == 0 else key_part + k_part
                value_part = v_part if head == 0 else value_part + v_part
                query_parts[head] = q_part if side == 0 else query_parts[head] + q_part
            target = keep_ref if side == 0 else give_ref
            target[:, :cols] = key_part.astype(target.dtype)
            target[:, cols:] = value_part.astype(target.dtype)
        total = jnp.zeros((count, cols), F32)
        for head in range(heads):
            total = total + only_head(query_parts[head], head)
        dq_ref[...] = (total.astype(BF).astype(F32) * scale).astype(BF)

    return call(
        body,
        "attend_back",
        [ids, slopes, queries] + list(back_rel) + [mixed, inv, kv_own, kv_other, q_row, k_col],
        [((count, cols), BF), ((chunk, 2 * cols), F32), ((chunk, 2 * cols), BF)],
        scratch=[pltpu.VMEM((count, cols), BF)],
        flops=10 * count * 2 * chunk * cols,
    )


def close_attention(ids, inputs, mixed_rel, weight, vec):
    rows, width = inputs.shape
    cols = mixed_rel[0].shape[1]

    def body(ids_ref, x_ref, a_ref, b_ref, c_ref, d_ref, w_ref, vec_ref, first_ref, low_ref, unit_ref, root_ref):
        total = x_ref[...].astype(F32) + vec_ref[2:3, :]
        for k, ref in enumerate((a_ref, b_ref, c_ref, d_ref)):
            total = total + dot_nn(ref[...], w_ref[piece_rows(ids_ref, k, cols, -1), :])
        unit, root = norm_stats(total)
        first = unit * vec_ref[3:4, :] + vec_ref[4:5, :]
        first_ref[...] = first
        low_ref[...] = first.astype(BF)
        unit_ref[...] = unit
        root_ref[...] = root

    return call(
        body,
        "close_attention",
        [ids, inputs] + list(mixed_rel) + [weight, vec],
        [((rows, width), F32), ((rows, width), BF), ((rows, width), F32), ((rows, 1), F32)],
        flops=2 * rows * width * width,
    )


def block_of(quarter):
    return math.gcd(quarter, 256)


def join_pieces(refs):
    return jnp.concatenate([ref[...] for ref in refs], axis=0)


def send_pieces(total, refs, rows):
    for k, ref in enumerate(refs):
        ref[...] = total[k * rows : (k + 1) * rows, :].astype(ref.dtype)


def widen_narrow(rel, w_gate, w_up, w_narrow, wide):
    rows, width = rel[0].shape
    quarter = w_narrow.shape[0]
    count = GROUPS * rows

    def body(*refs):
        wg_ref, wu_ref, wn_ref, wide_ref = refs[4:8]
        hid_ref, gate_ref, up_ref = refs[12:15]
        value = join_pieces(refs[:4])
        gate = dot_nn(value, wg_ref[...]) + wide_ref[:, :quarter]
        up = dot_nn(value, wu_ref[...]) + wide_ref[:, quarter:]
        gate_ref[...] = gate
        up_ref[...] = up
        hidden = (gate * (0.5 + 0.5 * lax.erf(gate * math.sqrt(0.5))) * up).astype(BF)
        hid_ref[...] = hidden
        send_pieces(dot_nn(hidden, wn_ref[...]), refs[8:12], rows)

    return call(
        body,
        "widen_narrow",
        list(rel) + [w_gate, w_up, w_narrow, wide],
        [((rows, width), F32)]
        + [((rows, width), BF)] * 3
        + [((count, quarter), BF), ((count, quarter), F32), ((count, quarter), F32)],
        flops=6 * count * width * quarter,
    )


def gate_slopes(gate, up):
    phi_big = 0.5 + 0.5 * lax.erf(gate * math.sqrt(0.5))
    slope = phi_big + gate * jnp.exp(-0.5 * gate * gate) * (1.0 / math.sqrt(2.0 * math.pi))
    return up * slope, gate * phi_big


def widen_narrow_back(rel, w_gate, w_up, w_narrow, gate_factor, up_factor):
    rows, width = rel[0].shape
    quarter = w_narrow.shape[0]
    count = GROUPS * rows

    def body(*refs):
        wg_ref, wu_ref, wn_ref, gf_ref, uf_ref = refs[4:9]
        bg_ref, bu_ref = refs[13:15]
        hidden_back = dot_nt(join_pieces(refs[:4]), wn_ref[...])
        gate_back = (hidden_back * gf_ref[...]).astype(BF)
        up_back = (hidden_back * uf_ref[...]).astype(BF)
        bg_ref[...] = gate_back
        bu_ref[...] = up_back
        total = dot_nt(gate_back, wg_ref[...]) + dot_nt(up_back, wu_ref[...])
        send_pieces(total, refs[9:13], rows)

    return call(
        body,
        "widen_narrow_back",
        list(rel) + [w_gate, w_up, w_narrow, gate_factor, up_factor],
        [((rows, width), F32)] + [((rows, width), BF)] * 3 + [((count, quarter), BF)] * 2,
        flops=6 * count * width * quarter,
    )


def turn_final(own, received, first, upstream, vec):
    rows, width = own.shape

    def body(own_ref, a_ref, b_ref, c_ref, first_ref, up_ref, vec_ref, res_ref, back_ref, low_ref, sum_ref):
        total = first_ref[...] + vec_ref[5:6, :] + own_ref[...]
        for ref in (a_ref, b_ref, c_ref):
            total = total + ref[...].astype(F32)
        unit, root = norm_stats(total)
        gain = vec_ref[6:7, :]
        res_ref[...] = (unit * gain + vec_ref[7:8, :]).astype(BF)
        upstream = up_ref[...].astype(F32)
        back = norm_back(unit, root, gain, upstream)
        low = back.astype(BF)
        back_ref[...] = back
        low_ref[...] = low
        sum_ref[...] = jnp.zeros_like(sum_ref)
        sum_ref[0:1, :] = jnp.sum(low.astype(F32), axis=0, keepdims=True)
        sum_ref[1:2, :] = jnp.sum(upstream * unit, axis=0, keepdims=True)
        sum_ref[2:3, :] = jnp.sum(upstream, axis=0, keepdims=True)

    return call(
        body,
        "turn_final",
        [own] + list(received) + [first, upstream, vec],
        [((rows, width), BF), ((rows, width), F32), ((rows, width), BF), ((8, width), F32)],
    )


def turn_first(ids, own, received, final_back, unit, root, weight, vec):
    rows, width = own.shape
    cols = width // GROUPS

    def body(ids_ref, own_ref, a_ref, b_ref, c_ref, fb_ref, unit_ref, root_ref, w_ref, vec_ref, *outs):
        attn_ref, low_ref, sum_ref = outs[:3]
        total = fb_ref[...] + own_ref[...]
        for ref in (a_ref, b_ref, c_ref):
            total = total + ref[...].astype(F32)
        unit = unit_ref[...]
        back = norm_back(unit, root_ref[...], vec_ref[3:4, :], total)
        low = back.astype(BF)
        attn_ref[...] = back
        low_ref[...] = low
        for k, ref in enumerate(outs[3:]):
            ref[...] = dot_nt(low, w_ref[piece_rows(ids_ref, k, cols), :]).astype(BF)
        sum_ref[...] = jnp.zeros_like(sum_ref)
        sum_ref[0:1, :] = jnp.sum(low.astype(F32), axis=0, keepdims=True)
        sum_ref[1:2, :] = jnp.sum(total * unit, axis=0, keepdims=True)
        sum_ref[2:3, :] = jnp.sum(total, axis=0, keepdims=True)

    return call(
        body,
        "turn_first",
        [ids, own] + list(received) + [final_back, unit, root, weight, vec],
        [((rows, width), F32), ((rows, width), BF), ((8, width), F32)] + [((rows, cols), BF)] * GROUPS,
        flops=2 * rows * width * width,
    )


def split_rows(ids_ref, full_ref, keep_ref, give_ref, kb, lead=()):
    m, y = ids_ref[1], ids_ref[2]
    for turn in range(2):
        row = y if turn == 0 else 1 - y
        for g in range(GROUPS):
            base = (row * GROUPS + g) * 2
            mine = pl.ds(pl.multiple_of((base + m) * kb, 16), kb)
            other = pl.ds(pl.multiple_of((base + 1 - m) * kb, 16), kb)
            keep_ref[lead + (turn, g, slice(0, kb), slice(None))] = full_ref[mine, :]
            give_ref[lead + (turn, g, slice(0, kb), slice(None))] = full_ref[other, :].astype(BF)


def widen_grads(ids, rel, gate_back, up_back, kb):
    rows, width = rel[0].shape
    count, quarter = gate_back.shape
    block = block_of(quarter)
    steps = quarter // block

    def body(ids_ref, a_ref, b_ref, c_ref, d_ref, gate_ref, up_ref, keep_ref, give_ref, gs_ref, us_ref, full_ref):
        value = jnp.concatenate([a_ref[...], b_ref[...], c_ref[...], d_ref[...]], axis=0)
        x = ids_ref[3]
        for turn, (ref, sum_ref) in enumerate(((gate_ref, gs_ref), (up_ref, us_ref))):
            back = ref[...]
            full_ref[...] = dot_tn(value, back)
            sum_ref[...] = jnp.sum(back.astype(F32), axis=0, keepdims=True)
            split_rows(ids_ref, full_ref, keep_ref, give_ref, kb, ((x + turn) % 2,))

    piece = vmem((rows, width))
    tall = pl.BlockSpec((count, block), lambda i: (0, i))
    line = pl.BlockSpec((1, block), lambda i: (0, i))
    cut = pl.BlockSpec((2, 2, GROUPS, kb, block), lambda i: (0, 0, 0, 0, i))
    shape = (2, 2, GROUPS, kb, quarter)
    return call(
        body,
        "widen_grads",
        [ids] + list(rel) + [gate_back, up_back],
        [(shape, F32), (shape, BF), ((1, quarter), F32), ((1, quarter), F32)],
        scratch=[pltpu.VMEM((width, block), F32)],
        grid=(steps,),
        in_specs=[SMEM] + [piece] * 4 + [tall] * 2,
        out_specs=[cut, cut, line, line],
        flops=4 * count * width * quarter,
    )


def narrow_grads(ids, hidden, rel):
    rows, width = rel[0].shape
    count, quarter = hidden.shape
    own = quarter // 4

    def body(ids_ref, h_ref, a_ref, b_ref, c_ref, d_ref, keep_ref, give_ref, full_ref):
        value = jnp.concatenate([a_ref[...], b_ref[...], c_ref[...], d_ref[...]], axis=0)
        full_ref[...] = dot_tn(h_ref[...], value)
        m, y = ids_ref[1], ids_ref[2]
        for turn in range(2):
            base = (y if turn == 0 else 1 - y) * 2
            mine = pl.ds(pl.multiple_of((base + m) * own, 16), own)
            other = pl.ds(pl.multiple_of((base + 1 - m) * own, 16), own)
            keep_ref[turn] = full_ref[mine, :]
            give_ref[turn] = full_ref[other, :].astype(BF)

    return call(
        body,
        "narrow_grads",
        [ids, hidden] + list(rel),
        [((2, own, width), F32), ((2, own, width), BF)],
        scratch=[pltpu.VMEM((quarter, width), F32)],
        flops=2 * count * width * quarter,
    )


def place_small(ids_ref, blocks, keep_ref, give_ref, kb):
    m, y = ids_ref[1], ids_ref[2]
    for turn in range(2):
        for g in range(GROUPS):
            picked = []
            for member in range(2):
                first = jnp.where(y == 0, blocks[0][g][member], blocks[1][g][member])
                second = jnp.where(y == 0, blocks[1][g][member], blocks[0][g][member])
                picked.append(first if turn == 0 else second)
            cols = keep_ref.shape[3]
            mine = jnp.where(m == 0, picked[0], picked[1])
            other = jnp.where(m == 0, picked[1], picked[0])
            keep_ref[turn, g, kb:, :] = jnp.zeros((16, cols), F32)
            give_ref[turn, g, kb:, :] = jnp.zeros((16, cols), BF)
            keep_ref[turn, g, kb:, :kb] = mine
            give_ref[turn, g, kb:, :kb] = other.astype(BF)


def output_grads(ids, mixed_rel, back, first_sums, final_sums, gate_sum, up_sum, kb):
    rows, width = back.shape
    cols = mixed_rel[0].shape[1]

    def body(ids_ref, *refs):
        back_ref, fs_ref, ls_ref, gs_ref, us_ref, keep_ref, give_ref, full_ref = refs[GROUPS:]
        for k, ref in enumerate(refs[:GROUPS]):
            full_ref[piece_rows(ids_ref, k, cols, -1), :] = dot_tn(ref[...], back_ref[...])
        split_rows(ids_ref, full_ref, keep_ref, give_ref, kb)
        g_own = ids_ref[0]
        sums = jnp.concatenate([fs_ref[0:3, :], ls_ref[0:3, :]], axis=0)
        wide = (gs_ref[...], us_ref[...])
        span = 8 * kb
        blocks = []
        for row in range(2):
            blocks.append([])
            for g in range(GROUPS):
                blocks[-1].append([])
                for member in range(2):
                    b = row * 8 + g * 2 + member
                    part = wide[b // 8][:, ((b // 4) % 2) * span : ((b // 4) % 2 + 1) * span]
                    part = jnp.where(g_own == b % GROUPS, part, 0.0)
                    lines = [part[:, i * kb : (i + 1) * kb] for i in range(8)]
                    lines = [sums[:, b * kb : (b + 1) * kb]] + lines + [jnp.zeros((2, kb), F32)]
                    blocks[-1][-1].append(jnp.concatenate(lines, axis=0))
        place_small(ids_ref, blocks, keep_ref, give_ref, kb)

    shape = (2, GROUPS, kb + 16, width)
    return call(
        body,
        "output_grads",
        [ids] + list(mixed_rel) + [back, first_sums, final_sums, gate_sum, up_sum],
        [(shape, F32), (shape, BF)],
        scratch=[pltpu.VMEM((width, width), F32)],
        flops=2 * rows * width * width,
    )


def tokens_parts(ids, back, weight):
    count, cols = back.shape
    rows = count // GROUPS
    width = weight.shape[0]

    def body(ids_ref, jb_ref, w_ref, *outs):
        for k, ref in enumerate(outs):
            part = dot_nt(jb_ref[piece_rows(ids_ref, k, rows, -1), :], w_ref[...])
            ref[...] = part.astype(ref.dtype)

    return call(
        body,
        "tokens_parts",
        [ids, back, weight],
        [((rows, width), F32)] + [((rows, width), BF)] * 3,
        flops=2 * count * width * cols,
    )


def joined_grads(ids, x_four, query_back, keep, got, kb):
    count, width = x_four.shape
    cols = query_back.shape[1]
    wide = 3 * cols

    def body(ids_ref, x_ref, q_ref, kv_ref, got_ref, keep_ref, give_ref, back_ref, full_ref):
        back_ref[:, :cols] = q_ref[...]
        back_ref[:, cols:] = (kv_ref[...] + got_ref[...].astype(F32)).astype(BF)
        full_ref[...] = dot_tn(x_ref[...], back_ref[...])
        split_rows(ids_ref, full_ref, keep_ref, give_ref, kb)
        g_own = ids_ref[0]
        sums = jnp.sum(back_ref[...].astype(F32), axis=0, keepdims=True)
        pair = jnp.concatenate([sums[:, :cols], sums[:, 2 * cols :], jnp.zeros((14, cols), F32)], axis=0)
        blocks = []
        for row in range(2):
            blocks.append([])
            for g in range(GROUPS):
                blocks[-1].append([])
                for member in range(2):
                    b = row * 8 + g * 2 + member
                    part = pair[:, (b % GROUPS) * kb : (b % GROUPS + 1) * kb]
                    blocks[-1][-1].append(jnp.where(g_own == b // GROUPS, part, 0.0))
        place_small(ids_ref, blocks, keep_ref, give_ref, kb)

    shape = (2, GROUPS, kb + 16, wide)
    return call(
        body,
        "joined_grads",
        [ids, x_four, query_back, keep, got],
        [(shape, F32), (shape, BF), ((count, wide), BF)],
        scratch=[pltpu.VMEM((width, wide), F32)],
        flops=2 * count * width * wide,
    )


def finish_widen(ids, own, other):
    kb, cols = own.shape[1:]
    span = cols // 2

    def body(ids_ref, own_ref, other_ref, out_ref):
        x = ids_ref[3]
        for part in range(2):
            for g in range(GROUPS):
                picked = jnp.where(x == part, own_ref[g].astype(F32), other_ref[g].astype(F32))
                for row in range(2):
                    at = ((part * 2 + row) * GROUPS + g) * span
                    out_ref[:, at : at + span] = picked[:, row * span : (row + 1) * span]

    return call(body, "finish_widen", [ids, own, other], [((kb, 4 * GROUPS * span), F32)])[0]


def finish_joined(got, kb):
    wide = got.shape[2]
    cols = wide // 3

    def body(got_ref, out_ref, small_ref):
        for g in range(GROUPS):
            for part in range(3):
                at = (part * GROUPS + g) * cols
                out_ref[:, at : at + cols] = got_ref[g, :kb, part * cols : (part + 1) * cols].astype(F32)
        small = jnp.zeros((16, wide), F32)
        for g in range(GROUPS):
            small = small + got_ref[g, kb:, :].astype(F32)
        small_ref[...] = small

    return call(body, "finish_joined", [got], [((kb, GROUPS * wide), F32), ((16, wide), F32)])


def fast_device(
    tokens,
    segments,
    joined_weight,
    query_bias,
    value_bias,
    output_weight,
    output_bias,
    first_gain,
    first_shift,
    widen_weight,
    widen_bias,
    narrow_weight,
    narrow_bias,
    final_gain,
    final_shift,
    cotangent,
):
    at = Layout()
    n, r = at.size, at.members
    rows, width = tokens.shape[1:]
    heads = width // HEAD_DIM
    near_heads = heads // GROUPS
    cols = near_heads * HEAD_DIM
    kb = joined_weight.shape[0]
    ff_own = narrow_weight.shape[0]
    quarter = 4 * ff_own
    span = 2 * ff_own
    seg_row = segments[0]
    length = seg_row.shape[0]
    scale = 1.0 / math.sqrt(HEAD_DIM)
    inputs = tokens[0]
    columns = [[g * r + m for g in range(GROUPS)] for m in range(r)]
    ids = jnp.stack([at.group, at.member, at.seq, at.rep]).astype(jnp.int32)

    def across(value):
        return lax.all_to_all(value, "ctx", 0, 0, axis_index_groups=columns, tiled=True)

    def spread_out(value):
        far = at.swap(value, "seq")
        return (value, far, at.partner(value), at.partner(far))

    x_four = across(jnp.broadcast_to(inputs[None], (GROUPS, rows, width))).reshape(-1, width)
    packed = pack_joined(
        ids,
        joined_weight,
        [
            query_bias,
            value_bias,
            output_bias,
            first_gain,
            first_shift,
            narrow_bias,
            final_gain,
            final_shift,
        ],
        widen_bias,
        cols,
    )
    joined_got = jnp.stack([packed[0]] + [at.shift(packed[k], k) for k in range(1, GROUPS)])
    joined_parts = spread_out(joined_got)
    w_joined, vec, near, wide = assemble_joined(ids, joined_parts, kb)
    narrow_parts = spread_out(after(narrow_weight, joined_parts[1]))
    output_cut = jnp.broadcast_to(after(output_weight, x_four)[None], (GROUPS, kb, width))
    output_got = across(output_cut)
    widen_cut = widen_weight.reshape(kb, 2, 2, GROUPS, span)
    widen_got = [
        across(
            after(jnp.transpose(widen_cut[:, t], (2, 0, 1, 3)).reshape(GROUPS, kb, quarter), output_got)
        )
        for t in range(2)
    ]

    queries, kv_own = split_joined(x_four, w_joined, near, scale)
    kv_other = at.partner(kv_own)
    lanes = jnp.arange(rows, dtype=jnp.int32)

    def places(member):
        return ((jnp.arange(GROUPS, dtype=jnp.int32) * r + member)[:, None] * rows + lanes).reshape(-1)

    by_member = jnp.transpose(seg_row.reshape(GROUPS, r, rows), (1, 0, 2)).reshape(r, -1)

    def documents(member):
        return lax.dynamic_index_in_dim(by_member, member, 0, keepdims=False)

    q_row = jnp.stack([places(at.member), documents(at.member)]).astype(F32)
    o_row = jnp.stack([places(1 - at.member), documents(1 - at.member)]).astype(F32)
    k_row = jnp.concatenate([q_row, o_row], axis=1)
    q_col = jnp.transpose(q_row)
    k_col = jnp.transpose(k_row)
    order_heads = at.group * near_heads + jnp.arange(near_heads, dtype=jnp.int32)
    slopes = jnp.power(2.0, -8.0 * (order_heads.astype(F32) + 1.0) / heads) * (512.0 / length)
    attended = attend(ids, slopes, queries, kv_own, kv_other, q_col, k_row)
    mixed_near, inv = attended[:2]
    mixed_send = attended[2:]
    mixed_rel = [mixed_send[0]] + [at.shift(mixed_send[k], k) for k in range(1, GROUPS)]
    w_output = assemble_rows(ids, spread_out(output_got), "assemble_output")
    w_narrow = assemble_narrow(ids, narrow_parts)
    w_gate = assemble_rows(ids, spread_out(widen_got[0]), "assemble_gate")
    w_up = assemble_rows(ids, spread_out(widen_got[1]), "assemble_up")

    first, first_low, first_unit, first_root = close_attention(ids, inputs, mixed_rel, w_output, vec)
    first_rel = at.gather(first_low)
    own, s1, s2, s3, hidden, gate, up = widen_narrow(first_rel, w_gate, w_up, w_narrow, wide)
    received = [at.shift(s1, -1), at.shift(s2, -2), at.shift(s3, -3)]
    gate_factor, up_factor = gate_slopes(gate, up)
    result, final_back, narrow_back, final_sums = turn_final(own, received, first, cotangent[0], vec)

    back_rel = at.gather(narrow_back)
    own, s1, s2, s3, gate_back, up_back = widen_narrow_back(
        back_rel, w_gate, w_up, w_narrow, gate_factor, up_factor
    )
    received = [at.shift(s1, -1), at.shift(s2, -2), at.shift(s3, -3)]
    narrow_keep, narrow_give = narrow_grads(ids, hidden, back_rel)
    widen_keep, widen_give, gate_sum, up_sum = widen_grads(ids, first_rel, gate_back, up_back, kb)
    turned = turn_first(ids, own, received, final_back, first_unit, first_root, w_output, vec)
    attn_back, output_back, first_sums = turned[:3]
    back_send = turned[3:]
    back_near = [back_send[0]] + [at.shift(back_send[k], k) for k in range(1, GROUPS)]

    narrow_got = at.partner(after(narrow_give, received[2]))
    widen_got = at.partner(after(widen_give, received[2]))
    output_keep, output_give = output_grads(
        ids, mixed_rel, output_back, first_sums, final_sums, gate_sum, up_sum, kb
    )

    def seq_send(keep, got):
        return (keep + got.astype(F32)).astype(BF)

    narrow_far = at.swap(seq_send(narrow_keep[1], narrow_got[1]), "seq")
    widen_far = at.swap(seq_send(widen_keep[:, 1], widen_got[:, 1]), "seq")
    output_got = at.partner(output_give)

    query_back, kv_keep, kv_give = attend_back(
        ids, slopes, queries, back_near, mixed_near, inv, kv_own, kv_other, q_row, k_col, scale
    )
    kv_give, narrow_far, widen_far, output_got = lax.optimization_barrier(
        (kv_give, narrow_far, widen_far, output_got)
    )
    kv_got = at.partner(kv_give)

    narrow_sum = (narrow_keep[0] + narrow_got[0].astype(F32) + narrow_far.astype(F32)).astype(BF)
    narrow_total = narrow_sum.astype(F32) + at.swap(narrow_sum, "rep").astype(F32)
    widen_sum = widen_keep[:, 0] + widen_got[:, 0].astype(F32) + widen_far.astype(F32)
    widen_mine = widen_sum[0] + at.swap(widen_sum[1].astype(BF), "rep").astype(F32)
    output_far = at.swap(seq_send(output_keep[1], output_got[1]), "seq")
    output_sum = (output_keep[0] + output_got[0].astype(F32) + output_far.astype(F32)).astype(BF)

    joined_keep, joined_give, joined_back = joined_grads(ids, x_four, query_back, kv_keep, kv_got, kb)
    joined_got = at.partner(joined_give)
    own, s1, s2, s3 = tokens_parts(ids, joined_back, w_joined)
    received = [at.shift(s1, -1), at.shift(s2, -2), at.shift(s3, -3)]
    joined_far = at.swap(seq_send(joined_keep[1], joined_got[1]), "seq")
    joined_sum = (joined_keep[0] + joined_got[0].astype(F32) + joined_far.astype(F32)).astype(BF)
    joined_mine = (joined_sum.astype(F32) + at.swap(joined_sum, "rep").astype(F32)).astype(BF)
    widen_own = across(widen_mine.astype(BF))
    widen_total = finish_widen(ids, widen_own, at.swap(widen_own, "rep"))
    output_all = across(after(output_sum, widen_own))
    output_mine = jnp.sum(output_all.astype(F32), axis=0).astype(BF)
    output_total = output_mine.astype(F32) + at.swap(output_mine, "rep").astype(F32)
    joined_total, pair = finish_joined(across(joined_mine), kb)
    tokens_grad = attn_back + own
    for item in received:
        tokens_grad = tokens_grad + item.astype(F32)
    last = output_total[kb:, :kb]
    return (
        result[None],
        tokens_grad[None],
        joined_total,
        pair[0, :kb],
        pair[1, :kb],
        output_total[:kb],
        last[0],
        last[1],
        last[2],
        widen_total,
        last[6:14].reshape(-1),
        narrow_total,
        last[3],
        last[4],
        last[5],
    )


def solution(mesh):
    tokens = P(("rep", "seq"), "ctx", None)
    matrix = P(("seq", "ctx"), None)
    vector = P(("seq", "ctx"))
    near = mesh.shape["ctx"] == 2 * GROUPS and mesh.shape["rep"] == 2
    return jax.shard_map(
        fast_device if near else on_device,
        mesh=mesh,
        in_specs=(
            tokens,
            P(("rep", "seq"), None),
            matrix,
            vector,
            vector,
            matrix,
            vector,
            vector,
            vector,
            matrix,
            vector,
            matrix,
            vector,
            vector,
            vector,
            tokens,
        ),
        out_specs=(
            tokens,
            tokens,
            matrix,
            vector,
            vector,
            matrix,
            vector,
            vector,
            vector,
            matrix,
            vector,
            matrix,
            vector,
            vector,
            vector,
        ),
        check_vma=False,
    )
```

```python
import math

import jax
import jax.numpy as jnp
from jax import lax
from jax.experimental import pallas as pl
from jax.experimental.pallas import tpu as pltpu
from jax.sharding import PartitionSpec as P

HEAD_DIM = 64
GROUPS = 4
FAR = 1e30
BF = jnp.bfloat16
F32 = jnp.float32


def dot_nn(left, right):
    return lax.dot_general(left, right, (((1,), (0,)), ((), ())), preferred_element_type=F32)


def dot_tn(left, right):
    return lax.dot_general(left, right, (((0,), (0,)), ((), ())), preferred_element_type=F32)


def dot_nt(left, right):
    return lax.dot_general(left, right, (((1,), (1,)), ((), ())), preferred_element_type=F32)


def head_mask(head, cols):
    lane = lax.broadcasted_iota(jnp.int32, (1, cols), 1)
    return (lane >= head * HEAD_DIM) & (lane < (head + 1) * HEAD_DIM)


def only_head(value, head):
    return jnp.where(head_mask(head, value.shape[1]), value, jnp.zeros_like(value))


def each_chunk(count, body):
    if count <= 4:
        for index in range(count):
            body(index)
    else:
        lax.fori_loop(0, count, lambda index, carry: (body(index), carry)[1], 0)


def forward_kernel(slope_ref, q_ref, kv_ref, qinfo_ref, kinfo_ref, out_ref, inv_ref, acc_ref, sum_ref, *, chunk):
    rows, cols = q_ref.shape
    heads = cols // HEAD_DIM
    count = kv_ref.shape[0] // chunk
    acc_ref[...] = jnp.zeros_like(acc_ref)
    sum_ref[...] = jnp.zeros_like(sum_ref)
    q = q_ref[...]
    qpos = qinfo_ref[:, 0:1]
    qseg = qinfo_ref[:, 1:2]
    ones = jnp.ones((8, chunk), BF)

    def step(index):
        begin = index * chunk
        here = pl.ds(begin, chunk)
        keys = kv_ref[here, :cols]
        values = kv_ref[here, cols:]
        kpos = kinfo_ref[0:1, here]
        kseg = kinfo_ref[1:2, here]
        far = jnp.where(qseg == kseg, jnp.abs(qpos - kpos), FAR)
        for head in range(heads):
            scores = dot_nt(only_head(q, head), keys) - slope_ref[head] * far
            raised = jnp.exp(scores).astype(BF)
            sum_ref[head] += dot_nt(ones, raised)
            acc_ref[head] += dot_nn(raised, values)

    each_chunk(count, step)
    total = jnp.zeros((rows, cols), F32)
    for head in range(heads):
        inv = 1.0 / sum_ref[head]
        inv_ref[head] = inv
        column = jnp.transpose(inv)[:, 0:1]
        total = total + only_head(acc_ref[head] * column, head)
    out_ref[...] = total


def attend_forward(slopes, queries, key_value, qinfo, kinfo, interpret=False):
    count, cols = queries.shape
    heads = cols // HEAD_DIM
    keys = key_value.shape[0]
    chunk = math.gcd(keys, 512)
    rows = math.gcd(count, 128)
    whole = lambda shape: pl.BlockSpec(shape, lambda i: tuple(0 for _ in shape))
    return pl.pallas_call(
        lambda *refs: forward_kernel(*refs, chunk=chunk),
        grid=(count // rows,),
        in_specs=[
            pl.BlockSpec(memory_space=pltpu.SMEM),
            pl.BlockSpec((rows, cols), lambda i: (i, 0)),
            whole((keys, 2 * cols)),
            pl.BlockSpec((rows, 2), lambda i: (i, 0)),
            whole((2, keys)),
        ],
        out_specs=[
            pl.BlockSpec((rows, cols), lambda i: (i, 0)),
            pl.BlockSpec((heads, 8, rows), lambda i: (0, 0, i)),
        ],
        out_shape=[
            jax.ShapeDtypeStruct((count, cols), F32),
            jax.ShapeDtypeStruct((heads, 8, count), F32),
        ],
        scratch_shapes=[pltpu.VMEM((heads, rows, cols), F32), pltpu.VMEM((heads, 8, rows), F32)],
        name="attend_forward",
        interpret=interpret,
    )(slopes, queries, key_value, qinfo, kinfo)


def backward_kernel(
    slope_ref, q_ref, do_ref, out_ref, inv_ref, kv_ref, qinfo_ref, kinfo_ref, dq_ref, dkv_ref, acc_ref, *, chunk
):
    rows, cols = q_ref.shape
    heads = cols // HEAD_DIM
    count = kv_ref.shape[0] // chunk
    q = q_ref[...]
    back = do_ref[...]
    product = back.astype(F32) * out_ref[...]
    qpos = qinfo_ref[0:1, :]
    qseg = qinfo_ref[1:2, :]
    acc_ref[...] = jnp.zeros_like(acc_ref)
    row_dots = []
    for head in range(heads):
        chosen = jnp.broadcast_to(head_mask(head, cols), (8, cols)).astype(F32)
        row_dots.append(
            lax.dot_general(
                chosen,
                product,
                (((1,), (1,)), ((), ())),
                precision=lax.Precision.HIGHEST,
                preferred_element_type=F32,
            )[0:1]
        )

    @pl.when(pl.program_id(0) == 0)
    def _():
        dkv_ref[...] = jnp.zeros_like(dkv_ref)

    def step(index):
        begin = index * chunk
        here = pl.ds(begin, chunk)
        keys = kv_ref[here, :cols]
        values = kv_ref[here, cols:]
        kpos = kinfo_ref[here, 0:1]
        kseg = kinfo_ref[here, 1:2]
        far = jnp.where(qseg == kseg, jnp.abs(qpos - kpos), FAR)
        key_part = jnp.zeros((chunk, cols), F32)
        value_part = jnp.zeros((chunk, cols), F32)
        for head in range(heads):
            q_head = only_head(q, head)
            back_head = only_head(back, head)
            scores = dot_nt(keys, q_head) - slope_ref[head] * far
            probs = jnp.exp(scores) * inv_ref[head, 0:1, :]
            prob_back = dot_nt(values, back_head)
            score_back = (probs * (prob_back - row_dots[head])).astype(BF)
            key_part = key_part + dot_nn(score_back, q_head)
            value_part = value_part + dot_nn(probs.astype(BF), back_head)
            acc_ref[head] += dot_tn(score_back, keys)
        dkv_ref[here, :cols] += key_part
        dkv_ref[here, cols:] += value_part

    each_chunk(count, step)
    total = jnp.zeros((rows, cols), F32)
    for head in range(heads):
        total = total + only_head(acc_ref[head], head)
    dq_ref[...] = total


def attend_backward(slopes, queries, back, mixed, inv, key_value, qinfo, kinfo, interpret=False):
    count, cols = queries.shape
    heads = cols // HEAD_DIM
    keys = key_value.shape[0]
    chunk = math.gcd(keys, 512)
    rows = math.gcd(count, 128)
    whole = lambda shape: pl.BlockSpec(shape, lambda i: tuple(0 for _ in shape))
    by_row = pl.BlockSpec((rows, cols), lambda i: (i, 0))
    return pl.pallas_call(
        lambda *refs: backward_kernel(*refs, chunk=chunk),
        grid=(count // rows,),
        in_specs=[
            pl.BlockSpec(memory_space=pltpu.SMEM),
            by_row,
            by_row,
            by_row,
            pl.BlockSpec((heads, 8, rows), lambda i: (0, 0, i)),
            whole((keys, 2 * cols)),
            pl.BlockSpec((2, rows), lambda i: (0, i)),
            whole((keys, 2)),
        ],
        out_specs=[by_row, whole((keys, 2 * cols))],
        out_shape=[
            jax.ShapeDtypeStruct((count, cols), F32),
            jax.ShapeDtypeStruct((keys, 2 * cols), F32),
        ],
        scratch_shapes=[pltpu.VMEM((heads, rows, cols), F32)],
        name="attend_backward",
        interpret=interpret,
    )(slopes, queries, back, mixed, inv, key_value, qinfo, kinfo)


def norm_stats(value):
    centre = jnp.mean(value, axis=-1, keepdims=True)
    centred = value - centre
    spread = jnp.mean(centred * centred, axis=-1, keepdims=True)
    root = lax.rsqrt(spread + 1e-06)
    return centred * root, root


def norm_back(unit, root, gain, back):
    scaled = back * gain
    return root * (
        scaled
        - jnp.mean(scaled, axis=-1, keepdims=True)
        - unit * jnp.mean(scaled * unit, axis=-1, keepdims=True)
    )


def after(value, *others):
    return lax.optimization_barrier((value,) + others)[0]


class Layout:
    def __init__(self):
        self.size = lax.axis_size("ctx")
        self.members = self.size // GROUPS
        index = lax.axis_index("ctx")
        self.group = index // self.members
        self.member = index % self.members
        self.seq = lax.axis_index("seq")
        self.rep = lax.axis_index("rep")
        self.inner = [
            [g * self.members + m for m in range(self.members)] for g in range(GROUPS)
        ]

    def shift(self, value, steps):
        n, r = self.size, self.members
        return lax.ppermute(value, "ctx", [(i, (i + steps * r) % n) for i in range(n)])

    def swap(self, value, axis):
        return lax.ppermute(value, axis, [(0, 1), (1, 0)])

    def plane(self, value, k):
        if k == 3:
            return lax.ppermute(value, ("rep", "seq"), [(i, 3 - i) for i in range(4)])
        return self.swap(value, "rep" if k == 1 else "seq")

    def gather(self, value):
        return [value] + [self.shift(value, k) for k in range(1, GROUPS)]

    def scatter_sum(self, parts):
        total = parts[0]
        for k in range(1, GROUPS):
            total = total + self.shift(parts[k].astype(BF), -k).astype(F32)
        return total

    def exchange(self, pieces):
        own = lax.dynamic_index_in_dim(pieces, self.group, 0, keepdims=False)
        out = [own]
        for k in range(1, GROUPS):
            target = (self.group + k) % GROUPS
            out.append(
                self.shift(lax.dynamic_index_in_dim(pieces, target, 0, keepdims=False), k)
            )
        return out

    def ordered(self, relative):
        line = [relative[0], relative[3], relative[2], relative[1]]
        twice = jnp.stack(line + line[:3])
        return lax.dynamic_slice_in_dim(twice, (GROUPS - self.group) % GROUPS, GROUPS, 0)

    def both_seq(self, value):
        other = self.swap(value, "seq")
        first = self.seq == 0
        return jnp.stack([jnp.where(first, value, other), jnp.where(first, other, value)])

    def partner(self, value):
        return lax.ppermute(
            value, "ctx", [(i, i ^ 1) for i in range(self.size)]
        )

    def all_members(self, value, axis):
        if self.members == 2:
            other = self.partner(value)
            first = self.member == 0
            return jnp.stack(
                [jnp.where(first, value, other), jnp.where(first, other, value)], axis
            )
        out = lax.all_gather(value, "ctx", axis_index_groups=self.inner)
        return jnp.moveaxis(out, 0, axis)

    def member_sum(self, pieces):
        if self.members == 2:
            keep = lax.dynamic_index_in_dim(pieces, self.member, 0, keepdims=False)
            give = lax.dynamic_index_in_dim(pieces, 1 - self.member, 0, keepdims=False)
            return keep + self.partner(give.astype(BF)).astype(F32)
        got = lax.all_to_all(
            pieces.astype(BF), "ctx", 0, 0, axis_index_groups=self.inner, tiled=True
        )
        return jnp.sum(got.astype(F32), axis=0)

    def seq_sum(self, pieces):
        keep = lax.dynamic_index_in_dim(pieces, self.seq, 0, keepdims=False)
        give = lax.dynamic_index_in_dim(pieces, 1 - self.seq, 0, keepdims=False)
        return keep + self.swap(give.astype(BF), "seq").astype(F32)

    def rep_sum(self, value):
        low = value.astype(BF)
        return low.astype(F32) + self.swap(low, "rep").astype(F32)


def on_device(
    tokens,
    segments,
    joined_weight,
    query_bias,
    value_bias,
    output_weight,
    output_bias,
    first_gain,
    first_shift,
    widen_weight,
    widen_bias,
    narrow_weight,
    narrow_bias,
    final_gain,
    final_shift,
    cotangent,
):
    at = Layout()
    n, r = at.size, at.members
    rows, width = tokens.shape[1:]
    heads = width // HEAD_DIM
    near_heads = heads // GROUPS
    cols = near_heads * HEAD_DIM
    kb = joined_weight.shape[0]
    ff_own = narrow_weight.shape[0]
    ff = ff_own * 2 * n
    quarter = ff // GROUPS
    span = r * ff_own
    seg_row = segments[0]
    length = seg_row.shape[0]
    scale = 1.0 / math.sqrt(HEAD_DIM)
    inputs = tokens[0]

    x_rel = at.gather(inputs)
    x_four = jnp.concatenate(x_rel, axis=0)

    small = jnp.concatenate(
        [
            query_bias,
            value_bias,
            output_bias,
            first_gain,
            first_shift,
            narrow_bias,
            final_gain,
            final_shift,
            widen_bias,
        ]
    )[None]
    small_all = at.all_members(at.both_seq(at.ordered(at.gather(small))), 2)
    small_all = small_all.reshape(2 * n, -1).astype(F32)

    def vector(place):
        return small_all[:, place * kb : (place + 1) * kb].reshape(width)

    b_query, b_value, b_output, g_first, s_first, b_narrow, g_final, s_final = (
        vector(place) for place in range(8)
    )
    b_widen = lax.dynamic_index_in_dim(
        small_all[:, 8 * kb :].reshape(2, 2, GROUPS, span), at.group, 2, keepdims=False
    ).reshape(2 * quarter)
    b_query = lax.dynamic_index_in_dim(b_query.reshape(GROUPS, cols), at.group, 0, keepdims=False)
    b_value = lax.dynamic_index_in_dim(b_value.reshape(GROUPS, cols), at.group, 0, keepdims=False)

    joined_cut = jnp.transpose(joined_weight.reshape(kb, 3, GROUPS, cols), (2, 0, 1, 3)).reshape(
        GROUPS, kb, 3 * cols
    )
    w_joined = at.all_members(at.both_seq(at.ordered(at.exchange(joined_cut))), 2).reshape(
        width, 3 * cols
    )

    output_low = after(output_weight, x_four)
    out_rel = at.ordered(at.gather(output_low)).reshape(GROUPS * kb, width)
    both = at.both_seq(jnp.concatenate([out_rel, narrow_weight], axis=0))
    both = at.all_members(both, 1)
    w_output = jnp.transpose(
        both[:, :, : GROUPS * kb].reshape(2, r, GROUPS, kb, width), (0, 2, 1, 3, 4)
    ).reshape(width, width)
    w_narrow = both[:, :, GROUPS * kb :].reshape(quarter, width)

    widen_cut = jnp.transpose(
        after(widen_weight, x_four).reshape(kb, 4, GROUPS, span), (2, 0, 1, 3)
    ).reshape(GROUPS, kb, 2 * quarter)
    w_widen = at.all_members(at.both_seq(at.ordered(at.exchange(widen_cut))), 2).reshape(
        width, 2 * quarter
    )

    lanes = jnp.arange(rows, dtype=jnp.int32)
    near = (at.group - jnp.arange(GROUPS, dtype=jnp.int32)) % GROUPS

    def places(member):
        return ((near * r + member)[:, None] * rows + lanes[None]).reshape(-1)

    if r == 2:
        key_members = jnp.stack([at.member, 1 - at.member])
    else:
        key_members = jnp.arange(r, dtype=jnp.int32)
    query_pos = places(at.member)
    key_pos = jnp.concatenate([places(key_members[i]) for i in range(r)])
    query_seg = jnp.take(seg_row, query_pos)
    key_seg = jnp.take(seg_row, key_pos)
    q_info = jnp.stack([query_pos, query_seg]).astype(F32)
    k_info = jnp.stack([key_pos, key_seg]).astype(F32)
    order_heads = at.group * near_heads + jnp.arange(near_heads, dtype=jnp.int32)
    slopes = jnp.power(2.0, -8.0 * (order_heads.astype(F32) + 1.0) / heads) * (512.0 / length)

    joined = dot_nn(x_four, w_joined)
    queries = ((joined[:, :cols] + b_query) * scale).astype(BF)
    kv_own = jnp.concatenate(
        [joined[:, cols : 2 * cols], joined[:, 2 * cols :] + b_value], axis=1
    ).astype(BF)
    if r == 2:
        key_value = jnp.concatenate([kv_own, at.partner(kv_own)], axis=0)
    else:
        key_value = at.all_members(kv_own, 0).reshape(-1, 2 * cols)
    mixed_near, inv = attend_forward(slopes, queries, key_value, jnp.transpose(q_info), k_info)
    mixed_low = mixed_near.astype(BF).reshape(GROUPS, rows, cols)
    mixed_rel = [mixed_low[0]] + [at.shift(mixed_low[k], -k) for k in range(1, GROUPS)]
    mixed_rel = [mixed_rel[0], mixed_rel[3], mixed_rel[2], mixed_rel[1]]
    mixed = jnp.transpose(at.ordered(mixed_rel), (1, 0, 2)).reshape(rows, width)

    first_in = inputs.astype(F32) + dot_nn(mixed, w_output) + b_output
    first_unit, first_root = norm_stats(first_in)
    first = first_unit * g_first + s_first
    first_low = first.astype(BF)

    first_four = jnp.concatenate(at.gather(first_low), axis=0)
    gate_up = dot_nn(first_four, w_widen) + b_widen
    gate, up = gate_up[:, :quarter], gate_up[:, quarter:]
    phi_big = 0.5 * (1.0 + lax.erf(gate * math.sqrt(0.5)))
    gelu = gate * phi_big
    slope_gate = phi_big + gate * jnp.exp(-0.5 * gate * gate) * (1.0 / math.sqrt(2.0 * math.pi))
    hidden = (gelu * up).astype(BF)
    final_part = dot_nn(hidden, w_narrow).reshape(GROUPS, rows, width)
    final_in = first + at.scatter_sum([final_part[k] for k in range(GROUPS)]) + b_narrow
    final_unit, final_root = norm_stats(final_in)
    result = final_unit * g_final + s_final

    upstream = cotangent[0].astype(F32)
    final_back = norm_back(final_unit, final_root, g_final, upstream)
    final_gain_grad = jnp.sum(upstream * final_unit, axis=0)
    final_shift_grad = jnp.sum(upstream, axis=0)
    narrow_back = final_back.astype(BF)
    narrow_bias_grad = jnp.sum(narrow_back.astype(F32), axis=0)
    back_four = jnp.concatenate(at.gather(narrow_back), axis=0)
    hidden_back = dot_nt(back_four, w_narrow)
    widen_back = jnp.concatenate(
        [hidden_back * up * slope_gate, hidden_back * gelu], axis=1
    ).astype(BF)
    first_part = dot_nt(widen_back, w_widen).reshape(GROUPS, rows, width)
    first_back = final_back + at.scatter_sum([first_part[k] for k in range(GROUPS)])
    narrow_grad = dot_tn(hidden, back_four)
    widen_grad = dot_tn(first_four, widen_back)
    widen_bias_grad = jnp.sum(widen_back.astype(F32), axis=0)

    attn_back = norm_back(first_unit, first_root, g_first, first_back)
    first_gain_grad = jnp.sum(first_back * first_unit, axis=0)
    first_shift_grad = jnp.sum(first_back, axis=0)
    output_back = attn_back.astype(BF)
    output_bias_grad = jnp.sum(output_back.astype(F32), axis=0)
    output_grad = dot_tn(mixed, output_back)
    mixed_back = dot_nt(output_back, w_output).astype(BF)
    mixed_back = jnp.transpose(mixed_back.reshape(rows, GROUPS, cols), (1, 0, 2))
    back_near = jnp.concatenate(at.exchange(mixed_back), axis=0)

    query_sum, kv_sum = attend_backward(
        slopes, queries, back_near, mixed_near, inv, key_value, q_info, jnp.transpose(k_info)
    )
    if r == 2:
        half = kv_sum.shape[0] // 2
        kv_back = kv_sum[:half] + at.partner(kv_sum[half:].astype(BF)).astype(F32)
    else:
        kv_back = at.member_sum(kv_sum.reshape(r, -1, 2 * cols))
    query_low = query_sum.astype(BF)
    query_scaled = (query_low.astype(F32) * scale).astype(BF)
    joined_back = jnp.concatenate([query_scaled, kv_back.astype(BF)], axis=1)
    tokens_part = dot_nt(joined_back, w_joined).reshape(GROUPS, rows, width)
    tokens_grad = attn_back + at.scatter_sum([tokens_part[k] for k in range(GROUPS)])
    joined_grad = dot_tn(x_four, joined_back)
    near_bias = jnp.sum(joined_back.astype(F32), axis=0)
    query_bias_grad = near_bias[:cols]
    value_bias_grad = near_bias[2 * cols :]

    narrow_sum = at.member_sum(jnp.transpose(narrow_grad.reshape(2, r, ff_own, width), (1, 0, 2, 3)))
    narrow_total = at.rep_sum(at.seq_sum(narrow_sum))

    def to_rows(grad):
        pieces = jnp.transpose(grad.reshape(2, GROUPS, r, kb, -1), (2, 0, 1, 3, 4))
        mine = at.rep_sum(at.seq_sum(at.member_sum(pieces))).astype(BF)
        return at.ordered(at.exchange(mine))

    widen_total = jnp.transpose(
        to_rows(widen_grad).reshape(GROUPS, kb, 4, span), (1, 2, 0, 3)
    ).reshape(kb, 2 * ff)
    joined_total = jnp.transpose(
        to_rows(joined_grad).reshape(GROUPS, kb, 3, cols), (1, 2, 0, 3)
    ).reshape(kb, 3 * width)

    def spread(vector, parts):
        wide = jnp.zeros((parts, GROUPS, vector.shape[0] // parts), F32)
        return lax.dynamic_update_slice_in_dim(
            wide, vector.reshape(parts, 1, -1), at.group, 1
        ).reshape(-1)

    vectors = [
        spread(query_bias_grad, 1),
        spread(value_bias_grad, 1),
        output_bias_grad,
        first_gain_grad,
        first_shift_grad,
        narrow_bias_grad,
        final_gain_grad,
        final_shift_grad,
    ]
    row = jnp.concatenate(
        [item.reshape(2 * n, kb) for item in vectors]
        + [spread(widen_bias_grad, 4).reshape(2 * n, 8 * kb)],
        axis=1,
    )
    row = jnp.pad(row[:, None, :], ((0, 0), (0, 15), (0, width - 16 * kb)))
    packed = jnp.concatenate([output_grad.reshape(2 * n, kb, width), row], axis=1)
    packed = jnp.transpose(packed.reshape(2, GROUPS, r, kb + 16, width), (2, 0, 1, 3, 4))
    packed = at.seq_sum(at.member_sum(packed)).astype(BF)
    packed = at.exchange(packed)
    packed = sum(item.astype(F32) for item in packed[1:]) + packed[0].astype(F32)
    packed = at.rep_sum(packed)
    output_total = packed[:kb]
    last = packed[kb]

    def owned(place):
        return last[place * kb : (place + 1) * kb]

    return (
        result.astype(BF)[None],
        tokens_grad[None],
        joined_total.astype(F32),
        owned(0),
        owned(1),
        output_total,
        owned(2),
        owned(3),
        owned(4),
        widen_total.astype(F32),
        last[8 * kb : 16 * kb],
        narrow_total,
        owned(5),
        owned(6),
        owned(7),
    )


def vmem(shape):
    return pl.BlockSpec(shape, lambda *_: tuple(0 for _ in shape))


COSTS = {
    "pack_joined": 0,
    "assemble_joined": 0,
    "pick_widen": 0,
    "pack_widen": 0,
    "split_joined": 3,
    "attend": 5,
    "attend_back": 8,
    "close_attention": 3,
    "widen_narrow": 6,
    "widen_narrow_back": 7,
    "turn_final": 3,
    "turn_first": 3,
    "wide_grads": 6,
    "output_grads": 3,
    "tokens_parts": 4,
    "joined_grads": 4,
    "finish_widen": 3,
    "finish_joined": 2,
}

SMEM = pl.BlockSpec(memory_space=pltpu.SMEM)


def call(body, name, inputs, outputs, scratch=(), grid=(1,), in_specs=None, out_specs=None, flops=0):
    shapes = [jax.ShapeDtypeStruct(shape, kind) for shape, kind in outputs]
    if in_specs is None:
        in_specs = [SMEM if item.ndim == 1 else vmem(item.shape) for item in inputs]
    if out_specs is None:
        out_specs = [vmem(shape) for shape, kind in outputs]
    moved = sum(item.size * item.dtype.itemsize for item in list(inputs) + shapes)
    return pl.pallas_call(
        body,
        grid=grid,
        in_specs=in_specs,
        out_specs=out_specs,
        out_shape=shapes,
        scratch_shapes=list(scratch),
        name=name,
        cost_estimate=pl.CostEstimate(flops=int(COSTS[name] * 5 * 1e9), transcendentals=0, bytes_accessed=0),
    )(*inputs)


def pack_joined(ids, weight, vectors, widen_bias, cols):
    kb = weight.shape[0]
    vectors = [item[None] for item in vectors]
    shape = (kb + 16, 3 * cols)

    def body(*refs):
        ids_ref, w_ref, wide_ref = refs[0], refs[1], refs[10]
        all_ref = refs[15]
        rows = [ref[...].astype(F32) for ref in refs[2:10]]
        wide = wide_ref[...].astype(F32)
        rows += [wide[:, k * kb : (k + 1) * kb] for k in range(8)]
        small = jnp.concatenate(rows, axis=0).astype(BF)
        for g in range(GROUPS):
            for part in range(3):
                at = (part * GROUPS + g) * cols
                all_ref[g, :kb, part * cols : (part + 1) * cols] = w_ref[:, at : at + cols]
            all_ref[g, kb:, :] = jnp.zeros((16, 3 * cols), BF)
            all_ref[g, kb:, :kb] = small
        for k in range(GROUPS):
            refs[11 + k][...] = all_ref[(ids_ref[0] + k) % GROUPS]

    inputs = [ids, weight] + vectors + [widen_bias[None]]
    return call(
        body,
        "pack_joined",
        inputs,
        [(shape, BF)] * GROUPS,
        scratch=[pltpu.VMEM((GROUPS,) + shape, BF)],
    )


def place_rows(ids_ref, pieces, out_ref, kb, relative=False):
    group, m, y = ids_ref[0], ids_ref[1], ids_ref[2]
    for index, piece in enumerate(pieces):
        row = y if index % 2 == 0 else 1 - y
        member = m if index < 2 else 1 - m
        for g in range(GROUPS):
            source = (group + GROUPS - g) % GROUPS if relative else g
            start = pl.multiple_of((row * GROUPS * 2 + source * 2 + member) * kb, 16)
            out_ref[pl.ds(start, kb), :] = piece[g, :kb, :]


def assemble_joined(ids, pieces, kb):
    cols = pieces[0].shape[2]
    near = cols // 3
    width = 4 * GROUPS * kb
    span = 8 * kb

    def body(ids_ref, a_ref, b_ref, c_ref, d_ref, w_ref, vec_ref, near_ref, wide_ref):
        place_rows(ids_ref, (a_ref, b_ref, c_ref, d_ref), w_ref, kb, True)
        g, m, y, x = ids_ref[0], ids_ref[1], ids_ref[2], ids_ref[3]
        blocks = []
        for row in range(2):
            for k in range(GROUPS):
                for member in range(2):
                    turn = (g + GROUPS - k) % GROUPS
                    picks = [ref[turn, kb:, :kb].astype(F32) for ref in (a_ref, b_ref, c_ref, d_ref)]
                    mine = jnp.where(row == y, picks[0], picks[1])
                    theirs = jnp.where(row == y, picks[2], picks[3])
                    blocks.append(jnp.where(member == m, mine, theirs))
        vec = jnp.concatenate(blocks, axis=1)
        vec_ref[...] = vec
        total = jnp.zeros((16, near), F32)
        for k in range(GROUPS):
            total = jnp.where(g == k, vec[:, k * near : (k + 1) * near], total)
        near_ref[...] = total
        lines = []
        for part in range(2):
            for c in range(8):
                low = 8 + (c % 2) * 4
                picks = []
                for row in range(2):
                    at = (part * 8 + row * 4 + c // 2) * kb
                    picks.append(vec[low : low + 4, at : at + kb])
                both = jnp.where(y == 0, picks[0], picks[1])
                pair = jnp.where(x == 0, both[0:2], both[2:4])
                lines += [pair[0:1], pair[1:2]]
        wide_ref[...] = jnp.concatenate(lines, axis=1)

    return call(
        body,
        "assemble_joined",
        [ids] + list(pieces),
        [((width, cols), BF), ((16, width), F32), ((16, near), F32), ((1, 4 * span), F32)],
    )


def pick_widen(ids, weight, narrow):
    kb, total = weight.shape
    own, width = narrow.shape
    half = own // 2
    side = total // 4
    count = side // own
    quarter = count * half

    wide = 2 * quarter

    def body(ids_ref, w_ref, n_ref, near_ref, far_ref, low_ref, all_ref):
        y, x = ids_ref[2], ids_ref[3]
        for row in range(2):
            for col in range(2):
                pieces = []
                for part in range(2):
                    for c in range(count):
                        at = part * 2 * side + row * side + c * own + col * half
                        pieces.append(w_ref[:, at : at + half])
                all_ref[row * 2 + col] = jnp.concatenate(pieces, axis=1)
        near_ref[...] = all_ref[y * 2 + x]
        far_ref[...] = all_ref[(1 - y) * 2 + x]
        low_ref[...] = n_ref[pl.ds(pl.multiple_of(x * half, 16), half), :]

    return call(
        body,
        "pick_widen",
        [ids, weight, narrow],
        [((kb, wide), BF), ((kb, wide), BF), ((half, width), BF)],
        scratch=[pltpu.VMEM((4, kb, wide), BF)],
    )


def pack_widen(ids, near, got, low):
    kb, cols = near.shape
    width = low.shape[1]

    def body(ids_ref, near_ref, got_ref, low_ref, out_ref):
        y = ids_ref[2]
        out_ref[pl.ds(pl.multiple_of(y * kb, 16), kb), :cols] = near_ref[...]
        out_ref[pl.ds(pl.multiple_of((1 - y) * kb, 16), kb), :cols] = got_ref[...]
        out_ref[:, cols:] = low_ref[...]

    return call(body, "pack_widen", [ids, near, got, low], [((2 * kb, cols + width), BF)])[0]


def owner_order(value, kb):
    half = value.shape[1] // (2 * kb)
    blocks = [y * half + c for c in range(half) for y in range(2)]
    return jnp.concatenate([value[:, b * kb : (b + 1) * kb] for b in blocks], axis=1)


def column_order(value, kb):
    half = value.shape[1] // (2 * kb)
    blocks = [c * 2 + y for y in range(2) for c in range(half)]
    return jnp.concatenate([value[:, b * kb : (b + 1) * kb] for b in blocks], axis=1)


def split_joined(x_four, weight, near, scale):
    count, width = x_four.shape
    cols = weight.shape[1] // 3

    def body(x_ref, w_ref, near_ref, q_ref, kv_ref):
        joined = dot_nn(x_ref[...], w_ref[...])
        q_ref[...] = ((joined[:, :cols] + near_ref[0:1, :]) * scale).astype(BF)
        kv_ref[:, :cols] = joined[:, cols : 2 * cols].astype(BF)
        kv_ref[:, cols:] = (joined[:, 2 * cols :] + near_ref[1:2, :]).astype(BF)

    return call(
        body,
        "split_joined",
        [x_four, weight, near],
        [((count, cols), BF), ((count, 2 * cols), BF)],
        flops=2 * count * width * 3 * cols,
    )


def piece_rows(ids_ref, k, rows, sign=1):
    turn = (ids_ref[0] + (k if sign > 0 else GROUPS - k)) % GROUPS
    return pl.ds(pl.multiple_of(turn * rows, 16), rows)


def attend(ids, slopes, queries, kv_own, kv_other, q_col, k_row):
    count, cols = queries.shape
    heads = cols // HEAD_DIM
    rows = count // GROUPS
    chunk = kv_own.shape[0]

    def body(ids_ref, slope_ref, q_ref, own_ref, other_ref, qi_ref, ki_ref, out_ref, inv_ref, *sends):
        q = q_ref[...]
        qpos = qi_ref[:, 0:1]
        qseg = qi_ref[:, 1:2]
        ones = jnp.ones((chunk, 64), BF)
        q_heads = [only_head(q, head) for head in range(heads)]
        accs = [None] * heads
        for side, kv_ref in enumerate((own_ref, other_ref)):
            here = slice(side * chunk, (side + 1) * chunk)
            keys = kv_ref[:, :cols]
            values = jnp.concatenate([kv_ref[:, cols:], ones], axis=1)
            far = jnp.where(qseg == ki_ref[1:2, here], jnp.abs(qpos - ki_ref[0:1, here]), FAR)
            for head in range(heads):
                scores = dot_nt(q_heads[head], keys) - slope_ref[head] * far
                part = dot_nn(jnp.exp(scores).astype(BF), values)
                accs[head] = part if side == 0 else accs[head] + part
        total = jnp.zeros((count, cols), F32)
        for head in range(heads):
            inv = 1.0 / accs[head][:, cols : cols + 1]
            inv_ref[head] = jnp.transpose(jnp.broadcast_to(inv, (count, 128)))[:8]
            total = total + only_head(accs[head][:, :cols] * inv, head)
        out_ref[...] = total
        for k, ref in enumerate(sends):
            ref[...] = out_ref[piece_rows(ids_ref, k, rows), :].astype(BF)

    return call(
        body,
        "attend",
        [ids, slopes, queries, kv_own, kv_other, q_col, k_row],
        [((count, cols), F32), ((heads, 8, count), F32)] + [((rows, cols), BF)] * GROUPS,
        flops=4 * count * 2 * chunk * cols,
    )


def attend_back(ids, slopes, queries, back_rel, mixed, inv, kv_own, kv_other, q_row, k_col, scale):
    count, cols = queries.shape
    heads = cols // HEAD_DIM
    rows = count // GROUPS
    chunk = kv_own.shape[0]

    def body(ids_ref, slope_ref, q_ref, *refs):
        pieces = refs[:GROUPS]
        out_ref, inv_ref, own_ref, other_ref, qi_ref, ki_ref, dq_ref, keep_ref, give_ref, do_ref = refs[GROUPS:]
        for k, ref in enumerate(pieces):
            do_ref[piece_rows(ids_ref, k, rows, -1), :] = ref[...]
        q = q_ref[...]
        back = do_ref[...]
        product = back.astype(F32) * out_ref[...]
        qpos = qi_ref[0:1, :]
        qseg = qi_ref[1:2, :]
        q_heads = [only_head(q, head) for head in range(heads)]
        b_heads = [only_head(back, head) for head in range(heads)]
        place = lax.broadcasted_iota(jnp.int32, (8, cols), 0)
        lane = lax.broadcasted_iota(jnp.int32, (8, cols), 1)
        row_dots = lax.dot_general(
            (lane // HEAD_DIM == place).astype(F32),
            product,
            (((1,), (1,)), ((), ())),
            precision=lax.Precision.HIGHEST,
            preferred_element_type=F32,
        )
        query_parts = [None] * heads
        for side, kv_ref in enumerate((own_ref, other_ref)):
            here = slice(side * chunk, (side + 1) * chunk)
            keys = kv_ref[:, :cols]
            values = kv_ref[:, cols:]
            far = jnp.where(qseg == ki_ref[here, 1:2], jnp.abs(qpos - ki_ref[here, 0:1]), FAR)
            key_part = None
            value_part = None
            for head in range(heads):
                scores = dot_nt(keys, q_heads[head]) - slope_ref[head] * far
                probs = jnp.exp(scores) * inv_ref[head, 0:1, :]
                prob_back = dot_nt(values, b_heads[head])
                score_back = (probs * (prob_back - row_dots[head : head + 1])).astype(BF)
                k_part = dot_nn(score_back, q_heads[head])
                v_part = dot_nn(probs.astype(BF), b_heads[head])
                q_part = dot_tn(score_back, keys)
                key_part = k_part if head == 0 else key_part + k_part
                value_part = v_part if head == 0 else value_part + v_part
                query_parts[head] = q_part if side == 0 else query_parts[head] + q_part
            target = keep_ref if side == 0 else give_ref
            target[:, :cols] = key_part.astype(target.dtype)
            target[:, cols:] = value_part.astype(target.dtype)
        total = jnp.zeros((count, cols), F32)
        for head in range(heads):
            total = total + only_head(query_parts[head], head)
        dq_ref[...] = (total.astype(BF).astype(F32) * scale).astype(BF)

    return call(
        body,
        "attend_back",
        [ids, slopes, queries] + list(back_rel) + [mixed, inv, kv_own, kv_other, q_row, k_col],
        [((count, cols), BF), ((chunk, 2 * cols), F32), ((chunk, 2 * cols), BF)],
        scratch=[pltpu.VMEM((count, cols), BF)],
        flops=10 * count * 2 * chunk * cols,
    )


def close_attention(ids, inputs, mixed_rel, weight, vec, kb):
    rows, width = inputs.shape
    cols = mixed_rel[0].shape[1]

    def body(ids_ref, x_ref, a_ref, b_ref, c_ref, d_ref, w_ref, vec_ref, first_ref, low_ref, unit_ref, root_ref):
        total = x_ref[...].astype(F32) + vec_ref[2:3, :]
        for k, ref in enumerate((a_ref, b_ref, c_ref, d_ref)):
            total = total + dot_nn(ref[...], w_ref[piece_rows(ids_ref, k, cols, -1), :])
        unit, root = norm_stats(total)
        first = unit * vec_ref[3:4, :] + vec_ref[4:5, :]
        first_ref[...] = first
        low_ref[...] = owner_order(first, kb).astype(BF)
        unit_ref[...] = unit
        root_ref[...] = root

    return call(
        body,
        "close_attention",
        [ids, inputs] + list(mixed_rel) + [weight, vec],
        [((rows, width), F32), ((rows, width), BF), ((rows, width), F32), ((rows, 1), F32)],
        flops=2 * rows * width * width,
    )


def block_of(quarter):
    return math.gcd(quarter, 256)


def join_pieces(refs):
    return jnp.concatenate([ref[...] for ref in refs], axis=0)


def send_pieces(total, refs, rows):
    for k, ref in enumerate(refs):
        ref[...] = total[k * rows : (k + 1) * rows, :].astype(ref.dtype)


def widen_narrow(rel, weights, wide):
    rows, width = rel[0].shape
    quarter = wide.shape[1] // 2
    count = GROUPS * rows

    def body(*refs):
        w_ref, wide_ref = refs[4:6]
        hid_ref, gate_ref, up_ref = refs[10:13]
        value = join_pieces(refs[:4])
        gate = dot_nn(value, w_ref[:, :quarter]) + wide_ref[:, :quarter]
        up = dot_nn(value, w_ref[:, quarter : 2 * quarter]) + wide_ref[:, quarter:]
        gate_ref[...] = gate
        up_ref[...] = up
        hidden = (gate * (0.5 + 0.5 * lax.erf(gate * math.sqrt(0.5))) * up).astype(BF)
        hid_ref[...] = hidden
        send_pieces(dot_nn(hidden, w_ref[:, 2 * quarter :]), refs[6:10], rows)

    return call(
        body,
        "widen_narrow",
        list(rel) + [weights, wide],
        [((rows, width), F32)]
        + [((rows, width), BF)] * 3
        + [((count, quarter), BF), ((count, quarter), F32), ((count, quarter), F32)],
        flops=6 * count * width * quarter,
    )


def gate_slopes(gate, up):
    phi_big = 0.5 + 0.5 * lax.erf(gate * math.sqrt(0.5))
    slope = phi_big + gate * jnp.exp(-0.5 * gate * gate) * (1.0 / math.sqrt(2.0 * math.pi))
    return up * slope, gate * phi_big


def widen_narrow_back(rel, weights, gate_factor, up_factor):
    rows, width = rel[0].shape
    count, quarter = gate_factor.shape

    def body(*refs):
        w_ref, gf_ref, uf_ref = refs[4:7]
        bg_ref, bu_ref = refs[11:13]
        hidden_back = dot_nt(join_pieces(refs[:4]), w_ref[:, 2 * quarter :])
        gate_back = (hidden_back * gf_ref[...]).astype(BF)
        up_back = (hidden_back * uf_ref[...]).astype(BF)
        bg_ref[...] = gate_back
        bu_ref[...] = up_back
        total = dot_nt(gate_back, w_ref[:, :quarter]) + dot_nt(up_back, w_ref[:, quarter : 2 * quarter])
        send_pieces(total, refs[7:11], rows)

    return call(
        body,
        "widen_narrow_back",
        list(rel) + [weights, gate_factor, up_factor],
        [((rows, width), F32)] + [((rows, width), BF)] * 3 + [((count, quarter), BF)] * 2,
        flops=6 * count * width * quarter,
    )


def turn_final(own, received, first, upstream, vec):
    rows, width = own.shape

    def body(own_ref, a_ref, b_ref, c_ref, first_ref, up_ref, vec_ref, res_ref, back_ref, low_ref, sum_ref):
        total = first_ref[...] + vec_ref[5:6, :] + own_ref[...]
        for ref in (a_ref, b_ref, c_ref):
            total = total + ref[...].astype(F32)
        unit, root = norm_stats(total)
        gain = vec_ref[6:7, :]
        res_ref[...] = (unit * gain + vec_ref[7:8, :]).astype(BF)
        upstream = up_ref[...].astype(F32)
        back = norm_back(unit, root, gain, upstream)
        low = back.astype(BF)
        back_ref[...] = back
        low_ref[...] = low
        sum_ref[...] = jnp.zeros_like(sum_ref)
        sum_ref[0:1, :] = jnp.sum(low.astype(F32), axis=0, keepdims=True)
        sum_ref[1:2, :] = jnp.sum(upstream * unit, axis=0, keepdims=True)
        sum_ref[2:3, :] = jnp.sum(upstream, axis=0, keepdims=True)

    return call(
        body,
        "turn_final",
        [own] + list(received) + [first, upstream, vec],
        [((rows, width), BF), ((rows, width), F32), ((rows, width), BF), ((8, width), F32)],
    )


def turn_first(ids, own, received, final_back, unit, root, weight, vec, kb):
    rows, width = own.shape
    cols = width // GROUPS

    def body(ids_ref, own_ref, a_ref, b_ref, c_ref, fb_ref, unit_ref, root_ref, w_ref, vec_ref, *outs):
        attn_ref, low_ref, sum_ref = outs[:3]
        total = own_ref[...]
        for ref in (a_ref, b_ref, c_ref):
            total = total + ref[...].astype(F32)
        total = fb_ref[...] + column_order(total, kb)
        unit = unit_ref[...]
        back = norm_back(unit, root_ref[...], vec_ref[3:4, :], total)
        low = back.astype(BF)
        attn_ref[...] = back
        low_ref[...] = low
        for k, ref in enumerate(outs[3:]):
            ref[...] = dot_nt(low, w_ref[piece_rows(ids_ref, k, cols), :]).astype(BF)
        sum_ref[...] = jnp.zeros_like(sum_ref)
        sum_ref[0:1, :] = jnp.sum(low.astype(F32), axis=0, keepdims=True)
        sum_ref[1:2, :] = jnp.sum(total * unit, axis=0, keepdims=True)
        sum_ref[2:3, :] = jnp.sum(total, axis=0, keepdims=True)

    return call(
        body,
        "turn_first",
        [ids, own] + list(received) + [final_back, unit, root, weight, vec],
        [((rows, width), F32), ((rows, width), BF), ((8, width), F32)] + [((rows, cols), BF)] * GROUPS,
        flops=2 * rows * width * width,
    )


def split_rows(ids_ref, full_ref, keep_ref, give_ref, kb, lead=()):
    m, y = ids_ref[1], ids_ref[2]
    for turn in range(2):
        row = y if turn == 0 else 1 - y
        for g in range(GROUPS):
            base = (row * GROUPS + g) * 2
            mine = pl.ds(pl.multiple_of((base + m) * kb, 16), kb)
            other = pl.ds(pl.multiple_of((base + 1 - m) * kb, 16), kb)
            keep_ref[lead + (turn, g, slice(0, kb), slice(None))] = full_ref[mine, :]
            give_ref[lead + (turn, g, slice(0, kb), slice(None))] = full_ref[other, :].astype(BF)


def wide_grads(first_rel, gate_back, up_back, hidden, back_rel):
    rows, width = first_rel[0].shape
    count, quarter = gate_back.shape

    def body(*refs):
        gate_ref, up_ref, hid_ref = refs[8:11]
        out_ref, gs_ref, us_ref = refs[11:14]
        value = join_pieces(refs[:4])
        for turn, (ref, sum_ref) in enumerate(((gate_ref, gs_ref), (up_ref, us_ref))):
            back = ref[...]
            out_ref[:, turn * quarter : (turn + 1) * quarter] = dot_tn(value, back).astype(BF)
            sum_ref[...] = jnp.sum(back.astype(F32), axis=0, keepdims=True)
        out_ref[:, 2 * quarter :] = dot_tn(hid_ref[...], join_pieces(refs[4:8])).astype(BF)

    return call(
        body,
        "wide_grads",
        list(first_rel) + list(back_rel) + [gate_back, up_back, hidden],
        [((width, 2 * quarter + width), BF), ((1, quarter), F32), ((1, quarter), F32)],
        flops=6 * count * width * quarter,
    )


def place_small(ids_ref, blocks, keep_ref, give_ref, kb):
    m, y = ids_ref[1], ids_ref[2]
    for turn in range(2):
        for g in range(GROUPS):
            picked = []
            for member in range(2):
                first = jnp.where(y == 0, blocks[0][g][member], blocks[1][g][member])
                second = jnp.where(y == 0, blocks[1][g][member], blocks[0][g][member])
                picked.append(first if turn == 0 else second)
            cols = keep_ref.shape[3]
            mine = jnp.where(m == 0, picked[0], picked[1])
            other = jnp.where(m == 0, picked[1], picked[0])
            keep_ref[turn, g, kb:, :] = jnp.zeros((16, cols), F32)
            give_ref[turn, g, kb:, :] = jnp.zeros((16, cols), BF)
            keep_ref[turn, g, kb:, :kb] = mine
            give_ref[turn, g, kb:, :kb] = other.astype(BF)


def output_grads(ids, mixed_rel, back, first_sums, final_sums, gate_sum, up_sum, kb):
    rows, width = back.shape
    cols = mixed_rel[0].shape[1]

    def body(ids_ref, *refs):
        back_ref, fs_ref, ls_ref, gs_ref, us_ref, keep_ref, give_ref, full_ref = refs[GROUPS:]
        for k, ref in enumerate(refs[:GROUPS]):
            full_ref[piece_rows(ids_ref, k, cols, -1), :] = dot_tn(ref[...], back_ref[...])
        split_rows(ids_ref, full_ref, keep_ref, give_ref, kb)
        y, x = ids_ref[2], ids_ref[3]
        sums = jnp.concatenate([fs_ref[0:3, :], ls_ref[0:3, :]], axis=0)
        wide = (gs_ref[...], us_ref[...])
        blocks = []
        for row in range(2):
            blocks.append([])
            for g in range(GROUPS):
                blocks[-1].append([])
                for member in range(2):
                    b = row * 8 + g * 2 + member
                    lines = []
                    for i in range(8):
                        at = ((b % 4) * 4 + (i // 4) * 2 + i % 2) * kb
                        mine = (y == (b % 8) // 4) & (x == (i % 4) // 2)
                        lines.append(jnp.where(mine, wide[b // 8][:, at : at + kb], 0.0))
                    lines = [sums[:, b * kb : (b + 1) * kb]] + lines + [jnp.zeros((2, kb), F32)]
                    blocks[-1][-1].append(jnp.concatenate(lines, axis=0))
        place_small(ids_ref, blocks, keep_ref, give_ref, kb)

    shape = (2, GROUPS, kb + 16, width)
    return call(
        body,
        "output_grads",
        [ids] + list(mixed_rel) + [back, first_sums, final_sums, gate_sum, up_sum],
        [(shape, F32), (shape, BF)],
        scratch=[pltpu.VMEM((width, width), F32)],
        flops=2 * rows * width * width,
    )


def tokens_parts(ids, back, weight):
    count, cols = back.shape
    rows = count // GROUPS
    width = weight.shape[0]

    def body(ids_ref, jb_ref, w_ref, *outs):
        for k, ref in enumerate(outs):
            part = dot_nt(jb_ref[piece_rows(ids_ref, k, rows, -1), :], w_ref[...])
            ref[...] = part.astype(ref.dtype)

    return call(
        body,
        "tokens_parts",
        [ids, back, weight],
        [((rows, width), F32)] + [((rows, width), BF)] * 3,
        flops=2 * count * width * cols,
    )


def joined_grads(ids, x_four, query_back, keep, got, kb):
    count, width = x_four.shape
    cols = query_back.shape[1]
    wide = 3 * cols

    def body(ids_ref, x_ref, q_ref, kv_ref, got_ref, keep_ref, give_ref, back_ref, full_ref):
        back_ref[:, :cols] = q_ref[...]
        back_ref[:, cols:] = (kv_ref[...] + got_ref[...].astype(F32)).astype(BF)
        full_ref[...] = dot_tn(x_ref[...], back_ref[...])
        split_rows(ids_ref, full_ref, keep_ref, give_ref, kb)
        g_own = ids_ref[0]
        sums = jnp.sum(back_ref[...].astype(F32), axis=0, keepdims=True)
        pair = jnp.concatenate([sums[:, :cols], sums[:, 2 * cols :], jnp.zeros((14, cols), F32)], axis=0)
        blocks = []
        for row in range(2):
            blocks.append([])
            for g in range(GROUPS):
                blocks[-1].append([])
                for member in range(2):
                    b = row * 8 + g * 2 + member
                    part = pair[:, (b % GROUPS) * kb : (b % GROUPS + 1) * kb]
                    blocks[-1][-1].append(jnp.where(g_own == b // GROUPS, part, 0.0))
        place_small(ids_ref, blocks, keep_ref, give_ref, kb)

    shape = (2, GROUPS, kb + 16, wide)
    return call(
        body,
        "joined_grads",
        [ids, x_four, query_back, keep, got],
        [(shape, F32), (shape, BF), ((count, wide), BF)],
        scratch=[pltpu.VMEM((width, wide), F32)],
        flops=2 * count * width * wide,
    )


def finish_widen(ids, pieces, low, low_got):
    kb, cols = pieces[0].shape
    half, width = low.shape
    quarter = cols // 2
    count = quarter // half

    def body(ids_ref, *refs):
        low_ref, got_ref, out_ref, narrow_ref, all_ref = refs[4:]
        y, x = ids_ref[2], ids_ref[3]
        for k in range(4):
            row = y if k < 2 else 1 - y
            col = x if k % 2 == 0 else 1 - x
            all_ref[row * 2 + col] = refs[k][...].astype(F32)
        for part in range(2):
            for row in range(2):
                picks = []
                for c in range(count):
                    for col in range(2):
                        at = part * quarter + c * half
                        picks.append(all_ref[row * 2 + col, :, at : at + half])
                at = (part * 2 + row) * 2 * quarter
                out_ref[:, at : at + 2 * quarter] = jnp.concatenate(picks, axis=1)
        narrow_ref[pl.ds(pl.multiple_of(x * half, 16), half), :] = low_ref[...].astype(F32)
        narrow_ref[pl.ds(pl.multiple_of((1 - x) * half, 16), half), :] = got_ref[...].astype(F32)

    return call(
        body,
        "finish_widen",
        [ids] + list(pieces) + [low, low_got],
        [((kb, 8 * quarter), F32), ((2 * half, width), F32)],
        scratch=[pltpu.VMEM((4, kb, cols), F32)],
    )


def finish_joined(got, kb):
    wide = got.shape[2]
    cols = wide // 3

    def body(got_ref, out_ref, small_ref):
        for g in range(GROUPS):
            for part in range(3):
                at = (part * GROUPS + g) * cols
                out_ref[:, at : at + cols] = got_ref[g, :kb, part * cols : (part + 1) * cols].astype(F32)
        small = jnp.zeros((16, wide), F32)
        for g in range(GROUPS):
            small = small + got_ref[g, kb:, :].astype(F32)
        small_ref[...] = small

    return call(body, "finish_joined", [got], [((kb, GROUPS * wide), F32), ((16, wide), F32)])


def fast_device(
    tokens,
    segments,
    joined_weight,
    query_bias,
    value_bias,
    output_weight,
    output_bias,
    first_gain,
    first_shift,
    widen_weight,
    widen_bias,
    narrow_weight,
    narrow_bias,
    final_gain,
    final_shift,
    cotangent,
):
    at = Layout()
    n, r = at.size, at.members
    rows, width = tokens.shape[1:]
    heads = width // HEAD_DIM
    near_heads = heads // GROUPS
    cols = near_heads * HEAD_DIM
    kb = joined_weight.shape[0]
    ff_own = narrow_weight.shape[0]
    quarter = 4 * ff_own
    span = 2 * ff_own
    seg_row = segments[0]
    length = seg_row.shape[0]
    scale = 1.0 / math.sqrt(HEAD_DIM)
    inputs = tokens[0]
    columns = [[g * r + m for g in range(GROUPS)] for m in range(r)]
    ids = jnp.stack([at.group, at.member, at.seq, at.rep]).astype(jnp.int32)

    def across(value):
        return lax.all_to_all(value, "ctx", 0, 0, axis_index_groups=columns, tiled=True)

    def spread_out(value):
        far = at.swap(value, "seq")
        return (value, far, at.partner(value), at.partner(far))

    w_output = lax.all_gather(output_weight, ("seq", "ctx"), tiled=True)
    packed = pack_joined(
        ids,
        joined_weight,
        [
            query_bias,
            value_bias,
            output_bias,
            first_gain,
            first_shift,
            narrow_bias,
            final_gain,
            final_shift,
        ],
        widen_bias,
        cols,
    )
    joined_rel = [packed[0]] + [at.shift(packed[k], k) for k in range(1, GROUPS)]
    x_cut = jnp.broadcast_to(after(inputs, *joined_rel)[None], (GROUPS, rows, width))
    x_four = across(x_cut).reshape(-1, width)
    joined_got = jnp.stack(joined_rel)
    joined_parts = spread_out(joined_got)
    w_joined, vec, near, wide = assemble_joined(ids, joined_parts, kb)
    widen_near, widen_far, narrow_low = pick_widen(after(ids, packed[3]), widen_weight, narrow_weight)
    widen_got = at.swap(after(widen_far, joined_parts[1]), "seq")
    w_wide = lax.all_gather(pack_widen(ids, widen_near, widen_got, narrow_low), "ctx", tiled=True)

    queries, kv_own = split_joined(x_four, w_joined, near, scale)
    kv_other = at.partner(kv_own)
    lanes = jnp.arange(rows, dtype=jnp.int32)

    def places(member):
        return ((jnp.arange(GROUPS, dtype=jnp.int32) * r + member)[:, None] * rows + lanes).reshape(-1)

    by_member = jnp.transpose(seg_row.reshape(GROUPS, r, rows), (1, 0, 2)).reshape(r, -1)

    def documents(member):
        return lax.dynamic_index_in_dim(by_member, member, 0, keepdims=False)

    q_row = jnp.stack([places(at.member), documents(at.member)]).astype(F32)
    o_row = jnp.stack([places(1 - at.member), documents(1 - at.member)]).astype(F32)
    k_row = jnp.concatenate([q_row, o_row], axis=1)
    q_col = jnp.transpose(q_row)
    k_col = jnp.transpose(k_row)
    order_heads = at.group * near_heads + jnp.arange(near_heads, dtype=jnp.int32)
    slopes = jnp.power(2.0, -8.0 * (order_heads.astype(F32) + 1.0) / heads) * (512.0 / length)
    attended = attend(ids, slopes, queries, kv_own, kv_other, q_col, k_row)
    mixed_near, inv = attended[:2]
    mixed_send = attended[2:]
    mixed_rel = [mixed_send[0]] + [at.shift(mixed_send[k], k) for k in range(1, GROUPS)]
    first, first_low, first_unit, first_root = close_attention(
        ids, inputs, mixed_rel, w_output, vec, kb
    )
    first_rel = [first_low] + [at.plane(first_low, k) for k in (1, 2, 3)]
    own, s1, s2, s3, hidden, gate, up = widen_narrow(first_rel, w_wide, wide)
    received = [at.plane(s1, 1), at.plane(s2, 2), at.plane(s3, 3)]
    gate_factor, up_factor = gate_slopes(gate, up)
    result, final_back, narrow_back, final_sums = turn_final(own, received, first, cotangent[0], vec)

    back_rel = [narrow_back] + [at.plane(narrow_back, k) for k in (1, 2, 3)]
    own, s1, s2, s3, gate_back, up_back = widen_narrow_back(back_rel, w_wide, gate_factor, up_factor)
    received = [at.plane(s1, 1), at.plane(s2, 2), at.plane(s3, 3)]
    wide_grad, gate_sum, up_sum = wide_grads(
        first_rel, gate_back, up_back, hidden, back_rel
    )
    wide_sum = lax.psum_scatter(wide_grad, "ctx", tiled=True)
    turned = turn_first(ids, own, received, final_back, first_unit, first_root, w_output, vec, kb)
    attn_back, output_back, first_sums = turned[:3]
    back_send = turned[3:]
    back_near = [back_send[0]] + [at.shift(back_send[k], k) for k in range(1, GROUPS)]

    output_keep, output_give = output_grads(
        ids, mixed_rel, output_back, first_sums, final_sums, gate_sum, up_sum, kb
    )

    def seq_send(keep, got):
        return (keep + got.astype(F32)).astype(BF)

    output_got = at.partner(output_give)

    query_back, kv_keep, kv_give = attend_back(
        ids, slopes, queries, back_near, mixed_near, inv, kv_own, kv_other, q_row, k_col, scale
    )
    output_far = at.swap(seq_send(output_keep[1], output_got[1]), "seq")
    kv_give, output_far = lax.optimization_barrier((kv_give, output_far))
    kv_got = at.partner(kv_give)

    output_sum = (output_keep[0] + output_got[0].astype(F32) + output_far.astype(F32)).astype(BF)
    output_both = (output_sum.astype(F32) + at.swap(output_sum, "rep").astype(F32)).astype(BF)
    joined_keep, joined_give, joined_back = joined_grads(ids, x_four, query_back, kv_keep, kv_got, kb)
    joined_got = at.partner(joined_give)
    own, s1, s2, s3 = tokens_parts(ids, joined_back, w_joined)
    received = [at.shift(s1, -1), at.shift(s2, -2), at.shift(s3, -3)]
    joined_far = at.swap(seq_send(joined_keep[1], joined_got[1]), "seq")
    joined_sum = (joined_keep[0] + joined_got[0].astype(F32) + joined_far.astype(F32)).astype(BF)
    wide_sum = after(wide_sum, joined_got)
    low_sum = wide_sum[:, 2 * quarter :]
    row_own = lax.dynamic_slice_in_dim(wide_sum, at.seq * kb, kb, 0)[:, : 2 * quarter]
    row_far = lax.dynamic_slice_in_dim(wide_sum, (1 - at.seq) * kb, kb, 0)[:, : 2 * quarter]
    joined_both = (joined_sum.astype(F32) + at.swap(joined_sum, "rep").astype(F32)).astype(BF)
    widen_pieces = [row_own, at.plane(row_own, 1), at.plane(row_far, 2), at.plane(row_far, 3)]
    low_got = at.plane(low_sum, 1)
    joined_mine = after(joined_both, low_got, *widen_pieces)
    widen_total, narrow_total = finish_widen(ids, widen_pieces, low_sum, low_got)
    output_all = across(after(output_both, joined_far))
    output_total = jnp.sum(after(output_all, joined_mine).astype(F32), axis=0)
    joined_total, pair = finish_joined(across(joined_mine), kb)
    tokens_grad = after(attn_back, joined_mine) + own
    for item in received:
        tokens_grad = tokens_grad + item.astype(F32)
    last = output_total[kb:, :kb]
    return (
        result[None],
        tokens_grad[None],
        joined_total,
        pair[0, :kb],
        pair[1, :kb],
        output_total[:kb],
        last[0],
        last[1],
        last[2],
        widen_total,
        last[6:14].reshape(-1),
        narrow_total,
        last[3],
        last[4],
        last[5],
    )


def solution(mesh):
    tokens = P(("rep", "seq"), "ctx", None)
    matrix = P(("seq", "ctx"), None)
    vector = P(("seq", "ctx"))
    near = mesh.shape["ctx"] == 2 * GROUPS and mesh.shape["rep"] == 2
    return jax.shard_map(
        fast_device if near else on_device,
        mesh=mesh,
        in_specs=(
            tokens,
            P(("rep", "seq"), None),
            matrix,
            vector,
            vector,
            matrix,
            vector,
            vector,
            vector,
            matrix,
            vector,
            matrix,
            vector,
            vector,
            vector,
            tokens,
        ),
        out_specs=(
            tokens,
            tokens,
            matrix,
            vector,
            vector,
            matrix,
            vector,
            vector,
            vector,
            matrix,
            vector,
            matrix,
            vector,
            vector,
            vector,
        ),
        check_vma=False,
    )
```

```python
import math

import jax
import jax.numpy as jnp
from jax import lax
from jax.experimental import pallas as pl
from jax.experimental.pallas import tpu as pltpu
from jax.sharding import PartitionSpec as P

HEAD_DIM = 64
GROUPS = 4
FAR = 1e30
BF = jnp.bfloat16
F32 = jnp.float32


def dot_nn(left, right):
    return lax.dot_general(left, right, (((1,), (0,)), ((), ())), preferred_element_type=F32)


def dot_tn(left, right):
    return lax.dot_general(left, right, (((0,), (0,)), ((), ())), preferred_element_type=F32)


def dot_nt(left, right):
    return lax.dot_general(left, right, (((1,), (1,)), ((), ())), preferred_element_type=F32)


def head_mask(head, cols):
    lane = lax.broadcasted_iota(jnp.int32, (1, cols), 1)
    return (lane >= head * HEAD_DIM) & (lane < (head + 1) * HEAD_DIM)


def only_head(value, head):
    return jnp.where(head_mask(head, value.shape[1]), value, jnp.zeros_like(value))


def each_chunk(count, body):
    if count <= 4:
        for index in range(count):
            body(index)
    else:
        lax.fori_loop(0, count, lambda index, carry: (body(index), carry)[1], 0)


def forward_kernel(slope_ref, q_ref, kv_ref, qinfo_ref, kinfo_ref, out_ref, inv_ref, acc_ref, sum_ref, *, chunk):
    rows, cols = q_ref.shape
    heads = cols // HEAD_DIM
    count = kv_ref.shape[0] // chunk
    acc_ref[...] = jnp.zeros_like(acc_ref)
    sum_ref[...] = jnp.zeros_like(sum_ref)
    q = q_ref[...]
    qpos = qinfo_ref[:, 0:1]
    qseg = qinfo_ref[:, 1:2]
    ones = jnp.ones((8, chunk), BF)

    def step(index):
        begin = index * chunk
        here = pl.ds(begin, chunk)
        keys = kv_ref[here, :cols]
        values = kv_ref[here, cols:]
        kpos = kinfo_ref[0:1, here]
        kseg = kinfo_ref[1:2, here]
        far = jnp.where(qseg == kseg, jnp.abs(qpos - kpos), FAR)
        for head in range(heads):
            scores = dot_nt(only_head(q, head), keys) - slope_ref[head] * far
            raised = jnp.exp(scores).astype(BF)
            sum_ref[head] += dot_nt(ones, raised)
            acc_ref[head] += dot_nn(raised, values)

    each_chunk(count, step)
    total = jnp.zeros((rows, cols), F32)
    for head in range(heads):
        inv = 1.0 / sum_ref[head]
        inv_ref[head] = inv
        column = jnp.transpose(inv)[:, 0:1]
        total = total + only_head(acc_ref[head] * column, head)
    out_ref[...] = total


def attend_forward(slopes, queries, key_value, qinfo, kinfo, interpret=False):
    count, cols = queries.shape
    heads = cols // HEAD_DIM
    keys = key_value.shape[0]
    chunk = math.gcd(keys, 512)
    rows = math.gcd(count, 128)
    whole = lambda shape: pl.BlockSpec(shape, lambda i: tuple(0 for _ in shape))
    return pl.pallas_call(
        lambda *refs: forward_kernel(*refs, chunk=chunk),
        grid=(count // rows,),
        in_specs=[
            pl.BlockSpec(memory_space=pltpu.SMEM),
            pl.BlockSpec((rows, cols), lambda i: (i, 0)),
            whole((keys, 2 * cols)),
            pl.BlockSpec((rows, 2), lambda i: (i, 0)),
            whole((2, keys)),
        ],
        out_specs=[
            pl.BlockSpec((rows, cols), lambda i: (i, 0)),
            pl.BlockSpec((heads, 8, rows), lambda i: (0, 0, i)),
        ],
        out_shape=[
            jax.ShapeDtypeStruct((count, cols), F32),
            jax.ShapeDtypeStruct((heads, 8, count), F32),
        ],
        scratch_shapes=[pltpu.VMEM((heads, rows, cols), F32), pltpu.VMEM((heads, 8, rows), F32)],
        name="attend_forward",
        interpret=interpret,
    )(slopes, queries, key_value, qinfo, kinfo)


def backward_kernel(
    slope_ref, q_ref, do_ref, out_ref, inv_ref, kv_ref, qinfo_ref, kinfo_ref, dq_ref, dkv_ref, acc_ref, *, chunk
):
    rows, cols = q_ref.shape
    heads = cols // HEAD_DIM
    count = kv_ref.shape[0] // chunk
    q = q_ref[...]
    back = do_ref[...]
    product = back.astype(F32) * out_ref[...]
    qpos = qinfo_ref[0:1, :]
    qseg = qinfo_ref[1:2, :]
    acc_ref[...] = jnp.zeros_like(acc_ref)
    row_dots = []
    for head in range(heads):
        chosen = jnp.broadcast_to(head_mask(head, cols), (8, cols)).astype(F32)
        row_dots.append(
            lax.dot_general(
                chosen,
                product,
                (((1,), (1,)), ((), ())),
                precision=lax.Precision.HIGHEST,
                preferred_element_type=F32,
            )[0:1]
        )

    @pl.when(pl.program_id(0) == 0)
    def _():
        dkv_ref[...] = jnp.zeros_like(dkv_ref)

    def step(index):
        begin = index * chunk
        here = pl.ds(begin, chunk)
        keys = kv_ref[here, :cols]
        values = kv_ref[here, cols:]
        kpos = kinfo_ref[here, 0:1]
        kseg = kinfo_ref[here, 1:2]
        far = jnp.where(qseg == kseg, jnp.abs(qpos - kpos), FAR)
        key_part = jnp.zeros((chunk, cols), F32)
        value_part = jnp.zeros((chunk, cols), F32)
        for head in range(heads):
            q_head = only_head(q, head)
            back_head = only_head(back, head)
            scores = dot_nt(keys, q_head) - slope_ref[head] * far
            probs = jnp.exp(scores) * inv_ref[head, 0:1, :]
            prob_back = dot_nt(values, back_head)
            score_back = (probs * (prob_back - row_dots[head])).astype(BF)
            key_part = key_part + dot_nn(score_back, q_head)
            value_part = value_part + dot_nn(probs.astype(BF), back_head)
            acc_ref[head] += dot_tn(score_back, keys)
        dkv_ref[here, :cols] += key_part
        dkv_ref[here, cols:] += value_part

    each_chunk(count, step)
    total = jnp.zeros((rows, cols), F32)
    for head in range(heads):
        total = total + only_head(acc_ref[head], head)
    dq_ref[...] = total


def attend_backward(slopes, queries, back, mixed, inv, key_value, qinfo, kinfo, interpret=False):
    count, cols = queries.shape
    heads = cols // HEAD_DIM
    keys = key_value.shape[0]
    chunk = math.gcd(keys, 512)
    rows = math.gcd(count, 128)
    whole = lambda shape: pl.BlockSpec(shape, lambda i: tuple(0 for _ in shape))
    by_row = pl.BlockSpec((rows, cols), lambda i: (i, 0))
    return pl.pallas_call(
        lambda *refs: backward_kernel(*refs, chunk=chunk),
        grid=(count // rows,),
        in_specs=[
            pl.BlockSpec(memory_space=pltpu.SMEM),
            by_row,
            by_row,
            by_row,
            pl.BlockSpec((heads, 8, rows), lambda i: (0, 0, i)),
            whole((keys, 2 * cols)),
            pl.BlockSpec((2, rows), lambda i: (0, i)),
            whole((keys, 2)),
        ],
        out_specs=[by_row, whole((keys, 2 * cols))],
        out_shape=[
            jax.ShapeDtypeStruct((count, cols), F32),
            jax.ShapeDtypeStruct((keys, 2 * cols), F32),
        ],
        scratch_shapes=[pltpu.VMEM((heads, rows, cols), F32)],
        name="attend_backward",
        interpret=interpret,
    )(slopes, queries, back, mixed, inv, key_value, qinfo, kinfo)


def norm_stats(value):
    centre = jnp.mean(value, axis=-1, keepdims=True)
    centred = value - centre
    spread = jnp.mean(centred * centred, axis=-1, keepdims=True)
    root = lax.rsqrt(spread + 1e-06)
    return centred * root, root


def norm_back(unit, root, gain, back):
    scaled = back * gain
    return root * (
        scaled
        - jnp.mean(scaled, axis=-1, keepdims=True)
        - unit * jnp.mean(scaled * unit, axis=-1, keepdims=True)
    )


def after(value, *others):
    return lax.optimization_barrier((value,) + others)[0]


class Layout:
    def __init__(self):
        self.size = lax.axis_size("ctx")
        self.members = self.size // GROUPS
        index = lax.axis_index("ctx")
        self.group = index // self.members
        self.member = index % self.members
        self.seq = lax.axis_index("seq")
        self.rep = lax.axis_index("rep")
        self.inner = [
            [g * self.members + m for m in range(self.members)] for g in range(GROUPS)
        ]

    def shift(self, value, steps):
        n, r = self.size, self.members
        return lax.ppermute(value, "ctx", [(i, (i + steps * r) % n) for i in range(n)])

    def swap(self, value, axis):
        return lax.ppermute(value, axis, [(0, 1), (1, 0)])

    def plane(self, value, k):
        if k == 3:
            return lax.ppermute(value, ("rep", "seq"), [(i, 3 - i) for i in range(4)])
        return self.swap(value, "rep" if k == 1 else "seq")

    def gather(self, value):
        return [value] + [self.shift(value, k) for k in range(1, GROUPS)]

    def scatter_sum(self, parts):
        total = parts[0]
        for k in range(1, GROUPS):
            total = total + self.shift(parts[k].astype(BF), -k).astype(F32)
        return total

    def exchange(self, pieces):
        own = lax.dynamic_index_in_dim(pieces, self.group, 0, keepdims=False)
        out = [own]
        for k in range(1, GROUPS):
            target = (self.group + k) % GROUPS
            out.append(
                self.shift(lax.dynamic_index_in_dim(pieces, target, 0, keepdims=False), k)
            )
        return out

    def ordered(self, relative):
        line = [relative[0], relative[3], relative[2], relative[1]]
        twice = jnp.stack(line + line[:3])
        return lax.dynamic_slice_in_dim(twice, (GROUPS - self.group) % GROUPS, GROUPS, 0)

    def both_seq(self, value):
        other = self.swap(value, "seq")
        first = self.seq == 0
        return jnp.stack([jnp.where(first, value, other), jnp.where(first, other, value)])

    def partner(self, value):
        return lax.ppermute(
            value, "ctx", [(i, i ^ 1) for i in range(self.size)]
        )

    def all_members(self, value, axis):
        if self.members == 2:
            other = self.partner(value)
            first = self.member == 0
            return jnp.stack(
                [jnp.where(first, value, other), jnp.where(first, other, value)], axis
            )
        out = lax.all_gather(value, "ctx", axis_index_groups=self.inner)
        return jnp.moveaxis(out, 0, axis)

    def member_sum(self, pieces):
        if self.members == 2:
            keep = lax.dynamic_index_in_dim(pieces, self.member, 0, keepdims=False)
            give = lax.dynamic_index_in_dim(pieces, 1 - self.member, 0, keepdims=False)
            return keep + self.partner(give.astype(BF)).astype(F32)
        got = lax.all_to_all(
            pieces.astype(BF), "ctx", 0, 0, axis_index_groups=self.inner, tiled=True
        )
        return jnp.sum(got.astype(F32), axis=0)

    def seq_sum(self, pieces):
        keep = lax.dynamic_index_in_dim(pieces, self.seq, 0, keepdims=False)
        give = lax.dynamic_index_in_dim(pieces, 1 - self.seq, 0, keepdims=False)
        return keep + self.swap(give.astype(BF), "seq").astype(F32)

    def rep_sum(self, value):
        low = value.astype(BF)
        return low.astype(F32) + self.swap(low, "rep").astype(F32)


def on_device(
    tokens,
    segments,
    joined_weight,
    query_bias,
    value_bias,
    output_weight,
    output_bias,
    first_gain,
    first_shift,
    widen_weight,
    widen_bias,
    narrow_weight,
    narrow_bias,
    final_gain,
    final_shift,
    cotangent,
):
    at = Layout()
    n, r = at.size, at.members
    rows, width = tokens.shape[1:]
    heads = width // HEAD_DIM
    near_heads = heads // GROUPS
    cols = near_heads * HEAD_DIM
    kb = joined_weight.shape[0]
    ff_own = narrow_weight.shape[0]
    ff = ff_own * 2 * n
    quarter = ff // GROUPS
    span = r * ff_own
    seg_row = segments[0]
    length = seg_row.shape[0]
    scale = 1.0 / math.sqrt(HEAD_DIM)
    inputs = tokens[0]

    x_rel = at.gather(inputs)
    x_four = jnp.concatenate(x_rel, axis=0)

    small = jnp.concatenate(
        [
            query_bias,
            value_bias,
            output_bias,
            first_gain,
            first_shift,
            narrow_bias,
            final_gain,
            final_shift,
            widen_bias,
        ]
    )[None]
    small_all = at.all_members(at.both_seq(at.ordered(at.gather(small))), 2)
    small_all = small_all.reshape(2 * n, -1).astype(F32)

    def vector(place):
        return small_all[:, place * kb : (place + 1) * kb].reshape(width)

    b_query, b_value, b_output, g_first, s_first, b_narrow, g_final, s_final = (
        vector(place) for place in range(8)
    )
    b_widen = lax.dynamic_index_in_dim(
        small_all[:, 8 * kb :].reshape(2, 2, GROUPS, span), at.group, 2, keepdims=False
    ).reshape(2 * quarter)
    b_query = lax.dynamic_index_in_dim(b_query.reshape(GROUPS, cols), at.group, 0, keepdims=False)
    b_value = lax.dynamic_index_in_dim(b_value.reshape(GROUPS, cols), at.group, 0, keepdims=False)

    joined_cut = jnp.transpose(joined_weight.reshape(kb, 3, GROUPS, cols), (2, 0, 1, 3)).reshape(
        GROUPS, kb, 3 * cols
    )
    w_joined = at.all_members(at.both_seq(at.ordered(at.exchange(joined_cut))), 2).reshape(
        width, 3 * cols
    )

    output_low = after(output_weight, x_four)
    out_rel = at.ordered(at.gather(output_low)).reshape(GROUPS * kb, width)
    both = at.both_seq(jnp.concatenate([out_rel, narrow_weight], axis=0))
    both = at.all_members(both, 1)
    w_output = jnp.transpose(
        both[:, :, : GROUPS * kb].reshape(2, r, GROUPS, kb, width), (0, 2, 1, 3, 4)
    ).reshape(width, width)
    w_narrow = both[:, :, GROUPS * kb :].reshape(quarter, width)

    widen_cut = jnp.transpose(
        after(widen_weight, x_four).reshape(kb, 4, GROUPS, span), (2, 0, 1, 3)
    ).reshape(GROUPS, kb, 2 * quarter)
    w_widen = at.all_members(at.both_seq(at.ordered(at.exchange(widen_cut))), 2).reshape(
        width, 2 * quarter
    )

    lanes = jnp.arange(rows, dtype=jnp.int32)
    near = (at.group - jnp.arange(GROUPS, dtype=jnp.int32)) % GROUPS

    def places(member):
        return ((near * r + member)[:, None] * rows + lanes[None]).reshape(-1)

    if r == 2:
        key_members = jnp.stack([at.member, 1 - at.member])
    else:
        key_members = jnp.arange(r, dtype=jnp.int32)
    query_pos = places(at.member)
    key_pos = jnp.concatenate([places(key_members[i]) for i in range(r)])
    query_seg = jnp.take(seg_row, query_pos)
    key_seg = jnp.take(seg_row, key_pos)
    q_info = jnp.stack([query_pos, query_seg]).astype(F32)
    k_info = jnp.stack([key_pos, key_seg]).astype(F32)
    order_heads = at.group * near_heads + jnp.arange(near_heads, dtype=jnp.int32)
    slopes = jnp.power(2.0, -8.0 * (order_heads.astype(F32) + 1.0) / heads) * (512.0 / length)

    joined = dot_nn(x_four, w_joined)
    queries = ((joined[:, :cols] + b_query) * scale).astype(BF)
    kv_own = jnp.concatenate(
        [joined[:, cols : 2 * cols], joined[:, 2 * cols :] + b_value], axis=1
    ).astype(BF)
    if r == 2:
        key_value = jnp.concatenate([kv_own, at.partner(kv_own)], axis=0)
    else:
        key_value = at.all_members(kv_own, 0).reshape(-1, 2 * cols)
    mixed_near, inv = attend_forward(slopes, queries, key_value, jnp.transpose(q_info), k_info)
    mixed_low = mixed_near.astype(BF).reshape(GROUPS, rows, cols)
    mixed_rel = [mixed_low[0]] + [at.shift(mixed_low[k], -k) for k in range(1, GROUPS)]
    mixed_rel = [mixed_rel[0], mixed_rel[3], mixed_rel[2], mixed_rel[1]]
    mixed = jnp.transpose(at.ordered(mixed_rel), (1, 0, 2)).reshape(rows, width)

    first_in = inputs.astype(F32) + dot_nn(mixed, w_output) + b_output
    first_unit, first_root = norm_stats(first_in)
    first = first_unit * g_first + s_first
    first_low = first.astype(BF)

    first_four = jnp.concatenate(at.gather(first_low), axis=0)
    gate_up = dot_nn(first_four, w_widen) + b_widen
    gate, up = gate_up[:, :quarter], gate_up[:, quarter:]
    phi_big = 0.5 * (1.0 + lax.erf(gate * math.sqrt(0.5)))
    gelu = gate * phi_big
    slope_gate = phi_big + gate * jnp.exp(-0.5 * gate * gate) * (1.0 / math.sqrt(2.0 * math.pi))
    hidden = (gelu * up).astype(BF)
    final_part = dot_nn(hidden, w_narrow).reshape(GROUPS, rows, width)
    final_in = first + at.scatter_sum([final_part[k] for k in range(GROUPS)]) + b_narrow
    final_unit, final_root = norm_stats(final_in)
    result = final_unit * g_final + s_final

    upstream = cotangent[0].astype(F32)
    final_back = norm_back(final_unit, final_root, g_final, upstream)
    final_gain_grad = jnp.sum(upstream * final_unit, axis=0)
    final_shift_grad = jnp.sum(upstream, axis=0)
    narrow_back = final_back.astype(BF)
    narrow_bias_grad = jnp.sum(narrow_back.astype(F32), axis=0)
    back_four = jnp.concatenate(at.gather(narrow_back), axis=0)
    hidden_back = dot_nt(back_four, w_narrow)
    widen_back = jnp.concatenate(
        [hidden_back * up * slope_gate, hidden_back * gelu], axis=1
    ).astype(BF)
    first_part = dot_nt(widen_back, w_widen).reshape(GROUPS, rows, width)
    first_back = final_back + at.scatter_sum([first_part[k] for k in range(GROUPS)])
    narrow_grad = dot_tn(hidden, back_four)
    widen_grad = dot_tn(first_four, widen_back)
    widen_bias_grad = jnp.sum(widen_back.astype(F32), axis=0)

    attn_back = norm_back(first_unit, first_root, g_first, first_back)
    first_gain_grad = jnp.sum(first_back * first_unit, axis=0)
    first_shift_grad = jnp.sum(first_back, axis=0)
    output_back = attn_back.astype(BF)
    output_bias_grad = jnp.sum(output_back.astype(F32), axis=0)
    output_grad = dot_tn(mixed, output_back)
    mixed_back = dot_nt(output_back, w_output).astype(BF)
    mixed_back = jnp.transpose(mixed_back.reshape(rows, GROUPS, cols), (1, 0, 2))
    back_near = jnp.concatenate(at.exchange(mixed_back), axis=0)

    query_sum, kv_sum = attend_backward(
        slopes, queries, back_near, mixed_near, inv, key_value, q_info, jnp.transpose(k_info)
    )
    if r == 2:
        half = kv_sum.shape[0] // 2
        kv_back = kv_sum[:half] + at.partner(kv_sum[half:].astype(BF)).astype(F32)
    else:
        kv_back = at.member_sum(kv_sum.reshape(r, -1, 2 * cols))
    query_low = query_sum.astype(BF)
    query_scaled = (query_low.astype(F32) * scale).astype(BF)
    joined_back = jnp.concatenate([query_scaled, kv_back.astype(BF)], axis=1)
    tokens_part = dot_nt(joined_back, w_joined).reshape(GROUPS, rows, width)
    tokens_grad = attn_back + at.scatter_sum([tokens_part[k] for k in range(GROUPS)])
    joined_grad = dot_tn(x_four, joined_back)
    near_bias = jnp.sum(joined_back.astype(F32), axis=0)
    query_bias_grad = near_bias[:cols]
    value_bias_grad = near_bias[2 * cols :]

    narrow_sum = at.member_sum(jnp.transpose(narrow_grad.reshape(2, r, ff_own, width), (1, 0, 2, 3)))
    narrow_total = at.rep_sum(at.seq_sum(narrow_sum))

    def to_rows(grad):
        pieces = jnp.transpose(grad.reshape(2, GROUPS, r, kb, -1), (2, 0, 1, 3, 4))
        mine = at.rep_sum(at.seq_sum(at.member_sum(pieces))).astype(BF)
        return at.ordered(at.exchange(mine))

    widen_total = jnp.transpose(
        to_rows(widen_grad).reshape(GROUPS, kb, 4, span), (1, 2, 0, 3)
    ).reshape(kb, 2 * ff)
    joined_total = jnp.transpose(
        to_rows(joined_grad).reshape(GROUPS, kb, 3, cols), (1, 2, 0, 3)
    ).reshape(kb, 3 * width)

    def spread(vector, parts):
        wide = jnp.zeros((parts, GROUPS, vector.shape[0] // parts), F32)
        return lax.dynamic_update_slice_in_dim(
            wide, vector.reshape(parts, 1, -1), at.group, 1
        ).reshape(-1)

    vectors = [
        spread(query_bias_grad, 1),
        spread(value_bias_grad, 1),
        output_bias_grad,
        first_gain_grad,
        first_shift_grad,
        narrow_bias_grad,
        final_gain_grad,
        final_shift_grad,
    ]
    row = jnp.concatenate(
        [item.reshape(2 * n, kb) for item in vectors]
        + [spread(widen_bias_grad, 4).reshape(2 * n, 8 * kb)],
        axis=1,
    )
    row = jnp.pad(row[:, None, :], ((0, 0), (0, 15), (0, width - 16 * kb)))
    packed = jnp.concatenate([output_grad.reshape(2 * n, kb, width), row], axis=1)
    packed = jnp.transpose(packed.reshape(2, GROUPS, r, kb + 16, width), (2, 0, 1, 3, 4))
    packed = at.seq_sum(at.member_sum(packed)).astype(BF)
    packed = at.exchange(packed)
    packed = sum(item.astype(F32) for item in packed[1:]) + packed[0].astype(F32)
    packed = at.rep_sum(packed)
    output_total = packed[:kb]
    last = packed[kb]

    def owned(place):
        return last[place * kb : (place + 1) * kb]

    return (
        result.astype(BF)[None],
        tokens_grad[None],
        joined_total.astype(F32),
        owned(0),
        owned(1),
        output_total,
        owned(2),
        owned(3),
        owned(4),
        widen_total.astype(F32),
        last[8 * kb : 16 * kb],
        narrow_total,
        owned(5),
        owned(6),
        owned(7),
    )


def vmem(shape):
    return pl.BlockSpec(shape, lambda *_: tuple(0 for _ in shape))


COSTS = {
    "pack_joined": 0,
    "assemble_joined": 0,
    "pick_widen": 0,
    "pack_widen": 0,
    "cut_joined": 0,
    "cut_wide": 0,
    "assemble_output": 0,
    "finish_tokens": 0,
    "split_joined": 3,
    "attend": 5,
    "attend_back": 8,
    "close_attention": 3,
    "widen_narrow": 6,
    "widen_narrow_back": 7,
    "turn_final": 3,
    "turn_first": 3,
    "wide_grads": 6,
    "output_grads": 3,
    "tokens_parts": 0,
    "joined_grads": 4,
    "finish_widen": 0,
    "finish_joined": 0,
}

SMEM = pl.BlockSpec(memory_space=pltpu.SMEM)


def call(body, name, inputs, outputs, scratch=(), grid=(1,), in_specs=None, out_specs=None, flops=0):
    shapes = [jax.ShapeDtypeStruct(shape, kind) for shape, kind in outputs]
    if in_specs is None:
        in_specs = [SMEM if item.ndim == 1 else vmem(item.shape) for item in inputs]
    if out_specs is None:
        out_specs = [vmem(shape) for shape, kind in outputs]
    moved = sum(item.size * item.dtype.itemsize for item in list(inputs) + shapes)
    return pl.pallas_call(
        body,
        grid=grid,
        in_specs=in_specs,
        out_specs=out_specs,
        out_shape=shapes,
        scratch_shapes=list(scratch),
        name=name,
        cost_estimate=pl.CostEstimate(flops=int(COSTS[name] * 5 * 1e9), transcendentals=0, bytes_accessed=0),
    )(*inputs)


def pack_joined(ids, weight, vectors, widen_bias, cols):
    kb = weight.shape[0]
    vectors = [item[None] for item in vectors]
    shape = (kb + 16, 3 * cols)

    def body(*refs):
        ids_ref, w_ref, wide_ref = refs[0], refs[1], refs[10]
        all_ref = refs[15]
        rows = [ref[...].astype(F32) for ref in refs[2:10]]
        wide = wide_ref[...].astype(F32)
        rows += [wide[:, k * kb : (k + 1) * kb] for k in range(8)]
        small = jnp.concatenate(rows, axis=0).astype(BF)
        for g in range(GROUPS):
            for part in range(3):
                at = (part * GROUPS + g) * cols
                all_ref[g, :kb, part * cols : (part + 1) * cols] = w_ref[:, at : at + cols]
            all_ref[g, kb:, :] = jnp.zeros((16, 3 * cols), BF)
            all_ref[g, kb:, :kb] = small
        for k in range(GROUPS):
            refs[11 + k][...] = all_ref[(ids_ref[0] + k) % GROUPS]

    inputs = [ids, weight] + vectors + [widen_bias[None]]
    return call(
        body,
        "pack_joined",
        inputs,
        [(shape, BF)] * GROUPS,
        scratch=[pltpu.VMEM((GROUPS,) + shape, BF)],
    )


def place_rows(ids_ref, pieces, out_ref, kb, relative=False):
    group, m, y = ids_ref[0], ids_ref[1], ids_ref[2]
    for index, piece in enumerate(pieces):
        row = y if index % 2 == 0 else 1 - y
        member = m if index < 2 else 1 - m
        for g in range(GROUPS):
            source = (group + GROUPS - g) % GROUPS if relative else g
            start = pl.multiple_of((row * GROUPS * 2 + source * 2 + member) * kb, 16)
            out_ref[pl.ds(start, kb), :] = piece[g, :kb, :]


def assemble_joined(ids, pieces, kb):
    cols = pieces[0].shape[2]
    near = cols // 3
    width = 4 * GROUPS * kb
    span = 8 * kb

    def body(ids_ref, a_ref, b_ref, c_ref, d_ref, w_ref, vec_ref, near_ref, wide_ref):
        place_rows(ids_ref, (a_ref, b_ref, c_ref, d_ref), w_ref, kb, True)
        g, m, y, x = ids_ref[0], ids_ref[1], ids_ref[2], ids_ref[3]
        blocks = []
        for row in range(2):
            for k in range(GROUPS):
                for member in range(2):
                    turn = (g + GROUPS - k) % GROUPS
                    picks = [ref[turn, kb:, :kb].astype(F32) for ref in (a_ref, b_ref, c_ref, d_ref)]
                    mine = jnp.where(row == y, picks[0], picks[1])
                    theirs = jnp.where(row == y, picks[2], picks[3])
                    blocks.append(jnp.where(member == m, mine, theirs))
        vec = jnp.concatenate(blocks, axis=1)
        vec_ref[...] = vec
        total = jnp.zeros((16, near), F32)
        for k in range(GROUPS):
            total = jnp.where(g == k, vec[:, k * near : (k + 1) * near], total)
        near_ref[...] = total
        lines = []
        for part in range(2):
            for c in range(8):
                low = 8 + (c % 2) * 4
                picks = []
                for row in range(2):
                    at = (part * 8 + row * 4 + c // 2) * kb
                    picks.append(vec[low : low + 4, at : at + kb])
                both = jnp.where(y == 0, picks[0], picks[1])
                pair = jnp.where(x == 0, both[0:2], both[2:4])
                lines += [pair[0:1], pair[1:2]]
        wide_ref[...] = jnp.concatenate(lines, axis=1)

    return call(
        body,
        "assemble_joined",
        [ids] + list(pieces),
        [((width, cols), BF), ((16, width), F32), ((16, near), F32), ((1, 4 * span), F32)],
    )


def pick_widen(ids, weight, narrow):
    kb, total = weight.shape
    own, width = narrow.shape
    half = own // 2
    side = total // 4
    count = side // own
    quarter = count * half

    wide = 2 * quarter

    def body(ids_ref, w_ref, n_ref, near_ref, far_ref, low_ref, all_ref):
        y, x = ids_ref[2], ids_ref[3]
        for row in range(2):
            for col in range(2):
                pieces = []
                for part in range(2):
                    for c in range(count):
                        at = part * 2 * side + row * side + c * own + col * half
                        pieces.append(w_ref[:, at : at + half])
                all_ref[row * 2 + col] = jnp.concatenate(pieces, axis=1)
        near_ref[...] = all_ref[y * 2 + x]
        far_ref[...] = all_ref[(1 - y) * 2 + x]
        low_ref[...] = n_ref[pl.ds(pl.multiple_of(x * half, 16), half), :]

    return call(
        body,
        "pick_widen",
        [ids, weight, narrow],
        [((kb, wide), BF), ((kb, wide), BF), ((half, width), BF)],
        scratch=[pltpu.VMEM((4, kb, wide), BF)],
    )


def pack_widen(ids, near, got, low):
    kb, cols = near.shape
    width = low.shape[1]

    def body(ids_ref, near_ref, got_ref, low_ref, out_ref):
        y = ids_ref[2]
        out_ref[pl.ds(pl.multiple_of(y * kb, 16), kb), :cols] = near_ref[...]
        out_ref[pl.ds(pl.multiple_of((1 - y) * kb, 16), kb), :cols] = got_ref[...]
        out_ref[:, cols:] = low_ref[...]

    return call(body, "pack_widen", [ids, near, got, low], [((2 * kb, cols + width), BF)])[0]


def assemble_output(weights, kb):
    width, cols = weights.shape
    half = width // (2 * kb)

    def body(all_ref, w_ref):
        for y in range(2):
            for c in range(half):
                rows = slice((c * 2 + y) * kb, (c * 2 + y + 1) * kb)
                w_ref[(y * half + c) * kb : (y * half + c + 1) * kb, :] = all_ref[rows, :]

    return call(body, "assemble_output", [weights], [((width, cols), BF)])[0]


def owner_order(value, kb):
    half = value.shape[1] // (2 * kb)
    blocks = [y * half + c for c in range(half) for y in range(2)]
    return jnp.concatenate([value[:, b * kb : (b + 1) * kb] for b in blocks], axis=1)


def column_order(value, kb):
    half = value.shape[1] // (2 * kb)
    blocks = [c * 2 + y for y in range(2) for c in range(half)]
    return jnp.concatenate([value[:, b * kb : (b + 1) * kb] for b in blocks], axis=1)


def split_joined(x_four, weight, near, scale):
    count, width = x_four.shape
    cols = weight.shape[1] // 3

    def body(x_ref, w_ref, near_ref, q_ref, kv_ref):
        joined = dot_nn(x_ref[...], w_ref[...])
        q_ref[...] = ((joined[:, :cols] + near_ref[0:1, :]) * scale).astype(BF)
        kv_ref[:, :cols] = joined[:, cols : 2 * cols].astype(BF)
        kv_ref[:, cols:] = (joined[:, 2 * cols :] + near_ref[1:2, :]).astype(BF)

    return call(
        body,
        "split_joined",
        [x_four, weight, near],
        [((count, cols), BF), ((count, 2 * cols), BF)],
        flops=2 * count * width * 3 * cols,
    )


def piece_rows(ids_ref, k, rows, sign=1):
    turn = (ids_ref[0] + (k if sign > 0 else GROUPS - k)) % GROUPS
    return pl.ds(pl.multiple_of(turn * rows, 16), rows)


def attend(ids, slopes, queries, kv_own, kv_other, q_col, k_row):
    count, cols = queries.shape
    heads = cols // HEAD_DIM
    rows = count // GROUPS
    chunk = kv_own.shape[0]

    def body(ids_ref, slope_ref, q_ref, own_ref, other_ref, qi_ref, ki_ref, out_ref, inv_ref, *sends):
        q = q_ref[...]
        qpos = qi_ref[:, 0:1]
        qseg = qi_ref[:, 1:2]
        ones = jnp.ones((chunk, 64), BF)
        q_heads = [only_head(q, head) for head in range(heads)]
        accs = [None] * heads
        for side, kv_ref in enumerate((own_ref, other_ref)):
            here = slice(side * chunk, (side + 1) * chunk)
            keys = kv_ref[:, :cols]
            values = jnp.concatenate([kv_ref[:, cols:], ones], axis=1)
            far = jnp.where(qseg == ki_ref[1:2, here], jnp.abs(qpos - ki_ref[0:1, here]), FAR)
            for head in range(heads):
                scores = dot_nt(q_heads[head], keys) - slope_ref[head] * far
                part = dot_nn(jnp.exp(scores).astype(BF), values)
                accs[head] = part if side == 0 else accs[head] + part
        total = jnp.zeros((count, cols), F32)
        for head in range(heads):
            inv = 1.0 / accs[head][:, cols : cols + 1]
            inv_ref[head] = jnp.transpose(jnp.broadcast_to(inv, (count, 128)))[:8]
            total = total + only_head(accs[head][:, :cols] * inv, head)
        out_ref[...] = total
        for k, ref in enumerate(sends):
            ref[...] = out_ref[piece_rows(ids_ref, k, rows), :].astype(BF)

    return call(
        body,
        "attend",
        [ids, slopes, queries, kv_own, kv_other, q_col, k_row],
        [((count, cols), F32), ((heads, 8, count), F32)] + [((rows, cols), BF)] * GROUPS,
        flops=4 * count * 2 * chunk * cols,
    )


def attend_back(ids, slopes, queries, back_rel, mixed, inv, kv_own, kv_other, q_row, k_col, scale):
    count, cols = queries.shape
    heads = cols // HEAD_DIM
    rows = count // GROUPS
    chunk = kv_own.shape[0]

    def body(ids_ref, slope_ref, q_ref, *refs):
        pieces = refs[:GROUPS]
        out_ref, inv_ref, own_ref, other_ref, qi_ref, ki_ref, dq_ref, keep_ref, give_ref, do_ref = refs[GROUPS:]
        for k, ref in enumerate(pieces):
            do_ref[piece_rows(ids_ref, k, rows, -1), :] = ref[...]
        q = q_ref[...]
        back = do_ref[...]
        product = back.astype(F32) * out_ref[...]
        qpos = qi_ref[0:1, :]
        qseg = qi_ref[1:2, :]
        q_heads = [only_head(q, head) for head in range(heads)]
        b_heads = [only_head(back, head) for head in range(heads)]
        place = lax.broadcasted_iota(jnp.int32, (8, cols), 0)
        lane = lax.broadcasted_iota(jnp.int32, (8, cols), 1)
        row_dots = lax.dot_general(
            (lane // HEAD_DIM == place).astype(F32),
            product,
            (((1,), (1,)), ((), ())),
            precision=lax.Precision.HIGHEST,
            preferred_element_type=F32,
        )
        query_parts = [None] * heads
        for side, kv_ref in enumerate((own_ref, other_ref)):
            here = slice(side * chunk, (side + 1) * chunk)
            keys = kv_ref[:, :cols]
            values = kv_ref[:, cols:]
            far = jnp.where(qseg == ki_ref[here, 1:2], jnp.abs(qpos - ki_ref[here, 0:1]), FAR)
            key_part = None
            value_part = None
            for head in range(heads):
                scores = dot_nt(keys, q_heads[head]) - slope_ref[head] * far
                probs = jnp.exp(scores) * inv_ref[head, 0:1, :]
                prob_back = dot_nt(values, b_heads[head])
                score_back = (probs * (prob_back - row_dots[head : head + 1])).astype(BF)
                k_part = dot_nn(score_back, q_heads[head])
                v_part = dot_nn(probs.astype(BF), b_heads[head])
                q_part = dot_tn(score_back, keys)
                key_part = k_part if head == 0 else key_part + k_part
                value_part = v_part if head == 0 else value_part + v_part
                query_parts[head] = q_part if side == 0 else query_parts[head] + q_part
            target = keep_ref if side == 0 else give_ref
            target[:, :cols] = key_part.astype(target.dtype)
            target[:, cols:] = value_part.astype(target.dtype)
        total = jnp.zeros((count, cols), F32)
        for head in range(heads):
            total = total + only_head(query_parts[head], head)
        dq_ref[...] = (total.astype(BF).astype(F32) * scale).astype(BF)

    return call(
        body,
        "attend_back",
        [ids, slopes, queries] + list(back_rel) + [mixed, inv, kv_own, kv_other, q_row, k_col],
        [((count, cols), BF), ((chunk, 2 * cols), F32), ((chunk, 2 * cols), BF)],
        scratch=[pltpu.VMEM((count, cols), BF)],
        flops=10 * count * 2 * chunk * cols,
    )


def close_attention(ids, inputs, mixed_rel, weight, vec, kb):
    rows, width = inputs.shape
    cols = mixed_rel[0].shape[1]

    def body(ids_ref, x_ref, a_ref, b_ref, c_ref, d_ref, w_ref, vec_ref, first_ref, low_ref, unit_ref, root_ref):
        total = x_ref[...].astype(F32) + vec_ref[2:3, :]
        for k, ref in enumerate((a_ref, b_ref, c_ref, d_ref)):
            total = total + dot_nn(ref[...], w_ref[piece_rows(ids_ref, k, cols, -1), :])
        unit, root = norm_stats(total)
        first = unit * vec_ref[3:4, :] + vec_ref[4:5, :]
        first_ref[...] = first
        low_ref[...] = owner_order(first, kb).astype(BF)
        unit_ref[...] = unit
        root_ref[...] = root

    return call(
        body,
        "close_attention",
        [ids, inputs] + list(mixed_rel) + [weight, vec],
        [((rows, width), F32), ((rows, width), BF), ((rows, width), F32), ((rows, 1), F32)],
        flops=2 * rows * width * width,
    )


def block_of(quarter):
    return math.gcd(quarter, 256)


def join_pieces(refs):
    return jnp.concatenate([ref[...] for ref in refs], axis=0)


def send_pieces(total, refs, rows):
    for k, ref in enumerate(refs):
        ref[...] = total[k * rows : (k + 1) * rows, :].astype(ref.dtype)


def widen_narrow(rel, weights, wide):
    rows, width = rel[0].shape
    quarter = wide.shape[1] // 2
    count = GROUPS * rows

    def body(*refs):
        w_ref, wide_ref = refs[4:6]
        hid_ref, gate_ref, up_ref = refs[10:13]
        value = join_pieces(refs[:4])
        gate = dot_nn(value, w_ref[:, :quarter]) + wide_ref[:, :quarter]
        up = dot_nn(value, w_ref[:, quarter : 2 * quarter]) + wide_ref[:, quarter:]
        gate_ref[...] = gate
        up_ref[...] = up
        hidden = (gate * (0.5 + 0.5 * lax.erf(gate * math.sqrt(0.5))) * up).astype(BF)
        hid_ref[...] = hidden
        send_pieces(dot_nn(hidden, w_ref[:, 2 * quarter :]), refs[6:10], rows)

    return call(
        body,
        "widen_narrow",
        list(rel) + [weights, wide],
        [((rows, width), F32)]
        + [((rows, width), BF)] * 3
        + [((count, quarter), BF), ((count, quarter), F32), ((count, quarter), F32)],
        flops=6 * count * width * quarter,
    )


def gate_slopes(gate, up):
    phi_big = 0.5 + 0.5 * lax.erf(gate * math.sqrt(0.5))
    slope = phi_big + gate * jnp.exp(-0.5 * gate * gate) * (1.0 / math.sqrt(2.0 * math.pi))
    return up * slope, gate * phi_big


def widen_narrow_back(rel, weights, gate_factor, up_factor):
    rows, width = rel[0].shape
    count, quarter = gate_factor.shape

    def body(*refs):
        w_ref, gf_ref, uf_ref = refs[4:7]
        bg_ref, bu_ref = refs[11:13]
        hidden_back = dot_nt(join_pieces(refs[:4]), w_ref[:, 2 * quarter :])
        gate_back = (hidden_back * gf_ref[...]).astype(BF)
        up_back = (hidden_back * uf_ref[...]).astype(BF)
        bg_ref[...] = gate_back
        bu_ref[...] = up_back
        total = dot_nt(gate_back, w_ref[:, :quarter]) + dot_nt(up_back, w_ref[:, quarter : 2 * quarter])
        send_pieces(total, refs[7:11], rows)

    return call(
        body,
        "widen_narrow_back",
        list(rel) + [weights, gate_factor, up_factor],
        [((rows, width), F32)] + [((rows, width), BF)] * 3 + [((count, quarter), BF)] * 2,
        flops=6 * count * width * quarter,
    )


def turn_final(own, received, first, upstream, vec):
    rows, width = own.shape

    def body(own_ref, a_ref, b_ref, c_ref, first_ref, up_ref, vec_ref, res_ref, back_ref, low_ref, sum_ref):
        total = first_ref[...] + vec_ref[5:6, :] + own_ref[...]
        for ref in (a_ref, b_ref, c_ref):
            total = total + ref[...].astype(F32)
        unit, root = norm_stats(total)
        gain = vec_ref[6:7, :]
        res_ref[...] = (unit * gain + vec_ref[7:8, :]).astype(BF)
        upstream = up_ref[...].astype(F32)
        back = norm_back(unit, root, gain, upstream)
        low = back.astype(BF)
        back_ref[...] = back
        low_ref[...] = low
        sum_ref[...] = jnp.zeros_like(sum_ref)
        sum_ref[0:1, :] = jnp.sum(low.astype(F32), axis=0, keepdims=True)
        sum_ref[1:2, :] = jnp.sum(upstream * unit, axis=0, keepdims=True)
        sum_ref[2:3, :] = jnp.sum(upstream, axis=0, keepdims=True)

    return call(
        body,
        "turn_final",
        [own] + list(received) + [first, upstream, vec],
        [((rows, width), BF), ((rows, width), F32), ((rows, width), BF), ((8, width), F32)],
    )


def turn_first(ids, own, received, final_back, unit, root, weight, vec, kb):
    rows, width = own.shape
    cols = width // GROUPS

    def body(ids_ref, own_ref, a_ref, b_ref, c_ref, fb_ref, unit_ref, root_ref, w_ref, vec_ref, *outs):
        attn_ref, low_ref, sum_ref = outs[:3]
        total = own_ref[...]
        for ref in (a_ref, b_ref, c_ref):
            total = total + ref[...].astype(F32)
        total = fb_ref[...] + column_order(total, kb)
        unit = unit_ref[...]
        back = norm_back(unit, root_ref[...], vec_ref[3:4, :], total)
        low = back.astype(BF)
        attn_ref[...] = back
        low_ref[...] = low
        for k, ref in enumerate(outs[3:]):
            ref[...] = dot_nt(low, w_ref[piece_rows(ids_ref, k, cols), :]).astype(BF)
        sum_ref[...] = jnp.zeros_like(sum_ref)
        sum_ref[0:1, :] = jnp.sum(low.astype(F32), axis=0, keepdims=True)
        sum_ref[1:2, :] = jnp.sum(total * unit, axis=0, keepdims=True)
        sum_ref[2:3, :] = jnp.sum(total, axis=0, keepdims=True)

    return call(
        body,
        "turn_first",
        [ids, own] + list(received) + [final_back, unit, root, weight, vec],
        [((rows, width), F32), ((rows, width), BF), ((8, width), F32)] + [((rows, cols), BF)] * GROUPS,
        flops=2 * rows * width * width,
    )


def split_rows(ids_ref, full_ref, keep_ref, give_ref, kb, lead=()):
    m, y = ids_ref[1], ids_ref[2]
    for turn in range(2):
        row = y if turn == 0 else 1 - y
        for g in range(GROUPS):
            base = (row * GROUPS + g) * 2
            mine = pl.ds(pl.multiple_of((base + m) * kb, 16), kb)
            other = pl.ds(pl.multiple_of((base + 1 - m) * kb, 16), kb)
            keep_ref[lead + (turn, g, slice(0, kb), slice(None))] = full_ref[mine, :]
            give_ref[lead + (turn, g, slice(0, kb), slice(None))] = full_ref[other, :].astype(BF)


def wide_grads(first_rel, gate_back, up_back, hidden, back_rel):
    rows, width = first_rel[0].shape
    count, quarter = gate_back.shape

    def body(*refs):
        gate_ref, up_ref, hid_ref = refs[8:11]
        out_ref, gs_ref, us_ref = refs[11:14]
        value = join_pieces(refs[:4])
        for turn, (ref, sum_ref) in enumerate(((gate_ref, gs_ref), (up_ref, us_ref))):
            back = ref[...]
            out_ref[:, turn * quarter : (turn + 1) * quarter] = dot_tn(value, back).astype(BF)
            sum_ref[...] = jnp.sum(back.astype(F32), axis=0, keepdims=True)
        out_ref[:, 2 * quarter :] = dot_tn(hid_ref[...], join_pieces(refs[4:8])).astype(BF)

    return call(
        body,
        "wide_grads",
        list(first_rel) + list(back_rel) + [gate_back, up_back, hidden],
        [((width, 2 * quarter + width), BF), ((1, quarter), F32), ((1, quarter), F32)],
        flops=6 * count * width * quarter,
    )


def place_small(ids_ref, blocks, keep_ref, give_ref, kb):
    m, y = ids_ref[1], ids_ref[2]
    for turn in range(2):
        for g in range(GROUPS):
            picked = []
            for member in range(2):
                first = jnp.where(y == 0, blocks[0][g][member], blocks[1][g][member])
                second = jnp.where(y == 0, blocks[1][g][member], blocks[0][g][member])
                picked.append(first if turn == 0 else second)
            cols = keep_ref.shape[3]
            mine = jnp.where(m == 0, picked[0], picked[1])
            other = jnp.where(m == 0, picked[1], picked[0])
            keep_ref[turn, g, kb:, :] = jnp.zeros((16, cols), F32)
            give_ref[turn, g, kb:, :] = jnp.zeros((16, cols), BF)
            keep_ref[turn, g, kb:, :kb] = mine
            give_ref[turn, g, kb:, :kb] = other.astype(BF)


def output_grads(ids, mixed_rel, back, first_sums, final_sums, gate_sum, up_sum, kb):
    rows, width = back.shape
    cols = mixed_rel[0].shape[1]

    def body(ids_ref, *refs):
        back_ref, fs_ref, ls_ref, gs_ref, us_ref, keep_ref, give_ref, full_ref = refs[GROUPS:]
        for k, ref in enumerate(refs[:GROUPS]):
            full_ref[piece_rows(ids_ref, k, cols, -1), :] = dot_tn(ref[...], back_ref[...])
        split_rows(ids_ref, full_ref, keep_ref, give_ref, kb)
        y, x = ids_ref[2], ids_ref[3]
        sums = jnp.concatenate([fs_ref[0:3, :], ls_ref[0:3, :]], axis=0)
        wide = (gs_ref[...], us_ref[...])
        blocks = []
        for row in range(2):
            blocks.append([])
            for g in range(GROUPS):
                blocks[-1].append([])
                for member in range(2):
                    b = row * 8 + g * 2 + member
                    lines = []
                    for i in range(8):
                        at = ((b % 4) * 4 + (i // 4) * 2 + i % 2) * kb
                        mine = (y == (b % 8) // 4) & (x == (i % 4) // 2)
                        lines.append(jnp.where(mine, wide[b // 8][:, at : at + kb], 0.0))
                    lines = [sums[:, b * kb : (b + 1) * kb]] + lines + [jnp.zeros((2, kb), F32)]
                    blocks[-1][-1].append(jnp.concatenate(lines, axis=0))
        place_small(ids_ref, blocks, keep_ref, give_ref, kb)

    shape = (2, GROUPS, kb + 16, width)
    return call(
        body,
        "output_grads",
        [ids] + list(mixed_rel) + [back, first_sums, final_sums, gate_sum, up_sum],
        [(shape, F32), (shape, BF)],
        scratch=[pltpu.VMEM((width, width), F32)],
        flops=2 * rows * width * width,
    )


def tokens_parts(ids, back, weight, low):
    count, cols = back.shape
    rows = count // GROUPS
    width = weight.shape[0]
    more = low.shape[1]

    def body(jb_ref, w_ref, low_ref, out_ref):
        for g in range(GROUPS):
            part = dot_nt(jb_ref[g * rows : (g + 1) * rows, :], w_ref[...])
            out_ref[g, :rows, :] = part.astype(BF)
            out_ref[g, rows:, :] = low_ref[g]

    return call(
        body,
        "tokens_parts",
        [back, weight, low],
        [((GROUPS, rows + more, width), BF)],
        flops=2 * count * width * cols,
    )[0]


def finish_tokens(got, attn_back):
    rows, width = attn_back.shape
    more = got.shape[1] - rows

    def body(got_ref, attn_ref, out_ref, sum_ref):
        total = attn_ref[...]
        rest = jnp.zeros((more, width), F32)
        for g in range(GROUPS):
            total = total + got_ref[g, :rows, :].astype(F32)
            rest = rest + got_ref[g, rows:, :].astype(F32)
        out_ref[...] = total
        sum_ref[...] = rest.astype(BF)

    return call(
        body,
        "finish_tokens",
        [got, attn_back],
        [((rows, width), F32), ((more, width), BF)],
    )


def joined_grads(ids, x_four, query_back, keep, got, kb):
    count, width = x_four.shape
    cols = query_back.shape[1]
    wide = 3 * cols

    def body(ids_ref, x_ref, q_ref, kv_ref, got_ref, keep_ref, give_ref, back_ref, full_ref):
        back_ref[:, :cols] = q_ref[...]
        back_ref[:, cols:] = (kv_ref[...] + got_ref[...].astype(F32)).astype(BF)
        full_ref[...] = dot_tn(x_ref[...], back_ref[...])
        split_rows(ids_ref, full_ref, keep_ref, give_ref, kb)
        g_own = ids_ref[0]
        sums = jnp.sum(back_ref[...].astype(F32), axis=0, keepdims=True)
        pair = jnp.concatenate([sums[:, :cols], sums[:, 2 * cols :], jnp.zeros((14, cols), F32)], axis=0)
        blocks = []
        for row in range(2):
            blocks.append([])
            for g in range(GROUPS):
                blocks[-1].append([])
                for member in range(2):
                    b = row * 8 + g * 2 + member
                    part = pair[:, (b % GROUPS) * kb : (b % GROUPS + 1) * kb]
                    blocks[-1][-1].append(jnp.where(g_own == b // GROUPS, part, 0.0))
        place_small(ids_ref, blocks, keep_ref, give_ref, kb)

    shape = (2, GROUPS, kb + 16, wide)
    return call(
        body,
        "joined_grads",
        [ids, x_four, query_back, keep, got],
        [(shape, F32), (shape, BF), ((count, wide), BF)],
        scratch=[pltpu.VMEM((width, wide), F32)],
        flops=2 * count * width * wide,
    )


def cut_wide(ids, total, kb):
    cols = total.shape[1] - 16 * kb
    width = 16 * kb

    def body(ids_ref, all_ref, side_ref, far_ref):
        y = ids_ref[2]
        side_ref[:, :cols] = all_ref[pl.ds(pl.multiple_of(y * kb, 16), kb), :cols]
        for half in range(2):
            side_ref[:, cols + half * width : cols + (half + 1) * width] = all_ref[half * kb : (half + 1) * kb, cols:]
        far_ref[...] = all_ref[pl.ds(pl.multiple_of((1 - y) * kb, 16), kb), :cols]

    return call(body, "cut_wide", [ids, total], [((kb, cols + 2 * width), BF), ((kb, cols), BF)])


def finish_widen(ids, pieces):
    kb, cols = pieces[2].shape
    width = 16 * kb
    half = 2 * kb
    quarter = cols // 2
    count = quarter // half

    def body(ids_ref, *refs):
        out_ref, narrow_ref, all_ref = refs[4:]
        y, x = ids_ref[2], ids_ref[3]
        for k in range(4):
            row = y if k < 2 else 1 - y
            col = x if k % 2 == 0 else 1 - x
            all_ref[row * 2 + col] = refs[k][:, :cols].astype(F32)
        for part in range(2):
            for row in range(2):
                picks = []
                for c in range(count):
                    for col in range(2):
                        at = part * quarter + c * half
                        picks.append(all_ref[row * 2 + col, :, at : at + half])
                at = (part * 2 + row) * 2 * quarter
                out_ref[:, at : at + 2 * quarter] = jnp.concatenate(picks, axis=1)
        for k in range(2):
            for line in range(2):
                at = (x if k == 0 else 1 - x) * half + line * kb
                rows = pl.ds(pl.multiple_of(at, 16), kb)
                narrow_ref[rows, :] = refs[k][:, cols + line * width : cols + (line + 1) * width].astype(F32)

    return call(
        body,
        "finish_widen",
        [ids] + list(pieces),
        [((kb, 8 * quarter), F32), ((2 * half, width), F32)],
        scratch=[pltpu.VMEM((4, kb, cols), F32)],
    )


def cut_joined(ids, own, got):
    shape = own.shape[1:]

    def body(ids_ref, own_ref, got_ref, *outs):
        for k, ref in enumerate(outs):
            turn = (ids_ref[0] + k) % GROUPS
            ref[...] = (own_ref[turn].astype(F32) + got_ref[turn].astype(F32)).astype(BF)

    return call(body, "cut_joined", [ids, own, got], [(shape, BF)] * GROUPS)


def finish_joined(ids, pieces, kb):
    lines, wide = pieces[0].shape
    cols = wide // 3

    def body(ids_ref, *refs):
        out_ref, small_ref, got_ref = refs[GROUPS:]
        for k in range(GROUPS):
            got_ref[(ids_ref[0] + GROUPS - k) % GROUPS] = refs[k][...]
        for g in range(GROUPS):
            for part in range(3):
                at = (part * GROUPS + g) * cols
                out_ref[:, at : at + cols] = got_ref[g, :kb, part * cols : (part + 1) * cols].astype(F32)
        small = jnp.zeros((16, wide), F32)
        for g in range(GROUPS):
            small = small + got_ref[g, kb:, :].astype(F32)
        small_ref[...] = small

    return call(
        body,
        "finish_joined",
        [ids] + list(pieces),
        [((kb, GROUPS * wide), F32), ((16, wide), F32)],
        scratch=[pltpu.VMEM((GROUPS, lines, wide), BF)],
    )


def fast_device(
    tokens,
    segments,
    joined_weight,
    query_bias,
    value_bias,
    output_weight,
    output_bias,
    first_gain,
    first_shift,
    widen_weight,
    widen_bias,
    narrow_weight,
    narrow_bias,
    final_gain,
    final_shift,
    cotangent,
):
    at = Layout()
    n, r = at.size, at.members
    rows, width = tokens.shape[1:]
    heads = width // HEAD_DIM
    near_heads = heads // GROUPS
    cols = near_heads * HEAD_DIM
    kb = joined_weight.shape[0]
    ff_own = narrow_weight.shape[0]
    quarter = 4 * ff_own
    span = 2 * ff_own
    seg_row = segments[0]
    length = seg_row.shape[0]
    scale = 1.0 / math.sqrt(HEAD_DIM)
    inputs = tokens[0]
    columns = [[g * r + m for g in range(GROUPS)] for m in range(r)]
    ids = jnp.stack([at.group, at.member, at.seq, at.rep]).astype(jnp.int32)

    def across(value):
        return lax.all_to_all(value, "ctx", 0, 0, axis_index_groups=columns, tiled=True)

    def spread_out(value):
        far = at.swap(value, "seq")
        return (value, far, at.partner(value), at.partner(far))

    packed = pack_joined(
        ids,
        joined_weight,
        [
            query_bias,
            value_bias,
            output_bias,
            first_gain,
            first_shift,
            narrow_bias,
            final_gain,
            final_shift,
        ],
        widen_bias,
        cols,
    )
    output_far = after(at.swap(output_weight, "seq"), packed[0])
    output_pair = jnp.where(
        at.seq == 0,
        jnp.concatenate([output_weight, output_far], axis=0),
        jnp.concatenate([output_far, output_weight], axis=0),
    )
    output_got = lax.all_gather(output_pair, "ctx", tiled=True)
    joined_rel = [packed[0]] + [at.shift(packed[k], k) for k in range(1, GROUPS)]
    x_cut = jnp.broadcast_to(after(inputs, *joined_rel)[None], (GROUPS, rows, width))
    x_four = across(x_cut).reshape(-1, width)
    joined_got = jnp.stack(joined_rel)
    joined_parts = spread_out(joined_got)
    w_joined, vec, near, wide = assemble_joined(ids, joined_parts, kb)
    widen_near, widen_far, narrow_low = pick_widen(after(ids, packed[3]), widen_weight, narrow_weight)
    widen_got = at.swap(after(widen_far, *joined_rel), "seq")
    widen_all = pack_widen(ids, after(widen_near, w_joined), widen_got, narrow_low)
    w_wide = lax.all_gather(widen_all, "ctx", tiled=True)

    queries, kv_own = split_joined(x_four, w_joined, near, scale)
    kv_other = at.partner(kv_own)
    lanes = jnp.arange(rows, dtype=jnp.int32)

    def places(member):
        return ((jnp.arange(GROUPS, dtype=jnp.int32) * r + member)[:, None] * rows + lanes).reshape(-1)

    by_member = jnp.transpose(seg_row.reshape(GROUPS, r, rows), (1, 0, 2)).reshape(r, -1)

    def documents(member):
        return lax.dynamic_index_in_dim(by_member, member, 0, keepdims=False)

    q_row = jnp.stack([places(at.member), documents(at.member)]).astype(F32)
    o_row = jnp.stack([places(1 - at.member), documents(1 - at.member)]).astype(F32)
    k_row = jnp.concatenate([q_row, o_row], axis=1)
    q_col = jnp.transpose(q_row)
    k_col = jnp.transpose(k_row)
    order_heads = at.group * near_heads + jnp.arange(near_heads, dtype=jnp.int32)
    slopes = jnp.power(2.0, -8.0 * (order_heads.astype(F32) + 1.0) / heads) * (512.0 / length)
    attended = attend(ids, slopes, queries, kv_own, kv_other, q_col, k_row)
    mixed_near, inv = attended[:2]
    mixed_send = attended[2:]
    mixed_rel = [mixed_send[0]] + [at.shift(mixed_send[k], k) for k in range(1, GROUPS)]
    w_output = assemble_output(output_got, kb)

    first, first_low, first_unit, first_root = close_attention(
        ids, inputs, mixed_rel, w_output, vec, kb
    )
    first_rel = [first_low] + [at.plane(first_low, k) for k in (1, 2, 3)]
    own, s1, s2, s3, hidden, gate, up = widen_narrow(first_rel, w_wide, wide)
    received = [at.plane(s1, 1), at.plane(s2, 2), at.plane(s3, 3)]
    gate_factor, up_factor = gate_slopes(gate, up)
    result, final_back, narrow_back, final_sums = turn_final(own, received, first, cotangent[0], vec)

    back_rel = [narrow_back] + [at.plane(narrow_back, k) for k in (1, 2, 3)]
    own, s1, s2, s3, gate_back, up_back = widen_narrow_back(back_rel, w_wide, gate_factor, up_factor)
    received = [at.plane(s1, 1), at.plane(s2, 2), at.plane(s3, 3)]
    wide_grad, gate_sum, up_sum = wide_grads(
        first_rel, gate_back, up_back, hidden, back_rel
    )
    wide_sum = lax.psum_scatter(wide_grad, "ctx", tiled=True)
    turned = turn_first(ids, own, received, final_back, first_unit, first_root, w_output, vec, kb)
    attn_back, output_back, first_sums = turned[:3]
    back_send = turned[3:]
    back_near = [back_send[0]] + [at.shift(back_send[k], k) for k in range(1, GROUPS)]

    output_keep, output_give = output_grads(
        ids, mixed_rel, output_back, first_sums, final_sums, gate_sum, up_sum, kb
    )

    def seq_send(keep, got):
        return (keep + got.astype(F32)).astype(BF)

    output_got = at.partner(output_give)

    query_back, kv_keep, kv_give = attend_back(
        ids, slopes, queries, back_near, mixed_near, inv, kv_own, kv_other, q_row, k_col, scale
    )
    output_far = at.swap(seq_send(output_keep[1], output_got[1]), "seq")
    kv_give, output_far = lax.optimization_barrier((kv_give, output_far))
    kv_got = at.partner(kv_give)

    output_sum = (output_keep[0] + output_got[0].astype(F32) + output_far.astype(F32)).astype(BF)
    joined_keep, joined_give, joined_back = joined_grads(ids, x_four, query_back, kv_keep, kv_got, kb)
    joined_got = at.partner(joined_give)
    parts = tokens_parts(ids, joined_back, w_joined, output_sum)
    tokens_got = across(parts)
    joined_far = at.swap(seq_send(joined_keep[1], after(joined_got, parts)[1]), "seq")
    joined_sum = (joined_keep[0] + joined_got[0].astype(F32) + joined_far.astype(F32)).astype(BF)
    wide_sum = after(wide_sum, joined_got)
    side, far = cut_wide(ids, wide_sum, kb)
    widen_pieces = [side, at.plane(side, 1), at.plane(far, 2), at.plane(far, 3)]
    joined_mine = cut_joined(after(ids, *widen_pieces[1:]), joined_sum, at.swap(joined_sum, "rep"))
    widen_total, narrow_total = finish_widen(ids, widen_pieces)
    joined_total, pair = finish_joined(
        ids,
        [joined_mine[0]] + [at.shift(joined_mine[k], k) for k in range(1, GROUPS)],
        kb,
    )
    tokens_grad, output_mine = finish_tokens(tokens_got, after(attn_back, joined_mine[0]))
    output_total = output_mine.astype(F32) + at.swap(output_mine, "rep").astype(F32)
    last = output_total[kb:, :kb]
    return (
        result[None],
        tokens_grad[None],
        joined_total,
        pair[0, :kb],
        pair[1, :kb],
        output_total[:kb],
        last[0],
        last[1],
        last[2],
        widen_total,
        last[6:14].reshape(-1),
        narrow_total,
        last[3],
        last[4],
        last[5],
    )


def solution(mesh):
    tokens = P(("rep", "seq"), "ctx", None)
    matrix = P(("seq", "ctx"), None)
    vector = P(("seq", "ctx"))
    near = mesh.shape["ctx"] == 2 * GROUPS and mesh.shape["rep"] == 2
    return jax.shard_map(
        fast_device if near else on_device,
        mesh=mesh,
        in_specs=(
            tokens,
            P(("rep", "seq"), None),
            matrix,
            vector,
            vector,
            matrix,
            vector,
            vector,
            vector,
            matrix,
            vector,
            matrix,
            vector,
            vector,
            vector,
            tokens,
        ),
        out_specs=(
            tokens,
            tokens,
            matrix,
            vector,
            vector,
            matrix,
            vector,
            vector,
            vector,
            matrix,
            vector,
            matrix,
            vector,
            vector,
            vector,
        ),
        check_vma=False,
    )
```

```python
import math

import jax
import jax.numpy as jnp
from jax import lax
from jax.experimental import pallas as pl
from jax.experimental.pallas import tpu as pltpu
from jax.sharding import PartitionSpec as P

HEAD_DIM = 64
GROUPS = 4
FAR = 1e30
BF = jnp.bfloat16
F32 = jnp.float32


def dot_nn(left, right):
    return lax.dot_general(left, right, (((1,), (0,)), ((), ())), preferred_element_type=F32)


def dot_tn(left, right):
    return lax.dot_general(left, right, (((0,), (0,)), ((), ())), preferred_element_type=F32)


def dot_nt(left, right):
    return lax.dot_general(left, right, (((1,), (1,)), ((), ())), preferred_element_type=F32)


def head_mask(head, cols):
    lane = lax.broadcasted_iota(jnp.int32, (1, cols), 1)
    return (lane >= head * HEAD_DIM) & (lane < (head + 1) * HEAD_DIM)


def only_head(value, head):
    return jnp.where(head_mask(head, value.shape[1]), value, jnp.zeros_like(value))


def each_chunk(count, body):
    if count <= 4:
        for index in range(count):
            body(index)
    else:
        lax.fori_loop(0, count, lambda index, carry: (body(index), carry)[1], 0)


def forward_kernel(slope_ref, q_ref, kv_ref, qinfo_ref, kinfo_ref, out_ref, inv_ref, acc_ref, sum_ref, *, chunk):
    rows, cols = q_ref.shape
    heads = cols // HEAD_DIM
    count = kv_ref.shape[0] // chunk
    acc_ref[...] = jnp.zeros_like(acc_ref)
    sum_ref[...] = jnp.zeros_like(sum_ref)
    q = q_ref[...]
    qpos = qinfo_ref[:, 0:1]
    qseg = qinfo_ref[:, 1:2]
    ones = jnp.ones((8, chunk), BF)

    def step(index):
        begin = index * chunk
        here = pl.ds(begin, chunk)
        keys = kv_ref[here, :cols]
        values = kv_ref[here, cols:]
        kpos = kinfo_ref[0:1, here]
        kseg = kinfo_ref[1:2, here]
        far = jnp.where(qseg == kseg, jnp.abs(qpos - kpos), FAR)
        for head in range(heads):
            scores = dot_nt(only_head(q, head), keys) - slope_ref[head] * far
            raised = jnp.exp(scores).astype(BF)
            sum_ref[head] += dot_nt(ones, raised)
            acc_ref[head] += dot_nn(raised, values)

    each_chunk(count, step)
    total = jnp.zeros((rows, cols), F32)
    for head in range(heads):
        inv = 1.0 / sum_ref[head]
        inv_ref[head] = inv
        column = jnp.transpose(inv)[:, 0:1]
        total = total + only_head(acc_ref[head] * column, head)
    out_ref[...] = total


def attend_forward(slopes, queries, key_value, qinfo, kinfo, interpret=False):
    count, cols = queries.shape
    heads = cols // HEAD_DIM
    keys = key_value.shape[0]
    chunk = math.gcd(keys, 512)
    rows = math.gcd(count, 128)
    whole = lambda shape: pl.BlockSpec(shape, lambda i: tuple(0 for _ in shape))
    return pl.pallas_call(
        lambda *refs: forward_kernel(*refs, chunk=chunk),
        grid=(count // rows,),
        in_specs=[
            pl.BlockSpec(memory_space=pltpu.SMEM),
            pl.BlockSpec((rows, cols), lambda i: (i, 0)),
            whole((keys, 2 * cols)),
            pl.BlockSpec((rows, 2), lambda i: (i, 0)),
            whole((2, keys)),
        ],
        out_specs=[
            pl.BlockSpec((rows, cols), lambda i: (i, 0)),
            pl.BlockSpec((heads, 8, rows), lambda i: (0, 0, i)),
        ],
        out_shape=[
            jax.ShapeDtypeStruct((count, cols), F32),
            jax.ShapeDtypeStruct((heads, 8, count), F32),
        ],
        scratch_shapes=[pltpu.VMEM((heads, rows, cols), F32), pltpu.VMEM((heads, 8, rows), F32)],
        name="attend_forward",
        interpret=interpret,
    )(slopes, queries, key_value, qinfo, kinfo)


def backward_kernel(
    slope_ref, q_ref, do_ref, out_ref, inv_ref, kv_ref, qinfo_ref, kinfo_ref, dq_ref, dkv_ref, acc_ref, *, chunk
):
    rows, cols = q_ref.shape
    heads = cols // HEAD_DIM
    count = kv_ref.shape[0] // chunk
    q = q_ref[...]
    back = do_ref[...]
    product = back.astype(F32) * out_ref[...]
    qpos = qinfo_ref[0:1, :]
    qseg = qinfo_ref[1:2, :]
    acc_ref[...] = jnp.zeros_like(acc_ref)
    row_dots = []
    for head in range(heads):
        chosen = jnp.broadcast_to(head_mask(head, cols), (8, cols)).astype(F32)
        row_dots.append(
            lax.dot_general(
                chosen,
                product,
                (((1,), (1,)), ((), ())),
                precision=lax.Precision.HIGHEST,
                preferred_element_type=F32,
            )[0:1]
        )

    @pl.when(pl.program_id(0) == 0)
    def _():
        dkv_ref[...] = jnp.zeros_like(dkv_ref)

    def step(index):
        begin = index * chunk
        here = pl.ds(begin, chunk)
        keys = kv_ref[here, :cols]
        values = kv_ref[here, cols:]
        kpos = kinfo_ref[here, 0:1]
        kseg = kinfo_ref[here, 1:2]
        far = jnp.where(qseg == kseg, jnp.abs(qpos - kpos), FAR)
        key_part = jnp.zeros((chunk, cols), F32)
        value_part = jnp.zeros((chunk, cols), F32)
        for head in range(heads):
            q_head = only_head(q, head)
            back_head = only_head(back, head)
            scores = dot_nt(keys, q_head) - slope_ref[head] * far
            probs = jnp.exp(scores) * inv_ref[head, 0:1, :]
            prob_back = dot_nt(values, back_head)
            score_back = (probs * (prob_back - row_dots[head])).astype(BF)
            key_part = key_part + dot_nn(score_back, q_head)
            value_part = value_part + dot_nn(probs.astype(BF), back_head)
            acc_ref[head] += dot_tn(score_back, keys)
        dkv_ref[here, :cols] += key_part
        dkv_ref[here, cols:] += value_part

    each_chunk(count, step)
    total = jnp.zeros((rows, cols), F32)
    for head in range(heads):
        total = total + only_head(acc_ref[head], head)
    dq_ref[...] = total


def attend_backward(slopes, queries, back, mixed, inv, key_value, qinfo, kinfo, interpret=False):
    count, cols = queries.shape
    heads = cols // HEAD_DIM
    keys = key_value.shape[0]
    chunk = math.gcd(keys, 512)
    rows = math.gcd(count, 128)
    whole = lambda shape: pl.BlockSpec(shape, lambda i: tuple(0 for _ in shape))
    by_row = pl.BlockSpec((rows, cols), lambda i: (i, 0))
    return pl.pallas_call(
        lambda *refs: backward_kernel(*refs, chunk=chunk),
        grid=(count // rows,),
        in_specs=[
            pl.BlockSpec(memory_space=pltpu.SMEM),
            by_row,
            by_row,
            by_row,
            pl.BlockSpec((heads, 8, rows), lambda i: (0, 0, i)),
            whole((keys, 2 * cols)),
            pl.BlockSpec((2, rows), lambda i: (0, i)),
            whole((keys, 2)),
        ],
        out_specs=[by_row, whole((keys, 2 * cols))],
        out_shape=[
            jax.ShapeDtypeStruct((count, cols), F32),
            jax.ShapeDtypeStruct((keys, 2 * cols), F32),
        ],
        scratch_shapes=[pltpu.VMEM((heads, rows, cols), F32)],
        name="attend_backward",
        interpret=interpret,
    )(slopes, queries, back, mixed, inv, key_value, qinfo, kinfo)


def norm_stats(value):
    centre = jnp.mean(value, axis=-1, keepdims=True)
    centred = value - centre
    spread = jnp.mean(centred * centred, axis=-1, keepdims=True)
    root = lax.rsqrt(spread + 1e-06)
    return centred * root, root


def norm_back(unit, root, gain, back):
    scaled = back * gain
    return root * (
        scaled
        - jnp.mean(scaled, axis=-1, keepdims=True)
        - unit * jnp.mean(scaled * unit, axis=-1, keepdims=True)
    )


def after(value, *others):
    return lax.optimization_barrier((value,) + others)[0]


class Layout:
    def __init__(self):
        self.size = lax.axis_size("ctx")
        self.members = self.size // GROUPS
        index = lax.axis_index("ctx")
        self.group = index // self.members
        self.member = index % self.members
        self.seq = lax.axis_index("seq")
        self.rep = lax.axis_index("rep")
        self.inner = [
            [g * self.members + m for m in range(self.members)] for g in range(GROUPS)
        ]

    def shift(self, value, steps):
        n, r = self.size, self.members
        return lax.ppermute(value, "ctx", [(i, (i + steps * r) % n) for i in range(n)])

    def swap(self, value, axis):
        return lax.ppermute(value, axis, [(0, 1), (1, 0)])

    def plane(self, value, k):
        if k == 3:
            return lax.ppermute(value, ("rep", "seq"), [(i, 3 - i) for i in range(4)])
        return self.swap(value, "rep" if k == 1 else "seq")

    def gather(self, value):
        return [value] + [self.shift(value, k) for k in range(1, GROUPS)]

    def scatter_sum(self, parts):
        total = parts[0]
        for k in range(1, GROUPS):
            total = total + self.shift(parts[k].astype(BF), -k).astype(F32)
        return total

    def exchange(self, pieces):
        own = lax.dynamic_index_in_dim(pieces, self.group, 0, keepdims=False)
        out = [own]
        for k in range(1, GROUPS):
            target = (self.group + k) % GROUPS
            out.append(
                self.shift(lax.dynamic_index_in_dim(pieces, target, 0, keepdims=False), k)
            )
        return out

    def ordered(self, relative):
        line = [relative[0], relative[3], relative[2], relative[1]]
        twice = jnp.stack(line + line[:3])
        return lax.dynamic_slice_in_dim(twice, (GROUPS - self.group) % GROUPS, GROUPS, 0)

    def both_seq(self, value):
        other = self.swap(value, "seq")
        first = self.seq == 0
        return jnp.stack([jnp.where(first, value, other), jnp.where(first, other, value)])

    def partner(self, value):
        return lax.ppermute(
            value, "ctx", [(i, i ^ 1) for i in range(self.size)]
        )

    def all_members(self, value, axis):
        if self.members == 2:
            other = self.partner(value)
            first = self.member == 0
            return jnp.stack(
                [jnp.where(first, value, other), jnp.where(first, other, value)], axis
            )
        out = lax.all_gather(value, "ctx", axis_index_groups=self.inner)
        return jnp.moveaxis(out, 0, axis)

    def member_sum(self, pieces):
        if self.members == 2:
            keep = lax.dynamic_index_in_dim(pieces, self.member, 0, keepdims=False)
            give = lax.dynamic_index_in_dim(pieces, 1 - self.member, 0, keepdims=False)
            return keep + self.partner(give.astype(BF)).astype(F32)
        got = lax.all_to_all(
            pieces.astype(BF), "ctx", 0, 0, axis_index_groups=self.inner, tiled=True
        )
        return jnp.sum(got.astype(F32), axis=0)

    def seq_sum(self, pieces):
        keep = lax.dynamic_index_in_dim(pieces, self.seq, 0, keepdims=False)
        give = lax.dynamic_index_in_dim(pieces, 1 - self.seq, 0, keepdims=False)
        return keep + self.swap(give.astype(BF), "seq").astype(F32)

    def rep_sum(self, value):
        low = value.astype(BF)
        return low.astype(F32) + self.swap(low, "rep").astype(F32)


def on_device(
    tokens,
    segments,
    joined_weight,
    query_bias,
    value_bias,
    output_weight,
    output_bias,
    first_gain,
    first_shift,
    widen_weight,
    widen_bias,
    narrow_weight,
    narrow_bias,
    final_gain,
    final_shift,
    cotangent,
):
    at = Layout()
    n, r = at.size, at.members
    rows, width = tokens.shape[1:]
    heads = width // HEAD_DIM
    near_heads = heads // GROUPS
    cols = near_heads * HEAD_DIM
    kb = joined_weight.shape[0]
    ff_own = narrow_weight.shape[0]
    ff = ff_own * 2 * n
    quarter = ff // GROUPS
    span = r * ff_own
    seg_row = segments[0]
    length = seg_row.shape[0]
    scale = 1.0 / math.sqrt(HEAD_DIM)
    inputs = tokens[0]

    x_rel = at.gather(inputs)
    x_four = jnp.concatenate(x_rel, axis=0)

    small = jnp.concatenate(
        [
            query_bias,
            value_bias,
            output_bias,
            first_gain,
            first_shift,
            narrow_bias,
            final_gain,
            final_shift,
            widen_bias,
        ]
    )[None]
    small_all = at.all_members(at.both_seq(at.ordered(at.gather(small))), 2)
    small_all = small_all.reshape(2 * n, -1).astype(F32)

    def vector(place):
        return small_all[:, place * kb : (place + 1) * kb].reshape(width)

    b_query, b_value, b_output, g_first, s_first, b_narrow, g_final, s_final = (
        vector(place) for place in range(8)
    )
    b_widen = lax.dynamic_index_in_dim(
        small_all[:, 8 * kb :].reshape(2, 2, GROUPS, span), at.group, 2, keepdims=False
    ).reshape(2 * quarter)
    b_query = lax.dynamic_index_in_dim(b_query.reshape(GROUPS, cols), at.group, 0, keepdims=False)
    b_value = lax.dynamic_index_in_dim(b_value.reshape(GROUPS, cols), at.group, 0, keepdims=False)

    joined_cut = jnp.transpose(joined_weight.reshape(kb, 3, GROUPS, cols), (2, 0, 1, 3)).reshape(
        GROUPS, kb, 3 * cols
    )
    w_joined = at.all_members(at.both_seq(at.ordered(at.exchange(joined_cut))), 2).reshape(
        width, 3 * cols
    )

    output_low = after(output_weight, x_four)
    out_rel = at.ordered(at.gather(output_low)).reshape(GROUPS * kb, width)
    both = at.both_seq(jnp.concatenate([out_rel, narrow_weight], axis=0))
    both = at.all_members(both, 1)
    w_output = jnp.transpose(
        both[:, :, : GROUPS * kb].reshape(2, r, GROUPS, kb, width), (0, 2, 1, 3, 4)
    ).reshape(width, width)
    w_narrow = both[:, :, GROUPS * kb :].reshape(quarter, width)

    widen_cut = jnp.transpose(
        after(widen_weight, x_four).reshape(kb, 4, GROUPS, span), (2, 0, 1, 3)
    ).reshape(GROUPS, kb, 2 * quarter)
    w_widen = at.all_members(at.both_seq(at.ordered(at.exchange(widen_cut))), 2).reshape(
        width, 2 * quarter
    )

    lanes = jnp.arange(rows, dtype=jnp.int32)
    near = (at.group - jnp.arange(GROUPS, dtype=jnp.int32)) % GROUPS

    def places(member):
        return ((near * r + member)[:, None] * rows + lanes[None]).reshape(-1)

    if r == 2:
        key_members = jnp.stack([at.member, 1 - at.member])
    else:
        key_members = jnp.arange(r, dtype=jnp.int32)
    query_pos = places(at.member)
    key_pos = jnp.concatenate([places(key_members[i]) for i in range(r)])
    query_seg = jnp.take(seg_row, query_pos)
    key_seg = jnp.take(seg_row, key_pos)
    q_info = jnp.stack([query_pos, query_seg]).astype(F32)
    k_info = jnp.stack([key_pos, key_seg]).astype(F32)
    order_heads = at.group * near_heads + jnp.arange(near_heads, dtype=jnp.int32)
    slopes = jnp.power(2.0, -8.0 * (order_heads.astype(F32) + 1.0) / heads) * (512.0 / length)

    joined = dot_nn(x_four, w_joined)
    queries = ((joined[:, :cols] + b_query) * scale).astype(BF)
    kv_own = jnp.concatenate(
        [joined[:, cols : 2 * cols], joined[:, 2 * cols :] + b_value], axis=1
    ).astype(BF)
    if r == 2:
        key_value = jnp.concatenate([kv_own, at.partner(kv_own)], axis=0)
    else:
        key_value = at.all_members(kv_own, 0).reshape(-1, 2 * cols)
    mixed_near, inv = attend_forward(slopes, queries, key_value, jnp.transpose(q_info), k_info)
    mixed_low = mixed_near.astype(BF).reshape(GROUPS, rows, cols)
    mixed_rel = [mixed_low[0]] + [at.shift(mixed_low[k], -k) for k in range(1, GROUPS)]
    mixed_rel = [mixed_rel[0], mixed_rel[3], mixed_rel[2], mixed_rel[1]]
    mixed = jnp.transpose(at.ordered(mixed_rel), (1, 0, 2)).reshape(rows, width)

    first_in = inputs.astype(F32) + dot_nn(mixed, w_output) + b_output
    first_unit, first_root = norm_stats(first_in)
    first = first_unit * g_first + s_first
    first_low = first.astype(BF)

    first_four = jnp.concatenate(at.gather(first_low), axis=0)
    gate_up = dot_nn(first_four, w_widen) + b_widen
    gate, up = gate_up[:, :quarter], gate_up[:, quarter:]
    phi_big = 0.5 * (1.0 + lax.erf(gate * math.sqrt(0.5)))
    gelu = gate * phi_big
    slope_gate = phi_big + gate * jnp.exp(-0.5 * gate * gate) * (1.0 / math.sqrt(2.0 * math.pi))
    hidden = (gelu * up).astype(BF)
    final_part = dot_nn(hidden, w_narrow).reshape(GROUPS, rows, width)
    final_in = first + at.scatter_sum([final_part[k] for k in range(GROUPS)]) + b_narrow
    final_unit, final_root = norm_stats(final_in)
    result = final_unit * g_final + s_final

    upstream = cotangent[0].astype(F32)
    final_back = norm_back(final_unit, final_root, g_final, upstream)
    final_gain_grad = jnp.sum(upstream * final_unit, axis=0)
    final_shift_grad = jnp.sum(upstream, axis=0)
    narrow_back = final_back.astype(BF)
    narrow_bias_grad = jnp.sum(narrow_back.astype(F32), axis=0)
    back_four = jnp.concatenate(at.gather(narrow_back), axis=0)
    hidden_back = dot_nt(back_four, w_narrow)
    widen_back = jnp.concatenate(
        [hidden_back * up * slope_gate, hidden_back * gelu], axis=1
    ).astype(BF)
    first_part = dot_nt(widen_back, w_widen).reshape(GROUPS, rows, width)
    first_back = final_back + at.scatter_sum([first_part[k] for k in range(GROUPS)])
    narrow_grad = dot_tn(hidden, back_four)
    widen_grad = dot_tn(first_four, widen_back)
    widen_bias_grad = jnp.sum(widen_back.astype(F32), axis=0)

    attn_back = norm_back(first_unit, first_root, g_first, first_back)
    first_gain_grad = jnp.sum(first_back * first_unit, axis=0)
    first_shift_grad = jnp.sum(first_back, axis=0)
    output_back = attn_back.astype(BF)
    output_bias_grad = jnp.sum(output_back.astype(F32), axis=0)
    output_grad = dot_tn(mixed, output_back)
    mixed_back = dot_nt(output_back, w_output).astype(BF)
    mixed_back = jnp.transpose(mixed_back.reshape(rows, GROUPS, cols), (1, 0, 2))
    back_near = jnp.concatenate(at.exchange(mixed_back), axis=0)

    query_sum, kv_sum = attend_backward(
        slopes, queries, back_near, mixed_near, inv, key_value, q_info, jnp.transpose(k_info)
    )
    if r == 2:
        half = kv_sum.shape[0] // 2
        kv_back = kv_sum[:half] + at.partner(kv_sum[half:].astype(BF)).astype(F32)
    else:
        kv_back = at.member_sum(kv_sum.reshape(r, -1, 2 * cols))
    query_low = query_sum.astype(BF)
    query_scaled = (query_low.astype(F32) * scale).astype(BF)
    joined_back = jnp.concatenate([query_scaled, kv_back.astype(BF)], axis=1)
    tokens_part = dot_nt(joined_back, w_joined).reshape(GROUPS, rows, width)
    tokens_grad = attn_back + at.scatter_sum([tokens_part[k] for k in range(GROUPS)])
    joined_grad = dot_tn(x_four, joined_back)
    near_bias = jnp.sum(joined_back.astype(F32), axis=0)
    query_bias_grad = near_bias[:cols]
    value_bias_grad = near_bias[2 * cols :]

    narrow_sum = at.member_sum(jnp.transpose(narrow_grad.reshape(2, r, ff_own, width), (1, 0, 2, 3)))
    narrow_total = at.rep_sum(at.seq_sum(narrow_sum))

    def to_rows(grad):
        pieces = jnp.transpose(grad.reshape(2, GROUPS, r, kb, -1), (2, 0, 1, 3, 4))
        mine = at.rep_sum(at.seq_sum(at.member_sum(pieces))).astype(BF)
        return at.ordered(at.exchange(mine))

    widen_total = jnp.transpose(
        to_rows(widen_grad).reshape(GROUPS, kb, 4, span), (1, 2, 0, 3)
    ).reshape(kb, 2 * ff)
    joined_total = jnp.transpose(
        to_rows(joined_grad).reshape(GROUPS, kb, 3, cols), (1, 2, 0, 3)
    ).reshape(kb, 3 * width)

    def spread(vector, parts):
        wide = jnp.zeros((parts, GROUPS, vector.shape[0] // parts), F32)
        return lax.dynamic_update_slice_in_dim(
            wide, vector.reshape(parts, 1, -1), at.group, 1
        ).reshape(-1)

    vectors = [
        spread(query_bias_grad, 1),
        spread(value_bias_grad, 1),
        output_bias_grad,
        first_gain_grad,
        first_shift_grad,
        narrow_bias_grad,
        final_gain_grad,
        final_shift_grad,
    ]
    row = jnp.concatenate(
        [item.reshape(2 * n, kb) for item in vectors]
        + [spread(widen_bias_grad, 4).reshape(2 * n, 8 * kb)],
        axis=1,
    )
    row = jnp.pad(row[:, None, :], ((0, 0), (0, 15), (0, width - 16 * kb)))
    packed = jnp.concatenate([output_grad.reshape(2 * n, kb, width), row], axis=1)
    packed = jnp.transpose(packed.reshape(2, GROUPS, r, kb + 16, width), (2, 0, 1, 3, 4))
    packed = at.seq_sum(at.member_sum(packed)).astype(BF)
    packed = at.exchange(packed)
    packed = sum(item.astype(F32) for item in packed[1:]) + packed[0].astype(F32)
    packed = at.rep_sum(packed)
    output_total = packed[:kb]
    last = packed[kb]

    def owned(place):
        return last[place * kb : (place + 1) * kb]

    return (
        result.astype(BF)[None],
        tokens_grad[None],
        joined_total.astype(F32),
        owned(0),
        owned(1),
        output_total,
        owned(2),
        owned(3),
        owned(4),
        widen_total.astype(F32),
        last[8 * kb : 16 * kb],
        narrow_total,
        owned(5),
        owned(6),
        owned(7),
    )


def vmem(shape):
    return pl.BlockSpec(shape, lambda *_: tuple(0 for _ in shape))


COSTS = {
    "pack_joined": 0,
    "assemble_joined": 0,
    "pick_widen": 0,
    "pack_widen": 0,
    "cut_joined": 0,
    "cut_wide": 0,
    "assemble_output": 0,
    "finish_tokens": 0,
    "split_joined": 3,
    "attend": 5,
    "attend_back": 8,
    "close_attention": 3,
    "widen_narrow": 6,
    "widen_narrow_back": 7,
    "turn_final": 3,
    "turn_first": 3,
    "wide_grads": 6,
    "output_grads": 3,
    "tokens_parts": 0,
    "joined_grads": 4,
    "finish_widen": 0,
    "finish_joined": 0,
}

SMEM = pl.BlockSpec(memory_space=pltpu.SMEM)


def call(body, name, inputs, outputs, scratch=(), grid=(1,), in_specs=None, out_specs=None, flops=0):
    shapes = [jax.ShapeDtypeStruct(shape, kind) for shape, kind in outputs]
    if in_specs is None:
        in_specs = [SMEM if item.ndim == 1 else vmem(item.shape) for item in inputs]
    if out_specs is None:
        out_specs = [vmem(shape) for shape, kind in outputs]
    moved = sum(item.size * item.dtype.itemsize for item in list(inputs) + shapes)
    return pl.pallas_call(
        body,
        grid=grid,
        in_specs=in_specs,
        out_specs=out_specs,
        out_shape=shapes,
        scratch_shapes=list(scratch),
        name=name,
        cost_estimate=pl.CostEstimate(flops=int(COSTS[name] * 5 * 1e9), transcendentals=0, bytes_accessed=0),
    )(*inputs)


def pack_joined(ids, weight, vectors, widen_bias, cols):
    kb = weight.shape[0]
    vectors = [item[None] for item in vectors]
    shape = (kb + 16, 3 * cols)

    def body(*refs):
        ids_ref, w_ref, wide_ref = refs[0], refs[1], refs[10]
        all_ref = refs[15]
        rows = [ref[...].astype(F32) for ref in refs[2:10]]
        wide = wide_ref[...].astype(F32)
        rows += [wide[:, k * kb : (k + 1) * kb] for k in range(8)]
        small = jnp.concatenate(rows, axis=0).astype(BF)
        for g in range(GROUPS):
            for part in range(3):
                at = (part * GROUPS + g) * cols
                all_ref[g, :kb, part * cols : (part + 1) * cols] = w_ref[:, at : at + cols]
            all_ref[g, kb:, :] = jnp.zeros((16, 3 * cols), BF)
            all_ref[g, kb:, :kb] = small
        for k in range(GROUPS):
            refs[11 + k][...] = all_ref[(ids_ref[0] + k) % GROUPS]

    inputs = [ids, weight] + vectors + [widen_bias[None]]
    return call(
        body,
        "pack_joined",
        inputs,
        [(shape, BF)] * GROUPS,
        scratch=[pltpu.VMEM((GROUPS,) + shape, BF)],
    )


def place_rows(ids_ref, pieces, out_ref, kb, relative=False):
    group, m, y = ids_ref[0], ids_ref[1], ids_ref[2]
    for index, piece in enumerate(pieces):
        row = y if index % 2 == 0 else 1 - y
        member = m if index < 2 else 1 - m
        for g in range(GROUPS):
            source = (group + GROUPS - g) % GROUPS if relative else g
            start = pl.multiple_of((row * GROUPS * 2 + source * 2 + member) * kb, 16)
            out_ref[pl.ds(start, kb), :] = piece[g, :kb, :]


def assemble_joined(ids, pieces, kb):
    cols = pieces[0].shape[2]
    near = cols // 3
    width = 4 * GROUPS * kb
    span = 8 * kb

    def body(ids_ref, a_ref, b_ref, c_ref, d_ref, w_ref, vec_ref, near_ref, wide_ref):
        place_rows(ids_ref, (a_ref, b_ref, c_ref, d_ref), w_ref, kb, True)
        g, m, y, x = ids_ref[0], ids_ref[1], ids_ref[2], ids_ref[3]
        blocks = []
        for row in range(2):
            for k in range(GROUPS):
                for member in range(2):
                    turn = (g + GROUPS - k) % GROUPS
                    picks = [ref[turn, kb:, :kb].astype(F32) for ref in (a_ref, b_ref, c_ref, d_ref)]
                    mine = jnp.where(row == y, picks[0], picks[1])
                    theirs = jnp.where(row == y, picks[2], picks[3])
                    blocks.append(jnp.where(member == m, mine, theirs))
        vec = jnp.concatenate(blocks, axis=1)
        vec_ref[...] = vec
        total = jnp.zeros((16, near), F32)
        for k in range(GROUPS):
            total = jnp.where(g == k, vec[:, k * near : (k + 1) * near], total)
        near_ref[...] = total
        lines = []
        for part in range(2):
            for c in range(8):
                low = 8 + (c % 2) * 4
                picks = []
                for row in range(2):
                    at = (part * 8 + row * 4 + c // 2) * kb
                    picks.append(vec[low : low + 4, at : at + kb])
                both = jnp.where(y == 0, picks[0], picks[1])
                pair = jnp.where(x == 0, both[0:2], both[2:4])
                lines += [pair[0:1], pair[1:2]]
        wide_ref[...] = jnp.concatenate(lines, axis=1)

    return call(
        body,
        "assemble_joined",
        [ids] + list(pieces),
        [((width, cols), BF), ((16, width), F32), ((16, near), F32), ((1, 4 * span), F32)],
    )


def pick_widen(ids, weight, narrow):
    kb, total = weight.shape
    own, width = narrow.shape
    half = own // 2
    side = total // 4
    count = side // own
    quarter = count * half

    wide = 2 * quarter

    def body(ids_ref, w_ref, n_ref, near_ref, far_ref, low_ref, all_ref):
        y, x = ids_ref[2], ids_ref[3]
        for row in range(2):
            for col in range(2):
                pieces = []
                for part in range(2):
                    for c in range(count):
                        at = part * 2 * side + row * side + c * own + col * half
                        pieces.append(w_ref[:, at : at + half])
                all_ref[row * 2 + col] = jnp.concatenate(pieces, axis=1)
        near_ref[...] = all_ref[y * 2 + x]
        far_ref[...] = all_ref[(1 - y) * 2 + x]
        low_ref[...] = n_ref[pl.ds(pl.multiple_of(x * half, 16), half), :]

    return call(
        body,
        "pick_widen",
        [ids, weight, narrow],
        [((kb, wide), BF), ((kb, wide), BF), ((half, width), BF)],
        scratch=[pltpu.VMEM((4, kb, wide), BF)],
    )


def pack_widen(ids, near, got, low):
    kb, cols = near.shape
    width = low.shape[1]

    def body(ids_ref, near_ref, got_ref, low_ref, out_ref):
        y = ids_ref[2]
        out_ref[pl.ds(pl.multiple_of(y * kb, 16), kb), :cols] = near_ref[...]
        out_ref[pl.ds(pl.multiple_of((1 - y) * kb, 16), kb), :cols] = got_ref[...]
        out_ref[:, cols:] = low_ref[...]

    return call(body, "pack_widen", [ids, near, got, low], [((2 * kb, cols + width), BF)])[0]


def assemble_output(weights, kb):
    width, cols = weights.shape
    half = width // (2 * kb)

    def body(all_ref, w_ref):
        for y in range(2):
            for c in range(half):
                rows = slice((c * 2 + y) * kb, (c * 2 + y + 1) * kb)
                w_ref[(y * half + c) * kb : (y * half + c + 1) * kb, :] = all_ref[rows, :]

    return call(body, "assemble_output", [weights], [((width, cols), BF)])[0]


def owner_order(value, kb):
    half = value.shape[1] // (2 * kb)
    blocks = [y * half + c for c in range(half) for y in range(2)]
    return jnp.concatenate([value[:, b * kb : (b + 1) * kb] for b in blocks], axis=1)


def column_order(value, kb):
    half = value.shape[1] // (2 * kb)
    blocks = [c * 2 + y for y in range(2) for c in range(half)]
    return jnp.concatenate([value[:, b * kb : (b + 1) * kb] for b in blocks], axis=1)


def split_joined(x_four, weight, near, scale):
    count, width = x_four.shape
    cols = weight.shape[1] // 3

    def body(x_ref, w_ref, near_ref, q_ref, kv_ref):
        joined = dot_nn(x_ref[...], w_ref[...])
        q_ref[...] = ((joined[:, :cols] + near_ref[0:1, :]) * scale).astype(BF)
        kv_ref[:, :cols] = joined[:, cols : 2 * cols].astype(BF)
        kv_ref[:, cols:] = (joined[:, 2 * cols :] + near_ref[1:2, :]).astype(BF)

    return call(
        body,
        "split_joined",
        [x_four, weight, near],
        [((count, cols), BF), ((count, 2 * cols), BF)],
        flops=2 * count * width * 3 * cols,
    )


def piece_rows(ids_ref, k, rows, sign=1):
    turn = (ids_ref[0] + (k if sign > 0 else GROUPS - k)) % GROUPS
    return pl.ds(pl.multiple_of(turn * rows, 16), rows)


def attend(ids, slopes, queries, kv_own, kv_other, q_col, k_row):
    count, cols = queries.shape
    heads = cols // HEAD_DIM
    rows = count // GROUPS
    chunk = kv_own.shape[0]

    def body(ids_ref, slope_ref, q_ref, own_ref, other_ref, qi_ref, ki_ref, out_ref, inv_ref, *sends):
        q = q_ref[...]
        qpos = qi_ref[:, 0:1]
        qseg = qi_ref[:, 1:2]
        ones = jnp.ones((chunk, 64), BF)
        q_heads = [only_head(q, head) for head in range(heads)]
        accs = [None] * heads
        for side, kv_ref in enumerate((own_ref, other_ref)):
            here = slice(side * chunk, (side + 1) * chunk)
            keys = kv_ref[:, :cols]
            values = jnp.concatenate([kv_ref[:, cols:], ones], axis=1)
            far = jnp.where(qseg == ki_ref[1:2, here], jnp.abs(qpos - ki_ref[0:1, here]), FAR)
            for head in range(heads):
                scores = dot_nt(q_heads[head], keys) - slope_ref[head] * far
                part = dot_nn(jnp.exp(scores).astype(BF), values)
                accs[head] = part if side == 0 else accs[head] + part
        total = jnp.zeros((count, cols), F32)
        for head in range(heads):
            inv = 1.0 / accs[head][:, cols : cols + 1]
            inv_ref[head] = jnp.transpose(jnp.broadcast_to(inv, (count, 128)))[:8]
            total = total + only_head(accs[head][:, :cols] * inv, head)
        out_ref[...] = total
        for k, ref in enumerate(sends):
            ref[...] = out_ref[piece_rows(ids_ref, k, rows), :].astype(BF)

    return call(
        body,
        "attend",
        [ids, slopes, queries, kv_own, kv_other, q_col, k_row],
        [((count, cols), F32), ((heads, 8, count), F32)] + [((rows, cols), BF)] * GROUPS,
        flops=4 * count * 2 * chunk * cols,
    )


def attend_back(ids, slopes, queries, back_rel, mixed, inv, kv_own, kv_other, q_row, k_col, scale):
    count, cols = queries.shape
    heads = cols // HEAD_DIM
    rows = count // GROUPS
    chunk = kv_own.shape[0]

    def body(ids_ref, slope_ref, q_ref, *refs):
        pieces = refs[:GROUPS]
        out_ref, inv_ref, own_ref, other_ref, qi_ref, ki_ref, dq_ref, keep_ref, give_ref, do_ref = refs[GROUPS:]
        for k, ref in enumerate(pieces):
            do_ref[piece_rows(ids_ref, k, rows, -1), :] = ref[...]
        q = q_ref[...]
        back = do_ref[...]
        product = back.astype(F32) * out_ref[...]
        qpos = qi_ref[0:1, :]
        qseg = qi_ref[1:2, :]
        q_heads = [only_head(q, head) for head in range(heads)]
        b_heads = [only_head(back, head) for head in range(heads)]
        place = lax.broadcasted_iota(jnp.int32, (8, cols), 0)
        lane = lax.broadcasted_iota(jnp.int32, (8, cols), 1)
        row_dots = lax.dot_general(
            (lane // HEAD_DIM == place).astype(F32),
            product,
            (((1,), (1,)), ((), ())),
            precision=lax.Precision.HIGHEST,
            preferred_element_type=F32,
        )
        query_parts = [None] * heads
        for side, kv_ref in enumerate((own_ref, other_ref)):
            here = slice(side * chunk, (side + 1) * chunk)
            keys = kv_ref[:, :cols]
            values = kv_ref[:, cols:]
            far = jnp.where(qseg == ki_ref[here, 1:2], jnp.abs(qpos - ki_ref[here, 0:1]), FAR)
            key_part = None
            value_part = None
            for head in range(heads):
                scores = dot_nt(keys, q_heads[head]) - slope_ref[head] * far
                probs = jnp.exp(scores) * inv_ref[head, 0:1, :]
                prob_back = dot_nt(values, b_heads[head])
                score_back = (probs * (prob_back - row_dots[head : head + 1])).astype(BF)
                k_part = dot_nn(score_back, q_heads[head])
                v_part = dot_nn(probs.astype(BF), b_heads[head])
                q_part = dot_tn(score_back, keys)
                key_part = k_part if head == 0 else key_part + k_part
                value_part = v_part if head == 0 else value_part + v_part
                query_parts[head] = q_part if side == 0 else query_parts[head] + q_part
            target = keep_ref if side == 0 else give_ref
            target[:, :cols] = key_part.astype(target.dtype)
            target[:, cols:] = value_part.astype(target.dtype)
        total = jnp.zeros((count, cols), F32)
        for head in range(heads):
            total = total + only_head(query_parts[head], head)
        dq_ref[...] = (total.astype(BF).astype(F32) * scale).astype(BF)

    return call(
        body,
        "attend_back",
        [ids, slopes, queries] + list(back_rel) + [mixed, inv, kv_own, kv_other, q_row, k_col],
        [((count, cols), BF), ((chunk, 2 * cols), F32), ((chunk, 2 * cols), BF)],
        scratch=[pltpu.VMEM((count, cols), BF)],
        flops=10 * count * 2 * chunk * cols,
    )


def close_attention(ids, inputs, mixed_rel, weight, vec, kb):
    rows, width = inputs.shape
    cols = mixed_rel[0].shape[1]

    def body(ids_ref, x_ref, a_ref, b_ref, c_ref, d_ref, w_ref, vec_ref, first_ref, low_ref, unit_ref, root_ref):
        total = x_ref[...].astype(F32) + vec_ref[2:3, :]
        for k, ref in enumerate((a_ref, b_ref, c_ref, d_ref)):
            total = total + dot_nn(ref[...], w_ref[piece_rows(ids_ref, k, cols, -1), :])
        unit, root = norm_stats(total)
        first = unit * vec_ref[3:4, :] + vec_ref[4:5, :]
        first_ref[...] = first
        low_ref[...] = owner_order(first, kb).astype(BF)
        unit_ref[...] = unit
        root_ref[...] = root

    return call(
        body,
        "close_attention",
        [ids, inputs] + list(mixed_rel) + [weight, vec],
        [((rows, width), F32), ((rows, width), BF), ((rows, width), F32), ((rows, 1), F32)],
        flops=2 * rows * width * width,
    )


def block_of(quarter):
    return math.gcd(quarter, 256)


def join_pieces(refs):
    return jnp.concatenate([ref[...] for ref in refs], axis=0)


def send_pieces(total, refs, rows):
    for k, ref in enumerate(refs):
        ref[...] = total[k * rows : (k + 1) * rows, :].astype(ref.dtype)


def widen_narrow(rel, weights, wide):
    rows, width = rel[0].shape
    quarter = wide.shape[1] // 2
    count = GROUPS * rows

    def body(*refs):
        w_ref, wide_ref = refs[4:6]
        hid_ref, gate_ref, up_ref = refs[10:13]
        value = join_pieces(refs[:4])
        gate = dot_nn(value, w_ref[:, :quarter]) + wide_ref[:, :quarter]
        up = dot_nn(value, w_ref[:, quarter : 2 * quarter]) + wide_ref[:, quarter:]
        gate_ref[...] = gate
        up_ref[...] = up
        hidden = (gate * (0.5 + 0.5 * lax.erf(gate * math.sqrt(0.5))) * up).astype(BF)
        hid_ref[...] = hidden
        send_pieces(dot_nn(hidden, w_ref[:, 2 * quarter :]), refs[6:10], rows)

    return call(
        body,
        "widen_narrow",
        list(rel) + [weights, wide],
        [((rows, width), F32)]
        + [((rows, width), BF)] * 3
        + [((count, quarter), BF), ((count, quarter), F32), ((count, quarter), F32)],
        flops=6 * count * width * quarter,
    )


def gate_slopes(gate, up):
    phi_big = 0.5 + 0.5 * lax.erf(gate * math.sqrt(0.5))
    slope = phi_big + gate * jnp.exp(-0.5 * gate * gate) * (1.0 / math.sqrt(2.0 * math.pi))
    return up * slope, gate * phi_big


def widen_narrow_back(rel, weights, gate_factor, up_factor):
    rows, width = rel[0].shape
    count, quarter = gate_factor.shape

    def body(*refs):
        w_ref, gf_ref, uf_ref = refs[4:7]
        bg_ref, bu_ref = refs[11:13]
        hidden_back = dot_nt(join_pieces(refs[:4]), w_ref[:, 2 * quarter :])
        gate_back = (hidden_back * gf_ref[...]).astype(BF)
        up_back = (hidden_back * uf_ref[...]).astype(BF)
        bg_ref[...] = gate_back
        bu_ref[...] = up_back
        total = dot_nt(gate_back, w_ref[:, :quarter]) + dot_nt(up_back, w_ref[:, quarter : 2 * quarter])
        send_pieces(total, refs[7:11], rows)

    return call(
        body,
        "widen_narrow_back",
        list(rel) + [weights, gate_factor, up_factor],
        [((rows, width), F32)] + [((rows, width), BF)] * 3 + [((count, quarter), BF)] * 2,
        flops=6 * count * width * quarter,
    )


def turn_final(own, received, first, upstream, vec):
    rows, width = own.shape

    def body(own_ref, a_ref, b_ref, c_ref, first_ref, up_ref, vec_ref, res_ref, back_ref, low_ref, sum_ref):
        total = first_ref[...] + vec_ref[5:6, :] + own_ref[...]
        for ref in (a_ref, b_ref, c_ref):
            total = total + ref[...].astype(F32)
        unit, root = norm_stats(total)
        gain = vec_ref[6:7, :]
        res_ref[...] = (unit * gain + vec_ref[7:8, :]).astype(BF)
        upstream = up_ref[...].astype(F32)
        back = norm_back(unit, root, gain, upstream)
        low = back.astype(BF)
        back_ref[...] = back
        low_ref[...] = low
        sum_ref[...] = jnp.zeros_like(sum_ref)
        sum_ref[0:1, :] = jnp.sum(low.astype(F32), axis=0, keepdims=True)
        sum_ref[1:2, :] = jnp.sum(upstream * unit, axis=0, keepdims=True)
        sum_ref[2:3, :] = jnp.sum(upstream, axis=0, keepdims=True)

    return call(
        body,
        "turn_final",
        [own] + list(received) + [first, upstream, vec],
        [((rows, width), BF), ((rows, width), F32), ((rows, width), BF), ((8, width), F32)],
    )


def turn_first(ids, own, received, final_back, unit, root, weight, vec, kb):
    rows, width = own.shape
    cols = width // GROUPS

    def body(ids_ref, own_ref, a_ref, b_ref, c_ref, fb_ref, unit_ref, root_ref, w_ref, vec_ref, *outs):
        attn_ref, low_ref, sum_ref = outs[:3]
        total = own_ref[...]
        for ref in (a_ref, b_ref, c_ref):
            total = total + ref[...].astype(F32)
        total = fb_ref[...] + column_order(total, kb)
        unit = unit_ref[...]
        back = norm_back(unit, root_ref[...], vec_ref[3:4, :], total)
        low = back.astype(BF)
        attn_ref[...] = back
        low_ref[...] = low
        for k, ref in enumerate(outs[3:]):
            ref[...] = dot_nt(low, w_ref[piece_rows(ids_ref, k, cols), :]).astype(BF)
        sum_ref[...] = jnp.zeros_like(sum_ref)
        sum_ref[0:1, :] = jnp.sum(low.astype(F32), axis=0, keepdims=True)
        sum_ref[1:2, :] = jnp.sum(total * unit, axis=0, keepdims=True)
        sum_ref[2:3, :] = jnp.sum(total, axis=0, keepdims=True)

    return call(
        body,
        "turn_first",
        [ids, own] + list(received) + [final_back, unit, root, weight, vec],
        [((rows, width), F32), ((rows, width), BF), ((8, width), F32)] + [((rows, cols), BF)] * GROUPS,
        flops=2 * rows * width * width,
    )


def split_rows(ids_ref, full_ref, keep_ref, give_ref, kb, lead=()):
    m, y = ids_ref[1], ids_ref[2]
    for turn in range(2):
        row = y if turn == 0 else 1 - y
        for g in range(GROUPS):
            base = (row * GROUPS + g) * 2
            mine = pl.ds(pl.multiple_of((base + m) * kb, 16), kb)
            other = pl.ds(pl.multiple_of((base + 1 - m) * kb, 16), kb)
            keep_ref[lead + (turn, g, slice(0, kb), slice(None))] = full_ref[mine, :]
            give_ref[lead + (turn, g, slice(0, kb), slice(None))] = full_ref[other, :].astype(BF)


def wide_grads(first_rel, gate_back, up_back, hidden, back_rel):
    rows, width = first_rel[0].shape
    count, quarter = gate_back.shape

    def body(*refs):
        gate_ref, up_ref, hid_ref = refs[8:11]
        out_ref, gs_ref, us_ref = refs[11:14]
        value = join_pieces(refs[:4])
        for turn, (ref, sum_ref) in enumerate(((gate_ref, gs_ref), (up_ref, us_ref))):
            back = ref[...]
            out_ref[:, turn * quarter : (turn + 1) * quarter] = dot_tn(value, back).astype(BF)
            sum_ref[...] = jnp.sum(back.astype(F32), axis=0, keepdims=True)
        out_ref[:, 2 * quarter :] = dot_tn(hid_ref[...], join_pieces(refs[4:8])).astype(BF)

    return call(
        body,
        "wide_grads",
        list(first_rel) + list(back_rel) + [gate_back, up_back, hidden],
        [((width, 2 * quarter + width), BF), ((1, quarter), F32), ((1, quarter), F32)],
        flops=6 * count * width * quarter,
    )


def place_small(ids_ref, blocks, keep_ref, give_ref, kb):
    m, y = ids_ref[1], ids_ref[2]
    for turn in range(2):
        for g in range(GROUPS):
            picked = []
            for member in range(2):
                first = jnp.where(y == 0, blocks[0][g][member], blocks[1][g][member])
                second = jnp.where(y == 0, blocks[1][g][member], blocks[0][g][member])
                picked.append(first if turn == 0 else second)
            cols = keep_ref.shape[3]
            mine = jnp.where(m == 0, picked[0], picked[1])
            other = jnp.where(m == 0, picked[1], picked[0])
            keep_ref[turn, g, kb:, :] = jnp.zeros((16, cols), F32)
            give_ref[turn, g, kb:, :] = jnp.zeros((16, cols), BF)
            keep_ref[turn, g, kb:, :kb] = mine
            give_ref[turn, g, kb:, :kb] = other.astype(BF)


def output_grads(ids, mixed_rel, back, first_sums, final_sums, gate_sum, up_sum, kb):
    rows, width = back.shape
    cols = mixed_rel[0].shape[1]

    def body(ids_ref, *refs):
        back_ref, fs_ref, ls_ref, gs_ref, us_ref, keep_ref, give_ref, small_ref, full_ref = refs[GROUPS:]
        for k, ref in enumerate(refs[:GROUPS]):
            full_ref[piece_rows(ids_ref, k, cols, -1), :] = dot_tn(ref[...], back_ref[...])
        split_rows(ids_ref, full_ref, keep_ref, give_ref, kb)
        y, x = ids_ref[2], ids_ref[3]
        sums = jnp.concatenate([fs_ref[0:3, :], ls_ref[0:3, :]], axis=0)
        wide = (gs_ref[...], us_ref[...])
        for owner in range(16):
            lines = []
            for i in range(8):
                at = ((owner % 4) * 4 + (i // 4) * 2 + i % 2) * kb
                mine = (y == (owner % 8) // 4) & (x == (i % 4) // 2)
                lines.append(jnp.where(mine, wide[owner // 8][:, at : at + kb], 0.0))
            lines = [sums[:, owner * kb : (owner + 1) * kb]] + lines + [jnp.zeros((2, kb), F32)]
            small_ref[owner] = jnp.concatenate(lines, axis=0)

    shape = (2, GROUPS, kb, width)
    return call(
        body,
        "output_grads",
        [ids] + list(mixed_rel) + [back, first_sums, final_sums, gate_sum, up_sum],
        [(shape, F32), (shape, BF), ((16, 16, kb), F32)],
        scratch=[pltpu.VMEM((width, width), F32)],
        flops=2 * rows * width * width,
    )


def tokens_parts(ids, back, weight, keep, got, far):
    count, cols = back.shape
    rows = count // GROUPS
    width = weight.shape[0]
    more = far.shape[1]
    first = pl.BlockSpec((1, GROUPS, more, width), lambda i: (0, 0, 0, 0))

    def body(jb_ref, w_ref, keep_ref, got_ref, far_ref, out_ref):
        for g in range(GROUPS):
            part = dot_nt(jb_ref[g * rows : (g + 1) * rows, :], w_ref[...])
            out_ref[g, :rows, :] = part.astype(BF)
            low = keep_ref[0, g] + got_ref[0, g].astype(F32) + far_ref[g].astype(F32)
            out_ref[g, rows:, :] = low.astype(BF)

    return call(
        body,
        "tokens_parts",
        [back, weight, keep, got, far],
        [((GROUPS, rows + more, width), BF)],
        in_specs=[vmem(back.shape), vmem(weight.shape), first, first, vmem(far.shape)],
        flops=2 * count * width * cols,
    )[0]


def finish_tokens(got, attn_back):
    rows, width = attn_back.shape
    more = got.shape[1] - rows

    def body(got_ref, attn_ref, out_ref, sum_ref):
        total = attn_ref[...]
        rest = jnp.zeros((more, width), F32)
        for g in range(GROUPS):
            total = total + got_ref[g, :rows, :].astype(F32)
            rest = rest + got_ref[g, rows:, :].astype(F32)
        out_ref[...] = total
        sum_ref[...] = rest.astype(BF)

    return call(
        body,
        "finish_tokens",
        [got, attn_back],
        [((rows, width), F32), ((more, width), BF)],
    )


def joined_grads(ids, x_four, query_back, keep, got, small, kb):
    count, width = x_four.shape
    cols = query_back.shape[1]
    wide = 3 * cols

    def body(ids_ref, x_ref, q_ref, kv_ref, got_ref, small_ref, keep_ref, give_ref, back_ref, full_ref):
        back_ref[:, :cols] = q_ref[...]
        back_ref[:, cols:] = (kv_ref[...] + got_ref[...].astype(F32)).astype(BF)
        full_ref[...] = dot_tn(x_ref[...], back_ref[...])
        split_rows(ids_ref, full_ref, keep_ref, give_ref, kb)
        g_own = ids_ref[0]
        sums = jnp.sum(back_ref[...].astype(F32), axis=0, keepdims=True)
        pair = jnp.concatenate([jnp.zeros((14, cols), F32), sums[:, :cols], sums[:, 2 * cols :]], axis=0)
        blocks = []
        for row in range(2):
            blocks.append([])
            for g in range(GROUPS):
                blocks[-1].append([])
                for member in range(2):
                    b = row * 8 + g * 2 + member
                    part = pair[:, (b % GROUPS) * kb : (b % GROUPS + 1) * kb]
                    blocks[-1][-1].append(small_ref[b] + jnp.where(g_own == b // GROUPS, part, 0.0))
        place_small(ids_ref, blocks, keep_ref, give_ref, kb)

    shape = (2, GROUPS, kb + 16, wide)
    return call(
        body,
        "joined_grads",
        [ids, x_four, query_back, keep, got, small],
        [(shape, F32), (shape, BF), ((count, wide), BF)],
        scratch=[pltpu.VMEM((width, wide), F32)],
        flops=2 * count * width * wide,
    )


def cut_wide(ids, total, kb):
    cols = total.shape[1] - 16 * kb
    width = 16 * kb

    def body(ids_ref, all_ref, side_ref, far_ref):
        y = ids_ref[2]
        side_ref[:, :cols] = all_ref[pl.ds(pl.multiple_of(y * kb, 16), kb), :cols]
        for half in range(2):
            side_ref[:, cols + half * width : cols + (half + 1) * width] = all_ref[half * kb : (half + 1) * kb, cols:]
        far_ref[...] = all_ref[pl.ds(pl.multiple_of((1 - y) * kb, 16), kb), :cols]

    return call(body, "cut_wide", [ids, total], [((kb, cols + 2 * width), BF), ((kb, cols), BF)])


def finish_widen(ids, pieces):
    kb, cols = pieces[2].shape
    width = 16 * kb
    half = 2 * kb
    quarter = cols // 2
    count = quarter // half

    def body(ids_ref, *refs):
        out_ref, narrow_ref, all_ref = refs[4:]
        y, x = ids_ref[2], ids_ref[3]
        for k in range(4):
            row = y if k < 2 else 1 - y
            col = x if k % 2 == 0 else 1 - x
            all_ref[row * 2 + col] = refs[k][:, :cols].astype(F32)
        for part in range(2):
            for row in range(2):
                picks = []
                for c in range(count):
                    for col in range(2):
                        at = part * quarter + c * half
                        picks.append(all_ref[row * 2 + col, :, at : at + half])
                at = (part * 2 + row) * 2 * quarter
                out_ref[:, at : at + 2 * quarter] = jnp.concatenate(picks, axis=1)
        for k in range(2):
            for line in range(2):
                at = (x if k == 0 else 1 - x) * half + line * kb
                rows = pl.ds(pl.multiple_of(at, 16), kb)
                narrow_ref[rows, :] = refs[k][:, cols + line * width : cols + (line + 1) * width].astype(F32)

    return call(
        body,
        "finish_widen",
        [ids] + list(pieces),
        [((kb, 8 * quarter), F32), ((2 * half, width), F32)],
        scratch=[pltpu.VMEM((4, kb, cols), F32)],
    )


def cut_joined(ids, own, got):
    shape = own.shape[1:]

    def body(ids_ref, own_ref, got_ref, *outs):
        for k, ref in enumerate(outs):
            turn = (ids_ref[0] + k) % GROUPS
            ref[...] = (own_ref[turn].astype(F32) + got_ref[turn].astype(F32)).astype(BF)

    return call(body, "cut_joined", [ids, own, got], [(shape, BF)] * GROUPS)


def finish_joined(ids, pieces, kb):
    lines, wide = pieces[0].shape
    cols = wide // 3

    def body(ids_ref, *refs):
        out_ref, small_ref, got_ref = refs[GROUPS:]
        for k in range(GROUPS):
            got_ref[(ids_ref[0] + GROUPS - k) % GROUPS] = refs[k][...]
        for g in range(GROUPS):
            for part in range(3):
                at = (part * GROUPS + g) * cols
                out_ref[:, at : at + cols] = got_ref[g, :kb, part * cols : (part + 1) * cols].astype(F32)
        small = jnp.zeros((16, wide), F32)
        for g in range(GROUPS):
            small = small + got_ref[g, kb:, :].astype(F32)
        small_ref[...] = small

    return call(
        body,
        "finish_joined",
        [ids] + list(pieces),
        [((kb, GROUPS * wide), F32), ((16, wide), F32)],
        scratch=[pltpu.VMEM((GROUPS, lines, wide), BF)],
    )


def fast_device(
    tokens,
    segments,
    joined_weight,
    query_bias,
    value_bias,
    output_weight,
    output_bias,
    first_gain,
    first_shift,
    widen_weight,
    widen_bias,
    narrow_weight,
    narrow_bias,
    final_gain,
    final_shift,
    cotangent,
):
    at = Layout()
    n, r = at.size, at.members
    rows, width = tokens.shape[1:]
    heads = width // HEAD_DIM
    near_heads = heads // GROUPS
    cols = near_heads * HEAD_DIM
    kb = joined_weight.shape[0]
    ff_own = narrow_weight.shape[0]
    quarter = 4 * ff_own
    span = 2 * ff_own
    seg_row = segments[0]
    length = seg_row.shape[0]
    scale = 1.0 / math.sqrt(HEAD_DIM)
    inputs = tokens[0]
    columns = [[g * r + m for g in range(GROUPS)] for m in range(r)]
    ids = jnp.stack([at.group, at.member, at.seq, at.rep]).astype(jnp.int32)

    def across(value):
        return lax.all_to_all(value, "ctx", 0, 0, axis_index_groups=columns, tiled=True)

    def spread_out(value):
        far = at.swap(value, "seq")
        return (value, far, at.partner(value), at.partner(far))

    packed = pack_joined(
        ids,
        joined_weight,
        [
            query_bias,
            value_bias,
            output_bias,
            first_gain,
            first_shift,
            narrow_bias,
            final_gain,
            final_shift,
        ],
        widen_bias,
        cols,
    )
    output_far = after(at.swap(output_weight, "seq"), packed[0])
    output_pair = jnp.where(
        at.seq == 0,
        jnp.concatenate([output_weight, output_far], axis=0),
        jnp.concatenate([output_far, output_weight], axis=0),
    )
    output_got = lax.all_gather(output_pair, "ctx", tiled=True)
    joined_rel = [packed[0]] + [at.shift(packed[k], k) for k in range(1, GROUPS)]
    x_cut = jnp.broadcast_to(after(inputs, *joined_rel)[None], (GROUPS, rows, width))
    x_four = across(x_cut).reshape(-1, width)
    joined_got = jnp.stack(joined_rel)
    joined_parts = spread_out(joined_got)
    w_joined, vec, near, wide = assemble_joined(ids, joined_parts, kb)
    widen_near, widen_far, narrow_low = pick_widen(after(ids, packed[3]), widen_weight, narrow_weight)
    widen_got = at.swap(after(widen_far, *joined_rel), "seq")
    widen_all = pack_widen(ids, after(widen_near, w_joined), widen_got, narrow_low)
    w_wide = lax.all_gather(widen_all, "ctx", tiled=True)

    queries, kv_own = split_joined(x_four, w_joined, near, scale)
    kv_other = at.partner(kv_own)
    lanes = jnp.arange(rows, dtype=jnp.int32)

    def places(member):
        return ((jnp.arange(GROUPS, dtype=jnp.int32) * r + member)[:, None] * rows + lanes).reshape(-1)

    by_member = jnp.transpose(seg_row.reshape(GROUPS, r, rows), (1, 0, 2)).reshape(r, -1)

    def documents(member):
        return lax.dynamic_index_in_dim(by_member, member, 0, keepdims=False)

    q_row = jnp.stack([places(at.member), documents(at.member)]).astype(F32)
    o_row = jnp.stack([places(1 - at.member), documents(1 - at.member)]).astype(F32)
    k_row = jnp.concatenate([q_row, o_row], axis=1)
    q_col = jnp.transpose(q_row)
    k_col = jnp.transpose(k_row)
    order_heads = at.group * near_heads + jnp.arange(near_heads, dtype=jnp.int32)
    slopes = jnp.power(2.0, -8.0 * (order_heads.astype(F32) + 1.0) / heads) * (512.0 / length)
    attended = attend(ids, slopes, queries, kv_own, kv_other, q_col, k_row)
    mixed_near, inv = attended[:2]
    mixed_send = attended[2:]
    mixed_rel = [mixed_send[0]] + [at.shift(mixed_send[k], k) for k in range(1, GROUPS)]
    w_output = assemble_output(output_got, kb)

    first, first_low, first_unit, first_root = close_attention(
        ids, inputs, mixed_rel, w_output, vec, kb
    )
    first_rel = [first_low] + [at.plane(first_low, k) for k in (1, 2, 3)]
    own, s1, s2, s3, hidden, gate, up = widen_narrow(first_rel, w_wide, wide)
    received = [at.plane(s1, 1), at.plane(s2, 2), at.plane(s3, 3)]
    gate_factor, up_factor = gate_slopes(gate, up)
    result, final_back, narrow_back, final_sums = turn_final(own, received, first, cotangent[0], vec)

    back_rel = [narrow_back] + [at.plane(narrow_back, k) for k in (1, 2, 3)]
    own, s1, s2, s3, gate_back, up_back = widen_narrow_back(back_rel, w_wide, gate_factor, up_factor)
    received = [at.plane(s1, 1), at.plane(s2, 2), at.plane(s3, 3)]
    wide_grad, gate_sum, up_sum = wide_grads(
        first_rel, gate_back, up_back, hidden, back_rel
    )
    wide_sum = lax.psum_scatter(wide_grad, "ctx", tiled=True)
    turned = turn_first(ids, own, received, final_back, first_unit, first_root, w_output, vec, kb)
    attn_back, output_back, first_sums = turned[:3]
    back_send = turned[3:]
    back_near = [back_send[0]] + [at.shift(back_send[k], k) for k in range(1, GROUPS)]

    output_keep, output_give, small = output_grads(
        ids, mixed_rel, output_back, first_sums, final_sums, gate_sum, up_sum, kb
    )

    def seq_send(keep, got):
        return (keep + got.astype(F32)).astype(BF)

    output_got = at.partner(output_give)

    query_back, kv_keep, kv_give = attend_back(
        ids, slopes, queries, back_near, mixed_near, inv, kv_own, kv_other, q_row, k_col, scale
    )
    output_far = at.swap(seq_send(output_keep[1], after(output_got, query_back)[1]), "seq")
    kv_got = at.partner(kv_give)

    joined_keep, joined_give, joined_back = joined_grads(ids, x_four, query_back, kv_keep, kv_got, small, kb)
    joined_got = at.partner(joined_give)
    parts = tokens_parts(ids, joined_back, w_joined, output_keep, output_got, output_far)
    tokens_got = across(parts)
    joined_far = at.swap(seq_send(joined_keep[1], after(joined_got, parts)[1]), "seq")
    joined_sum = (joined_keep[0] + joined_got[0].astype(F32) + joined_far.astype(F32)).astype(BF)
    wide_sum = after(wide_sum, joined_got)
    side, far = cut_wide(ids, wide_sum, kb)
    widen_pieces = [side, at.plane(side, 1), at.plane(far, 2), at.plane(far, 3)]
    joined_mine = cut_joined(after(ids, *widen_pieces[1:]), joined_sum, at.swap(joined_sum, "rep"))
    widen_total, narrow_total = finish_widen(ids, widen_pieces)
    joined_total, pair = finish_joined(
        ids,
        [joined_mine[0]] + [at.shift(joined_mine[k], k) for k in range(1, GROUPS)],
        kb,
    )
    tokens_grad, output_mine = finish_tokens(tokens_got, after(attn_back, joined_mine[0]))
    output_total = output_mine.astype(F32) + at.swap(output_mine, "rep").astype(F32)
    last = pair[:, :kb]
    return (
        result[None],
        tokens_grad[None],
        joined_total,
        last[14],
        last[15],
        output_total,
        last[0],
        last[1],
        last[2],
        widen_total,
        last[6:14].reshape(-1),
        narrow_total,
        last[3],
        last[4],
        last[5],
    )


def solution(mesh):
    tokens = P(("rep", "seq"), "ctx", None)
    matrix = P(("seq", "ctx"), None)
    vector = P(("seq", "ctx"))
    near = mesh.shape["ctx"] == 2 * GROUPS and mesh.shape["rep"] == 2
    return jax.shard_map(
        fast_device if near else on_device,
        mesh=mesh,
        in_specs=(
            tokens,
            P(("rep", "seq"), None),
            matrix,
            vector,
            vector,
            matrix,
            vector,
            vector,
            vector,
            matrix,
            vector,
            matrix,
            vector,
            vector,
            vector,
            tokens,
        ),
        out_specs=(
            tokens,
            tokens,
            matrix,
            vector,
            vector,
            matrix,
            vector,
            vector,
            vector,
            matrix,
            vector,
            matrix,
            vector,
            vector,
            vector,
        ),
        check_vma=False,
    )
```

```python
import math

import jax
import jax.numpy as jnp
from jax import lax
from jax.experimental import pallas as pl
from jax.experimental.pallas import tpu as pltpu
from jax.sharding import PartitionSpec as P

HEAD_DIM = 64
GROUPS = 4
FAR = 1e30
BF = jnp.bfloat16
F32 = jnp.float32


def dot_nn(left, right):
    return lax.dot_general(left, right, (((1,), (0,)), ((), ())), preferred_element_type=F32)


def dot_tn(left, right):
    return lax.dot_general(left, right, (((0,), (0,)), ((), ())), preferred_element_type=F32)


def dot_nt(left, right):
    return lax.dot_general(left, right, (((1,), (1,)), ((), ())), preferred_element_type=F32)


def head_mask(head, cols):
    lane = lax.broadcasted_iota(jnp.int32, (1, cols), 1)
    return (lane >= head * HEAD_DIM) & (lane < (head + 1) * HEAD_DIM)


def only_head(value, head):
    return jnp.where(head_mask(head, value.shape[1]), value, jnp.zeros_like(value))


def each_chunk(count, body):
    if count <= 4:
        for index in range(count):
            body(index)
    else:
        lax.fori_loop(0, count, lambda index, carry: (body(index), carry)[1], 0)


def forward_kernel(slope_ref, q_ref, kv_ref, qinfo_ref, kinfo_ref, out_ref, inv_ref, acc_ref, sum_ref, *, chunk):
    rows, cols = q_ref.shape
    heads = cols // HEAD_DIM
    count = kv_ref.shape[0] // chunk
    acc_ref[...] = jnp.zeros_like(acc_ref)
    sum_ref[...] = jnp.zeros_like(sum_ref)
    q = q_ref[...]
    qpos = qinfo_ref[:, 0:1]
    qseg = qinfo_ref[:, 1:2]
    ones = jnp.ones((8, chunk), BF)

    def step(index):
        begin = index * chunk
        here = pl.ds(begin, chunk)
        keys = kv_ref[here, :cols]
        values = kv_ref[here, cols:]
        kpos = kinfo_ref[0:1, here]
        kseg = kinfo_ref[1:2, here]
        far = jnp.where(qseg == kseg, jnp.abs(qpos - kpos), FAR)
        for head in range(heads):
            scores = dot_nt(only_head(q, head), keys) - slope_ref[head] * far
            raised = jnp.exp(scores).astype(BF)
            sum_ref[head] += dot_nt(ones, raised)
            acc_ref[head] += dot_nn(raised, values)

    each_chunk(count, step)
    total = jnp.zeros((rows, cols), F32)
    for head in range(heads):
        inv = 1.0 / sum_ref[head]
        inv_ref[head] = inv
        column = jnp.transpose(inv)[:, 0:1]
        total = total + only_head(acc_ref[head] * column, head)
    out_ref[...] = total


def attend_forward(slopes, queries, key_value, qinfo, kinfo, interpret=False):
    count, cols = queries.shape
    heads = cols // HEAD_DIM
    keys = key_value.shape[0]
    chunk = math.gcd(keys, 512)
    rows = math.gcd(count, 128)
    whole = lambda shape: pl.BlockSpec(shape, lambda i: tuple(0 for _ in shape))
    return pl.pallas_call(
        lambda *refs: forward_kernel(*refs, chunk=chunk),
        grid=(count // rows,),
        in_specs=[
            pl.BlockSpec(memory_space=pltpu.SMEM),
            pl.BlockSpec((rows, cols), lambda i: (i, 0)),
            whole((keys, 2 * cols)),
            pl.BlockSpec((rows, 2), lambda i: (i, 0)),
            whole((2, keys)),
        ],
        out_specs=[
            pl.BlockSpec((rows, cols), lambda i: (i, 0)),
            pl.BlockSpec((heads, 8, rows), lambda i: (0, 0, i)),
        ],
        out_shape=[
            jax.ShapeDtypeStruct((count, cols), F32),
            jax.ShapeDtypeStruct((heads, 8, count), F32),
        ],
        scratch_shapes=[pltpu.VMEM((heads, rows, cols), F32), pltpu.VMEM((heads, 8, rows), F32)],
        name="attend_forward",
        interpret=interpret,
    )(slopes, queries, key_value, qinfo, kinfo)


def backward_kernel(
    slope_ref, q_ref, do_ref, out_ref, inv_ref, kv_ref, qinfo_ref, kinfo_ref, dq_ref, dkv_ref, acc_ref, *, chunk
):
    rows, cols = q_ref.shape
    heads = cols // HEAD_DIM
    count = kv_ref.shape[0] // chunk
    q = q_ref[...]
    back = do_ref[...]
    product = back.astype(F32) * out_ref[...]
    qpos = qinfo_ref[0:1, :]
    qseg = qinfo_ref[1:2, :]
    acc_ref[...] = jnp.zeros_like(acc_ref)
    row_dots = []
    for head in range(heads):
        chosen = jnp.broadcast_to(head_mask(head, cols), (8, cols)).astype(F32)
        row_dots.append(
            lax.dot_general(
                chosen,
                product,
                (((1,), (1,)), ((), ())),
                precision=lax.Precision.HIGHEST,
                preferred_element_type=F32,
            )[0:1]
        )

    @pl.when(pl.program_id(0) == 0)
    def _():
        dkv_ref[...] = jnp.zeros_like(dkv_ref)

    def step(index):
        begin = index * chunk
        here = pl.ds(begin, chunk)
        keys = kv_ref[here, :cols]
        values = kv_ref[here, cols:]
        kpos = kinfo_ref[here, 0:1]
        kseg = kinfo_ref[here, 1:2]
        far = jnp.where(qseg == kseg, jnp.abs(qpos - kpos), FAR)
        key_part = jnp.zeros((chunk, cols), F32)
        value_part = jnp.zeros((chunk, cols), F32)
        for head in range(heads):
            q_head = only_head(q, head)
            back_head = only_head(back, head)
            scores = dot_nt(keys, q_head) - slope_ref[head] * far
            probs = jnp.exp(scores) * inv_ref[head, 0:1, :]
            prob_back = dot_nt(values, back_head)
            score_back = (probs * (prob_back - row_dots[head])).astype(BF)
            key_part = key_part + dot_nn(score_back, q_head)
            value_part = value_part + dot_nn(probs.astype(BF), back_head)
            acc_ref[head] += dot_tn(score_back, keys)
        dkv_ref[here, :cols] += key_part
        dkv_ref[here, cols:] += value_part

    each_chunk(count, step)
    total = jnp.zeros((rows, cols), F32)
    for head in range(heads):
        total = total + only_head(acc_ref[head], head)
    dq_ref[...] = total


def attend_backward(slopes, queries, back, mixed, inv, key_value, qinfo, kinfo, interpret=False):
    count, cols = queries.shape
    heads = cols // HEAD_DIM
    keys = key_value.shape[0]
    chunk = math.gcd(keys, 512)
    rows = math.gcd(count, 128)
    whole = lambda shape: pl.BlockSpec(shape, lambda i: tuple(0 for _ in shape))
    by_row = pl.BlockSpec((rows, cols), lambda i: (i, 0))
    return pl.pallas_call(
        lambda *refs: backward_kernel(*refs, chunk=chunk),
        grid=(count // rows,),
        in_specs=[
            pl.BlockSpec(memory_space=pltpu.SMEM),
            by_row,
            by_row,
            by_row,
            pl.BlockSpec((heads, 8, rows), lambda i: (0, 0, i)),
            whole((keys, 2 * cols)),
            pl.BlockSpec((2, rows), lambda i: (0, i)),
            whole((keys, 2)),
        ],
        out_specs=[by_row, whole((keys, 2 * cols))],
        out_shape=[
            jax.ShapeDtypeStruct((count, cols), F32),
            jax.ShapeDtypeStruct((keys, 2 * cols), F32),
        ],
        scratch_shapes=[pltpu.VMEM((heads, rows, cols), F32)],
        name="attend_backward",
        interpret=interpret,
    )(slopes, queries, back, mixed, inv, key_value, qinfo, kinfo)


def norm_stats(value):
    centre = jnp.mean(value, axis=-1, keepdims=True)
    centred = value - centre
    spread = jnp.mean(centred * centred, axis=-1, keepdims=True)
    root = lax.rsqrt(spread + 1e-06)
    return centred * root, root


def norm_back(unit, root, gain, back):
    scaled = back * gain
    return root * (
        scaled
        - jnp.mean(scaled, axis=-1, keepdims=True)
        - unit * jnp.mean(scaled * unit, axis=-1, keepdims=True)
    )


def after(value, *others):
    return lax.optimization_barrier((value,) + others)[0]


class Layout:
    def __init__(self):
        self.size = lax.axis_size("ctx")
        self.members = self.size // GROUPS
        index = lax.axis_index("ctx")
        self.group = index // self.members
        self.member = index % self.members
        self.seq = lax.axis_index("seq")
        self.rep = lax.axis_index("rep")
        self.inner = [
            [g * self.members + m for m in range(self.members)] for g in range(GROUPS)
        ]

    def shift(self, value, steps):
        n, r = self.size, self.members
        return lax.ppermute(value, "ctx", [(i, (i + steps * r) % n) for i in range(n)])

    def swap(self, value, axis):
        return lax.ppermute(value, axis, [(0, 1), (1, 0)])

    def plane(self, value, k):
        if k == 3:
            return lax.ppermute(value, ("rep", "seq"), [(i, 3 - i) for i in range(4)])
        return self.swap(value, "rep" if k == 1 else "seq")

    def gather(self, value):
        return [value] + [self.shift(value, k) for k in range(1, GROUPS)]

    def scatter_sum(self, parts):
        total = parts[0]
        for k in range(1, GROUPS):
            total = total + self.shift(parts[k].astype(BF), -k).astype(F32)
        return total

    def exchange(self, pieces):
        own = lax.dynamic_index_in_dim(pieces, self.group, 0, keepdims=False)
        out = [own]
        for k in range(1, GROUPS):
            target = (self.group + k) % GROUPS
            out.append(
                self.shift(lax.dynamic_index_in_dim(pieces, target, 0, keepdims=False), k)
            )
        return out

    def ordered(self, relative):
        line = [relative[0], relative[3], relative[2], relative[1]]
        twice = jnp.stack(line + line[:3])
        return lax.dynamic_slice_in_dim(twice, (GROUPS - self.group) % GROUPS, GROUPS, 0)

    def both_seq(self, value):
        other = self.swap(value, "seq")
        first = self.seq == 0
        return jnp.stack([jnp.where(first, value, other), jnp.where(first, other, value)])

    def partner(self, value):
        return lax.ppermute(
            value, "ctx", [(i, i ^ 1) for i in range(self.size)]
        )

    def all_members(self, value, axis):
        if self.members == 2:
            other = self.partner(value)
            first = self.member == 0
            return jnp.stack(
                [jnp.where(first, value, other), jnp.where(first, other, value)], axis
            )
        out = lax.all_gather(value, "ctx", axis_index_groups=self.inner)
        return jnp.moveaxis(out, 0, axis)

    def member_sum(self, pieces):
        if self.members == 2:
            keep = lax.dynamic_index_in_dim(pieces, self.member, 0, keepdims=False)
            give = lax.dynamic_index_in_dim(pieces, 1 - self.member, 0, keepdims=False)
            return keep + self.partner(give.astype(BF)).astype(F32)
        got = lax.all_to_all(
            pieces.astype(BF), "ctx", 0, 0, axis_index_groups=self.inner, tiled=True
        )
        return jnp.sum(got.astype(F32), axis=0)

    def seq_sum(self, pieces):
        keep = lax.dynamic_index_in_dim(pieces, self.seq, 0, keepdims=False)
        give = lax.dynamic_index_in_dim(pieces, 1 - self.seq, 0, keepdims=False)
        return keep + self.swap(give.astype(BF), "seq").astype(F32)

    def rep_sum(self, value):
        low = value.astype(BF)
        return low.astype(F32) + self.swap(low, "rep").astype(F32)


def on_device(
    tokens,
    segments,
    joined_weight,
    query_bias,
    value_bias,
    output_weight,
    output_bias,
    first_gain,
    first_shift,
    widen_weight,
    widen_bias,
    narrow_weight,
    narrow_bias,
    final_gain,
    final_shift,
    cotangent,
):
    at = Layout()
    n, r = at.size, at.members
    rows, width = tokens.shape[1:]
    heads = width // HEAD_DIM
    near_heads = heads // GROUPS
    cols = near_heads * HEAD_DIM
    kb = joined_weight.shape[0]
    ff_own = narrow_weight.shape[0]
    ff = ff_own * 2 * n
    quarter = ff // GROUPS
    span = r * ff_own
    seg_row = segments[0]
    length = seg_row.shape[0]
    scale = 1.0 / math.sqrt(HEAD_DIM)
    inputs = tokens[0]

    x_rel = at.gather(inputs)
    x_four = jnp.concatenate(x_rel, axis=0)

    small = jnp.concatenate(
        [
            query_bias,
            value_bias,
            output_bias,
            first_gain,
            first_shift,
            narrow_bias,
            final_gain,
            final_shift,
            widen_bias,
        ]
    )[None]
    small_all = at.all_members(at.both_seq(at.ordered(at.gather(small))), 2)
    small_all = small_all.reshape(2 * n, -1).astype(F32)

    def vector(place):
        return small_all[:, place * kb : (place + 1) * kb].reshape(width)

    b_query, b_value, b_output, g_first, s_first, b_narrow, g_final, s_final = (
        vector(place) for place in range(8)
    )
    b_widen = lax.dynamic_index_in_dim(
        small_all[:, 8 * kb :].reshape(2, 2, GROUPS, span), at.group, 2, keepdims=False
    ).reshape(2 * quarter)
    b_query = lax.dynamic_index_in_dim(b_query.reshape(GROUPS, cols), at.group, 0, keepdims=False)
    b_value = lax.dynamic_index_in_dim(b_value.reshape(GROUPS, cols), at.group, 0, keepdims=False)

    joined_cut = jnp.transpose(joined_weight.reshape(kb, 3, GROUPS, cols), (2, 0, 1, 3)).reshape(
        GROUPS, kb, 3 * cols
    )
    w_joined = at.all_members(at.both_seq(at.ordered(at.exchange(joined_cut))), 2).reshape(
        width, 3 * cols
    )

    output_low = after(output_weight, x_four)
    out_rel = at.ordered(at.gather(output_low)).reshape(GROUPS * kb, width)
    both = at.both_seq(jnp.concatenate([out_rel, narrow_weight], axis=0))
    both = at.all_members(both, 1)
    w_output = jnp.transpose(
        both[:, :, : GROUPS * kb].reshape(2, r, GROUPS, kb, width), (0, 2, 1, 3, 4)
    ).reshape(width, width)
    w_narrow = both[:, :, GROUPS * kb :].reshape(quarter, width)

    widen_cut = jnp.transpose(
        after(widen_weight, x_four).reshape(kb, 4, GROUPS, span), (2, 0, 1, 3)
    ).reshape(GROUPS, kb, 2 * quarter)
    w_widen = at.all_members(at.both_seq(at.ordered(at.exchange(widen_cut))), 2).reshape(
        width, 2 * quarter
    )

    lanes = jnp.arange(rows, dtype=jnp.int32)
    near = (at.group - jnp.arange(GROUPS, dtype=jnp.int32)) % GROUPS

    def places(member):
        return ((near * r + member)[:, None] * rows + lanes[None]).reshape(-1)

    if r == 2:
        key_members = jnp.stack([at.member, 1 - at.member])
    else:
        key_members = jnp.arange(r, dtype=jnp.int32)
    query_pos = places(at.member)
    key_pos = jnp.concatenate([places(key_members[i]) for i in range(r)])
    query_seg = jnp.take(seg_row, query_pos)
    key_seg = jnp.take(seg_row, key_pos)
    q_info = jnp.stack([query_pos, query_seg]).astype(F32)
    k_info = jnp.stack([key_pos, key_seg]).astype(F32)
    order_heads = at.group * near_heads + jnp.arange(near_heads, dtype=jnp.int32)
    slopes = jnp.power(2.0, -8.0 * (order_heads.astype(F32) + 1.0) / heads) * (512.0 / length)

    joined = dot_nn(x_four, w_joined)
    queries = ((joined[:, :cols] + b_query) * scale).astype(BF)
    kv_own = jnp.concatenate(
        [joined[:, cols : 2 * cols], joined[:, 2 * cols :] + b_value], axis=1
    ).astype(BF)
    if r == 2:
        key_value = jnp.concatenate([kv_own, at.partner(kv_own)], axis=0)
    else:
        key_value = at.all_members(kv_own, 0).reshape(-1, 2 * cols)
    mixed_near, inv = attend_forward(slopes, queries, key_value, jnp.transpose(q_info), k_info)
    mixed_low = mixed_near.astype(BF).reshape(GROUPS, rows, cols)
    mixed_rel = [mixed_low[0]] + [at.shift(mixed_low[k], -k) for k in range(1, GROUPS)]
    mixed_rel = [mixed_rel[0], mixed_rel[3], mixed_rel[2], mixed_rel[1]]
    mixed = jnp.transpose(at.ordered(mixed_rel), (1, 0, 2)).reshape(rows, width)

    first_in = inputs.astype(F32) + dot_nn(mixed, w_output) + b_output
    first_unit, first_root = norm_stats(first_in)
    first = first_unit * g_first + s_first
    first_low = first.astype(BF)

    first_four = jnp.concatenate(at.gather(first_low), axis=0)
    gate_up = dot_nn(first_four, w_widen) + b_widen
    gate, up = gate_up[:, :quarter], gate_up[:, quarter:]
    phi_big = 0.5 * (1.0 + lax.erf(gate * math.sqrt(0.5)))
    gelu = gate * phi_big
    slope_gate = phi_big + gate * jnp.exp(-0.5 * gate * gate) * (1.0 / math.sqrt(2.0 * math.pi))
    hidden = (gelu * up).astype(BF)
    final_part = dot_nn(hidden, w_narrow).reshape(GROUPS, rows, width)
    final_in = first + at.scatter_sum([final_part[k] for k in range(GROUPS)]) + b_narrow
    final_unit, final_root = norm_stats(final_in)
    result = final_unit * g_final + s_final

    upstream = cotangent[0].astype(F32)
    final_back = norm_back(final_unit, final_root, g_final, upstream)
    final_gain_grad = jnp.sum(upstream * final_unit, axis=0)
    final_shift_grad = jnp.sum(upstream, axis=0)
    narrow_back = final_back.astype(BF)
    narrow_bias_grad = jnp.sum(narrow_back.astype(F32), axis=0)
    back_four = jnp.concatenate(at.gather(narrow_back), axis=0)
    hidden_back = dot_nt(back_four, w_narrow)
    widen_back = jnp.concatenate(
        [hidden_back * up * slope_gate, hidden_back * gelu], axis=1
    ).astype(BF)
    first_part = dot_nt(widen_back, w_widen).reshape(GROUPS, rows, width)
    first_back = final_back + at.scatter_sum([first_part[k] for k in range(GROUPS)])
    narrow_grad = dot_tn(hidden, back_four)
    widen_grad = dot_tn(first_four, widen_back)
    widen_bias_grad = jnp.sum(widen_back.astype(F32), axis=0)

    attn_back = norm_back(first_unit, first_root, g_first, first_back)
    first_gain_grad = jnp.sum(first_back * first_unit, axis=0)
    first_shift_grad = jnp.sum(first_back, axis=0)
    output_back = attn_back.astype(BF)
    output_bias_grad = jnp.sum(output_back.astype(F32), axis=0)
    output_grad = dot_tn(mixed, output_back)
    mixed_back = dot_nt(output_back, w_output).astype(BF)
    mixed_back = jnp.transpose(mixed_back.reshape(rows, GROUPS, cols), (1, 0, 2))
    back_near = jnp.concatenate(at.exchange(mixed_back), axis=0)

    query_sum, kv_sum = attend_backward(
        slopes, queries, back_near, mixed_near, inv, key_value, q_info, jnp.transpose(k_info)
    )
    if r == 2:
        half = kv_sum.shape[0] // 2
        kv_back = kv_sum[:half] + at.partner(kv_sum[half:].astype(BF)).astype(F32)
    else:
        kv_back = at.member_sum(kv_sum.reshape(r, -1, 2 * cols))
    query_low = query_sum.astype(BF)
    query_scaled = (query_low.astype(F32) * scale).astype(BF)
    joined_back = jnp.concatenate([query_scaled, kv_back.astype(BF)], axis=1)
    tokens_part = dot_nt(joined_back, w_joined).reshape(GROUPS, rows, width)
    tokens_grad = attn_back + at.scatter_sum([tokens_part[k] for k in range(GROUPS)])
    joined_grad = dot_tn(x_four, joined_back)
    near_bias = jnp.sum(joined_back.astype(F32), axis=0)
    query_bias_grad = near_bias[:cols]
    value_bias_grad = near_bias[2 * cols :]

    narrow_sum = at.member_sum(jnp.transpose(narrow_grad.reshape(2, r, ff_own, width), (1, 0, 2, 3)))
    narrow_total = at.rep_sum(at.seq_sum(narrow_sum))

    def to_rows(grad):
        pieces = jnp.transpose(grad.reshape(2, GROUPS, r, kb, -1), (2, 0, 1, 3, 4))
        mine = at.rep_sum(at.seq_sum(at.member_sum(pieces))).astype(BF)
        return at.ordered(at.exchange(mine))

    widen_total = jnp.transpose(
        to_rows(widen_grad).reshape(GROUPS, kb, 4, span), (1, 2, 0, 3)
    ).reshape(kb, 2 * ff)
    joined_total = jnp.transpose(
        to_rows(joined_grad).reshape(GROUPS, kb, 3, cols), (1, 2, 0, 3)
    ).reshape(kb, 3 * width)

    def spread(vector, parts):
        wide = jnp.zeros((parts, GROUPS, vector.shape[0] // parts), F32)
        return lax.dynamic_update_slice_in_dim(
            wide, vector.reshape(parts, 1, -1), at.group, 1
        ).reshape(-1)

    vectors = [
        spread(query_bias_grad, 1),
        spread(value_bias_grad, 1),
        output_bias_grad,
        first_gain_grad,
        first_shift_grad,
        narrow_bias_grad,
        final_gain_grad,
        final_shift_grad,
    ]
    row = jnp.concatenate(
        [item.reshape(2 * n, kb) for item in vectors]
        + [spread(widen_bias_grad, 4).reshape(2 * n, 8 * kb)],
        axis=1,
    )
    row = jnp.pad(row[:, None, :], ((0, 0), (0, 15), (0, width - 16 * kb)))
    packed = jnp.concatenate([output_grad.reshape(2 * n, kb, width), row], axis=1)
    packed = jnp.transpose(packed.reshape(2, GROUPS, r, kb + 16, width), (2, 0, 1, 3, 4))
    packed = at.seq_sum(at.member_sum(packed)).astype(BF)
    packed = at.exchange(packed)
    packed = sum(item.astype(F32) for item in packed[1:]) + packed[0].astype(F32)
    packed = at.rep_sum(packed)
    output_total = packed[:kb]
    last = packed[kb]

    def owned(place):
        return last[place * kb : (place + 1) * kb]

    return (
        result.astype(BF)[None],
        tokens_grad[None],
        joined_total.astype(F32),
        owned(0),
        owned(1),
        output_total,
        owned(2),
        owned(3),
        owned(4),
        widen_total.astype(F32),
        last[8 * kb : 16 * kb],
        narrow_total,
        owned(5),
        owned(6),
        owned(7),
    )


def vmem(shape):
    return pl.BlockSpec(shape, lambda *_: tuple(0 for _ in shape))


COSTS = {
    "pack_joined": 0,
    "assemble_joined": 0,
    "pick_widen": 0,
    "pack_widen": 0,
    "cut_joined": 0,
    "cut_wide": 0,
    "assemble_output": 0,
    "finish_tokens": 0,
    "split_joined": 3,
    "attend": 5,
    "attend_back": 8,
    "close_attention": 3,
    "widen_narrow": 6,
    "widen_narrow_back": 7,
    "turn_final": 3,
    "turn_first": 3,
    "wide_grads": 6,
    "output_grads": 3,
    "tokens_parts": 0,
    "joined_grads": 4,
    "finish_widen": 0,
    "finish_joined": 0,
}

SMEM = pl.BlockSpec(memory_space=pltpu.SMEM)


def call(body, name, inputs, outputs, scratch=(), grid=(1,), in_specs=None, out_specs=None, flops=0):
    shapes = [jax.ShapeDtypeStruct(shape, kind) for shape, kind in outputs]
    if in_specs is None:
        in_specs = [SMEM if item.ndim == 1 else vmem(item.shape) for item in inputs]
    if out_specs is None:
        out_specs = [vmem(shape) for shape, kind in outputs]
    moved = sum(item.size * item.dtype.itemsize for item in list(inputs) + shapes)
    return pl.pallas_call(
        body,
        grid=grid,
        in_specs=in_specs,
        out_specs=out_specs,
        out_shape=shapes,
        scratch_shapes=list(scratch),
        name=name,
        cost_estimate=pl.CostEstimate(flops=int(COSTS[name] * 5 * 1e9), transcendentals=0, bytes_accessed=0),
    )(*inputs)


def pack_joined(ids, weight, vectors, widen_bias, tokens, cols):
    kb = weight.shape[0]
    vectors = [item[None] for item in vectors]
    shape = (kb + 16, 3 * cols)

    def body(*refs):
        ids_ref, w_ref, wide_ref = refs[0], refs[1], refs[10]
        all_ref = refs[17]
        for g in range(GROUPS):
            refs[16][g] = refs[11][...]
        rows = [ref[...].astype(F32) for ref in refs[2:10]]
        wide = wide_ref[...].astype(F32)
        rows += [wide[:, k * kb : (k + 1) * kb] for k in range(8)]
        small = jnp.concatenate(rows, axis=0).astype(BF)
        for g in range(GROUPS):
            for part in range(3):
                at = (part * GROUPS + g) * cols
                all_ref[g, :kb, part * cols : (part + 1) * cols] = w_ref[:, at : at + cols]
            all_ref[g, kb:, :] = jnp.zeros((16, 3 * cols), BF)
            all_ref[g, kb:, :kb] = small
        for k in range(GROUPS):
            refs[12 + k][...] = all_ref[(ids_ref[0] + k) % GROUPS]

    inputs = [ids, weight] + vectors + [widen_bias[None], tokens]
    return call(
        body,
        "pack_joined",
        inputs,
        [(shape, BF)] * GROUPS + [((GROUPS,) + tokens.shape, BF)],
        scratch=[pltpu.VMEM((GROUPS,) + shape, BF)],
    )


def place_rows(ids_ref, pieces, out_ref, kb, relative=False):
    group, m, y = ids_ref[0], ids_ref[1], ids_ref[2]
    for index, piece in enumerate(pieces):
        row = y if index % 2 == 0 else 1 - y
        member = m if index < 2 else 1 - m
        for g in range(GROUPS):
            source = (group + GROUPS - g) % GROUPS if relative else g
            start = pl.multiple_of((row * GROUPS * 2 + source * 2 + member) * kb, 16)
            out_ref[pl.ds(start, kb), :] = piece[g, :kb, :]


def assemble_joined(ids, pieces, kb):
    cols = pieces[0].shape[2]
    near = cols // 3
    width = 4 * GROUPS * kb
    span = 8 * kb

    def body(ids_ref, a_ref, b_ref, c_ref, d_ref, w_ref, vec_ref, near_ref, wide_ref):
        place_rows(ids_ref, (a_ref, b_ref, c_ref, d_ref), w_ref, kb, True)
        g, m, y, x = ids_ref[0], ids_ref[1], ids_ref[2], ids_ref[3]
        blocks = []
        for row in range(2):
            for k in range(GROUPS):
                for member in range(2):
                    turn = (g + GROUPS - k) % GROUPS
                    picks = [ref[turn, kb:, :kb].astype(F32) for ref in (a_ref, b_ref, c_ref, d_ref)]
                    mine = jnp.where(row == y, picks[0], picks[1])
                    theirs = jnp.where(row == y, picks[2], picks[3])
                    blocks.append(jnp.where(member == m, mine, theirs))
        vec = jnp.concatenate(blocks, axis=1)
        vec_ref[...] = vec
        total = jnp.zeros((16, near), F32)
        for k in range(GROUPS):
            total = jnp.where(g == k, vec[:, k * near : (k + 1) * near], total)
        near_ref[...] = total
        lines = []
        for part in range(2):
            for c in range(8):
                low = 8 + (c % 2) * 4
                picks = []
                for row in range(2):
                    at = (part * 8 + row * 4 + c // 2) * kb
                    picks.append(vec[low : low + 4, at : at + kb])
                both = jnp.where(y == 0, picks[0], picks[1])
                pair = jnp.where(x == 0, both[0:2], both[2:4])
                lines += [pair[0:1], pair[1:2]]
        wide_ref[...] = jnp.concatenate(lines, axis=1)

    return call(
        body,
        "assemble_joined",
        [ids] + list(pieces),
        [((width, cols), BF), ((16, width), F32), ((16, near), F32), ((1, 4 * span), F32)],
    )


def pick_widen(ids, weight, narrow):
    kb, total = weight.shape
    own, width = narrow.shape
    half = own // 2
    side = total // 4
    count = side // own
    quarter = count * half

    wide = 2 * quarter

    def body(ids_ref, w_ref, n_ref, near_ref, far_ref, low_ref, all_ref):
        y, x = ids_ref[2], ids_ref[3]
        for row in range(2):
            for col in range(2):
                pieces = []
                for part in range(2):
                    for c in range(count):
                        at = part * 2 * side + row * side + c * own + col * half
                        pieces.append(w_ref[:, at : at + half])
                all_ref[row * 2 + col] = jnp.concatenate(pieces, axis=1)
        near_ref[...] = all_ref[y * 2 + x]
        far_ref[...] = all_ref[(1 - y) * 2 + x]
        low_ref[...] = n_ref[pl.ds(pl.multiple_of(x * half, 16), half), :]

    return call(
        body,
        "pick_widen",
        [ids, weight, narrow],
        [((kb, wide), BF), ((kb, wide), BF), ((half, width), BF)],
        scratch=[pltpu.VMEM((4, kb, wide), BF)],
    )


def pack_widen(ids, near, got, low):
    kb, cols = near.shape
    width = low.shape[1]

    def body(ids_ref, near_ref, got_ref, low_ref, out_ref):
        y = ids_ref[2]
        out_ref[pl.ds(pl.multiple_of(y * kb, 16), kb), :cols] = near_ref[...]
        out_ref[pl.ds(pl.multiple_of((1 - y) * kb, 16), kb), :cols] = got_ref[...]
        out_ref[:, cols:] = low_ref[...]

    return call(body, "pack_widen", [ids, near, got, low], [((2 * kb, cols + width), BF)])[0]


def assemble_output(weights, kb):
    width, cols = weights.shape
    half = width // (2 * kb)

    def body(all_ref, w_ref):
        for y in range(2):
            for c in range(half):
                rows = slice((c * 2 + y) * kb, (c * 2 + y + 1) * kb)
                w_ref[(y * half + c) * kb : (y * half + c + 1) * kb, :] = all_ref[rows, :]

    return call(body, "assemble_output", [weights], [((width, cols), BF)])[0]


def owner_order(value, kb):
    half = value.shape[1] // (2 * kb)
    blocks = [y * half + c for c in range(half) for y in range(2)]
    return jnp.concatenate([value[:, b * kb : (b + 1) * kb] for b in blocks], axis=1)


def column_order(value, kb):
    half = value.shape[1] // (2 * kb)
    blocks = [c * 2 + y for y in range(2) for c in range(half)]
    return jnp.concatenate([value[:, b * kb : (b + 1) * kb] for b in blocks], axis=1)


def split_joined(x_four, weight, near, scale):
    count, width = x_four.shape
    cols = weight.shape[1] // 3

    def body(x_ref, w_ref, near_ref, q_ref, kv_ref):
        joined = dot_nn(x_ref[...], w_ref[...])
        q_ref[...] = ((joined[:, :cols] + near_ref[0:1, :]) * scale).astype(BF)
        kv_ref[:, :cols] = joined[:, cols : 2 * cols].astype(BF)
        kv_ref[:, cols:] = (joined[:, 2 * cols :] + near_ref[1:2, :]).astype(BF)

    return call(
        body,
        "split_joined",
        [x_four, weight, near],
        [((count, cols), BF), ((count, 2 * cols), BF)],
        flops=2 * count * width * 3 * cols,
    )


def piece_rows(ids_ref, k, rows, sign=1):
    turn = (ids_ref[0] + (k if sign > 0 else GROUPS - k)) % GROUPS
    return pl.ds(pl.multiple_of(turn * rows, 16), rows)


def attend(ids, slopes, queries, kv_own, kv_other, q_col, k_row):
    count, cols = queries.shape
    heads = cols // HEAD_DIM
    rows = count // GROUPS
    chunk = kv_own.shape[0]

    def body(ids_ref, slope_ref, q_ref, own_ref, other_ref, qi_ref, ki_ref, out_ref, inv_ref, *sends):
        q = q_ref[...]
        qpos = qi_ref[:, 0:1]
        qseg = qi_ref[:, 1:2]
        ones = jnp.ones((chunk, 64), BF)
        q_heads = [only_head(q, head) for head in range(heads)]
        accs = [None] * heads
        for side, kv_ref in enumerate((own_ref, other_ref)):
            here = slice(side * chunk, (side + 1) * chunk)
            keys = kv_ref[:, :cols]
            values = jnp.concatenate([kv_ref[:, cols:], ones], axis=1)
            far = jnp.where(qseg == ki_ref[1:2, here], jnp.abs(qpos - ki_ref[0:1, here]), FAR)
            for head in range(heads):
                scores = dot_nt(q_heads[head], keys) - slope_ref[head] * far
                part = dot_nn(jnp.exp(scores).astype(BF), values)
                accs[head] = part if side == 0 else accs[head] + part
        total = jnp.zeros((count, cols), F32)
        for head in range(heads):
            inv = 1.0 / accs[head][:, cols : cols + 1]
            inv_ref[head] = jnp.transpose(jnp.broadcast_to(inv, (count, 128)))[:8]
            total = total + only_head(accs[head][:, :cols] * inv, head)
        out_ref[...] = total
        for k, ref in enumerate(sends):
            ref[...] = out_ref[piece_rows(ids_ref, k, rows), :].astype(BF)

    return call(
        body,
        "attend",
        [ids, slopes, queries, kv_own, kv_other, q_col, k_row],
        [((count, cols), F32), ((heads, 8, count), F32)] + [((rows, cols), BF)] * GROUPS,
        flops=4 * count * 2 * chunk * cols,
    )


def attend_back(ids, slopes, queries, back_rel, mixed, inv, kv_own, kv_other, q_row, k_col, scale):
    count, cols = queries.shape
    heads = cols // HEAD_DIM
    rows = count // GROUPS
    chunk = kv_own.shape[0]

    def body(ids_ref, slope_ref, q_ref, *refs):
        pieces = refs[:GROUPS]
        out_ref, inv_ref, own_ref, other_ref, qi_ref, ki_ref, dq_ref, keep_ref, give_ref, do_ref = refs[GROUPS:]
        for k, ref in enumerate(pieces):
            do_ref[piece_rows(ids_ref, k, rows, -1), :] = ref[...]
        q = q_ref[...]
        back = do_ref[...]
        product = back.astype(F32) * out_ref[...]
        qpos = qi_ref[0:1, :]
        qseg = qi_ref[1:2, :]
        q_heads = [only_head(q, head) for head in range(heads)]
        b_heads = [only_head(back, head) for head in range(heads)]
        place = lax.broadcasted_iota(jnp.int32, (8, cols), 0)
        lane = lax.broadcasted_iota(jnp.int32, (8, cols), 1)
        row_dots = lax.dot_general(
            (lane // HEAD_DIM == place).astype(F32),
            product,
            (((1,), (1,)), ((), ())),
            precision=lax.Precision.HIGHEST,
            preferred_element_type=F32,
        )
        query_parts = [None] * heads
        for side, kv_ref in enumerate((own_ref, other_ref)):
            here = slice(side * chunk, (side + 1) * chunk)
            keys = kv_ref[:, :cols]
            values = kv_ref[:, cols:]
            far = jnp.where(qseg == ki_ref[here, 1:2], jnp.abs(qpos - ki_ref[here, 0:1]), FAR)
            key_part = None
            value_part = None
            for head in range(heads):
                scores = dot_nt(keys, q_heads[head]) - slope_ref[head] * far
                probs = jnp.exp(scores) * inv_ref[head, 0:1, :]
                prob_back = dot_nt(values, b_heads[head])
                score_back = (probs * (prob_back - row_dots[head : head + 1])).astype(BF)
                k_part = dot_nn(score_back, q_heads[head])
                v_part = dot_nn(probs.astype(BF), b_heads[head])
                q_part = dot_tn(score_back, keys)
                key_part = k_part if head == 0 else key_part + k_part
                value_part = v_part if head == 0 else value_part + v_part
                query_parts[head] = q_part if side == 0 else query_parts[head] + q_part
            target = keep_ref if side == 0 else give_ref
            target[:, :cols] = key_part.astype(target.dtype)
            target[:, cols:] = value_part.astype(target.dtype)
        total = jnp.zeros((count, cols), F32)
        for head in range(heads):
            total = total + only_head(query_parts[head], head)
        dq_ref[...] = (total.astype(BF).astype(F32) * scale).astype(BF)

    return call(
        body,
        "attend_back",
        [ids, slopes, queries] + list(back_rel) + [mixed, inv, kv_own, kv_other, q_row, k_col],
        [((count, cols), BF), ((chunk, 2 * cols), F32), ((chunk, 2 * cols), BF)],
        scratch=[pltpu.VMEM((count, cols), BF)],
        flops=10 * count * 2 * chunk * cols,
    )


def close_attention(ids, inputs, mixed_rel, weight, vec, kb):
    rows, width = inputs.shape
    cols = mixed_rel[0].shape[1]

    def body(ids_ref, x_ref, a_ref, b_ref, c_ref, d_ref, w_ref, vec_ref, first_ref, low_ref, unit_ref, root_ref):
        total = x_ref[...].astype(F32) + vec_ref[2:3, :]
        for k, ref in enumerate((a_ref, b_ref, c_ref, d_ref)):
            total = total + dot_nn(ref[...], w_ref[piece_rows(ids_ref, k, cols, -1), :])
        unit, root = norm_stats(total)
        first = unit * vec_ref[3:4, :] + vec_ref[4:5, :]
        first_ref[...] = first
        low_ref[...] = owner_order(first, kb).astype(BF)
        unit_ref[...] = unit
        root_ref[...] = root

    return call(
        body,
        "close_attention",
        [ids, inputs] + list(mixed_rel) + [weight, vec],
        [((rows, width), F32), ((rows, width), BF), ((rows, width), F32), ((rows, 1), F32)],
        flops=2 * rows * width * width,
    )


def block_of(quarter):
    return math.gcd(quarter, 256)


def join_pieces(refs):
    return jnp.concatenate([ref[...] for ref in refs], axis=0)


def send_pieces(total, refs, rows):
    for k, ref in enumerate(refs):
        ref[...] = total[k * rows : (k + 1) * rows, :].astype(ref.dtype)


def widen_narrow(rel, weights, wide):
    rows, width = rel[0].shape
    quarter = wide.shape[1] // 2
    count = GROUPS * rows

    def body(*refs):
        w_ref, wide_ref = refs[4:6]
        hid_ref, gate_ref, up_ref = refs[10:13]
        value = join_pieces(refs[:4])
        gate = dot_nn(value, w_ref[:, :quarter]) + wide_ref[:, :quarter]
        up = dot_nn(value, w_ref[:, quarter : 2 * quarter]) + wide_ref[:, quarter:]
        gate_ref[...] = gate
        up_ref[...] = up
        hidden = (gate * (0.5 + 0.5 * lax.erf(gate * math.sqrt(0.5))) * up).astype(BF)
        hid_ref[...] = hidden
        send_pieces(dot_nn(hidden, w_ref[:, 2 * quarter :]), refs[6:10], rows)

    return call(
        body,
        "widen_narrow",
        list(rel) + [weights, wide],
        [((rows, width), F32)]
        + [((rows, width), BF)] * 3
        + [((count, quarter), BF), ((count, quarter), F32), ((count, quarter), F32)],
        flops=6 * count * width * quarter,
    )


def gate_slopes(gate, up):
    phi_big = 0.5 + 0.5 * lax.erf(gate * math.sqrt(0.5))
    slope = phi_big + gate * jnp.exp(-0.5 * gate * gate) * (1.0 / math.sqrt(2.0 * math.pi))
    return up * slope, gate * phi_big


def widen_narrow_back(rel, weights, gate_factor, up_factor):
    rows, width = rel[0].shape
    count, quarter = gate_factor.shape

    def body(*refs):
        w_ref, gf_ref, uf_ref = refs[4:7]
        bg_ref, bu_ref = refs[11:13]
        hidden_back = dot_nt(join_pieces(refs[:4]), w_ref[:, 2 * quarter :])
        gate_back = (hidden_back * gf_ref[...]).astype(BF)
        up_back = (hidden_back * uf_ref[...]).astype(BF)
        bg_ref[...] = gate_back
        bu_ref[...] = up_back
        total = dot_nt(gate_back, w_ref[:, :quarter]) + dot_nt(up_back, w_ref[:, quarter : 2 * quarter])
        send_pieces(total, refs[7:11], rows)

    return call(
        body,
        "widen_narrow_back",
        list(rel) + [weights, gate_factor, up_factor],
        [((rows, width), F32)] + [((rows, width), BF)] * 3 + [((count, quarter), BF)] * 2,
        flops=6 * count * width * quarter,
    )


def turn_final(own, received, first, upstream, vec):
    rows, width = own.shape

    def body(own_ref, a_ref, b_ref, c_ref, first_ref, up_ref, vec_ref, res_ref, back_ref, low_ref, sum_ref):
        total = first_ref[...] + vec_ref[5:6, :] + own_ref[...]
        for ref in (a_ref, b_ref, c_ref):
            total = total + ref[...].astype(F32)
        unit, root = norm_stats(total)
        gain = vec_ref[6:7, :]
        res_ref[...] = (unit * gain + vec_ref[7:8, :]).astype(BF)
        upstream = up_ref[...].astype(F32)
        back = norm_back(unit, root, gain, upstream)
        low = back.astype(BF)
        back_ref[...] = back
        low_ref[...] = low
        sum_ref[...] = jnp.zeros_like(sum_ref)
        sum_ref[0:1, :] = jnp.sum(low.astype(F32), axis=0, keepdims=True)
        sum_ref[1:2, :] = jnp.sum(upstream * unit, axis=0, keepdims=True)
        sum_ref[2:3, :] = jnp.sum(upstream, axis=0, keepdims=True)

    return call(
        body,
        "turn_final",
        [own] + list(received) + [first, upstream, vec],
        [((rows, width), BF), ((rows, width), F32), ((rows, width), BF), ((8, width), F32)],
    )


def turn_first(ids, own, received, final_back, unit, root, weight, vec, kb):
    rows, width = own.shape
    cols = width // GROUPS

    def body(ids_ref, own_ref, a_ref, b_ref, c_ref, fb_ref, unit_ref, root_ref, w_ref, vec_ref, *outs):
        attn_ref, low_ref, sum_ref = outs[:3]
        total = own_ref[...]
        for ref in (a_ref, b_ref, c_ref):
            total = total + ref[...].astype(F32)
        total = fb_ref[...] + column_order(total, kb)
        unit = unit_ref[...]
        back = norm_back(unit, root_ref[...], vec_ref[3:4, :], total)
        low = back.astype(BF)
        attn_ref[...] = back
        low_ref[...] = low
        for k, ref in enumerate(outs[3:]):
            ref[...] = dot_nt(low, w_ref[piece_rows(ids_ref, k, cols), :]).astype(BF)
        sum_ref[...] = jnp.zeros_like(sum_ref)
        sum_ref[0:1, :] = jnp.sum(low.astype(F32), axis=0, keepdims=True)
        sum_ref[1:2, :] = jnp.sum(total * unit, axis=0, keepdims=True)
        sum_ref[2:3, :] = jnp.sum(total, axis=0, keepdims=True)

    return call(
        body,
        "turn_first",
        [ids, own] + list(received) + [final_back, unit, root, weight, vec],
        [((rows, width), F32), ((rows, width), BF), ((8, width), F32)] + [((rows, cols), BF)] * GROUPS,
        flops=2 * rows * width * width,
    )


def split_rows(ids_ref, full_ref, keep_ref, give_ref, kb, lead=()):
    m, y = ids_ref[1], ids_ref[2]
    for turn in range(2):
        row = y if turn == 0 else 1 - y
        for g in range(GROUPS):
            base = (row * GROUPS + g) * 2
            mine = pl.ds(pl.multiple_of((base + m) * kb, 16), kb)
            other = pl.ds(pl.multiple_of((base + 1 - m) * kb, 16), kb)
            keep_ref[lead + (turn, g, slice(0, kb), slice(None))] = full_ref[mine, :]
            give_ref[lead + (turn, g, slice(0, kb), slice(None))] = full_ref[other, :].astype(BF)


def wide_grads(first_rel, gate_back, up_back, hidden, back_rel):
    rows, width = first_rel[0].shape
    count, quarter = gate_back.shape

    def body(*refs):
        gate_ref, up_ref, hid_ref = refs[8:11]
        out_ref, gs_ref, us_ref = refs[11:14]
        value = join_pieces(refs[:4])
        for turn, (ref, sum_ref) in enumerate(((gate_ref, gs_ref), (up_ref, us_ref))):
            back = ref[...]
            out_ref[:, turn * quarter : (turn + 1) * quarter] = dot_tn(value, back).astype(BF)
            sum_ref[...] = jnp.sum(back.astype(F32), axis=0, keepdims=True)
        out_ref[:, 2 * quarter :] = dot_tn(hid_ref[...], join_pieces(refs[4:8])).astype(BF)

    return call(
        body,
        "wide_grads",
        list(first_rel) + list(back_rel) + [gate_back, up_back, hidden],
        [((width, 2 * quarter + width), BF), ((1, quarter), F32), ((1, quarter), F32)],
        flops=6 * count * width * quarter,
    )


def place_small(ids_ref, blocks, keep_ref, give_ref, kb):
    m, y = ids_ref[1], ids_ref[2]
    for turn in range(2):
        for g in range(GROUPS):
            picked = []
            for member in range(2):
                first = jnp.where(y == 0, blocks[0][g][member], blocks[1][g][member])
                second = jnp.where(y == 0, blocks[1][g][member], blocks[0][g][member])
                picked.append(first if turn == 0 else second)
            cols = keep_ref.shape[3]
            mine = jnp.where(m == 0, picked[0], picked[1])
            other = jnp.where(m == 0, picked[1], picked[0])
            keep_ref[turn, g, kb:, :] = jnp.zeros((16, cols), F32)
            give_ref[turn, g, kb:, :] = jnp.zeros((16, cols), BF)
            keep_ref[turn, g, kb:, :kb] = mine
            give_ref[turn, g, kb:, :kb] = other.astype(BF)


def output_grads(ids, mixed_rel, back, first_sums, final_sums, gate_sum, up_sum, kb):
    rows, width = back.shape
    cols = mixed_rel[0].shape[1]

    def body(ids_ref, *refs):
        back_ref, fs_ref, ls_ref, gs_ref, us_ref, keep_ref, give_ref, small_ref, full_ref = refs[GROUPS:]
        for k, ref in enumerate(refs[:GROUPS]):
            full_ref[piece_rows(ids_ref, k, cols, -1), :] = dot_tn(ref[...], back_ref[...])
        split_rows(ids_ref, full_ref, keep_ref, give_ref, kb)
        y, x = ids_ref[2], ids_ref[3]
        sums = jnp.concatenate([fs_ref[0:3, :], ls_ref[0:3, :]], axis=0)
        wide = (gs_ref[...], us_ref[...])
        for owner in range(16):
            lines = []
            for i in range(8):
                at = ((owner % 4) * 4 + (i // 4) * 2 + i % 2) * kb
                mine = (y == (owner % 8) // 4) & (x == (i % 4) // 2)
                lines.append(jnp.where(mine, wide[owner // 8][:, at : at + kb], 0.0))
            lines = [sums[:, owner * kb : (owner + 1) * kb]] + lines + [jnp.zeros((2, kb), F32)]
            small_ref[owner] = jnp.concatenate(lines, axis=0)

    shape = (2, GROUPS, kb, width)
    return call(
        body,
        "output_grads",
        [ids] + list(mixed_rel) + [back, first_sums, final_sums, gate_sum, up_sum],
        [(shape, F32), (shape, BF), ((16, 16, kb), F32)],
        scratch=[pltpu.VMEM((width, width), F32)],
        flops=2 * rows * width * width,
    )


def tokens_parts(ids, back, weight, keep, got, far):
    count, cols = back.shape
    rows = count // GROUPS
    width = weight.shape[0]
    more = far.shape[1]
    first = pl.BlockSpec((1, GROUPS, more, width), lambda i: (0, 0, 0, 0))

    def body(jb_ref, w_ref, keep_ref, got_ref, far_ref, out_ref):
        for g in range(GROUPS):
            part = dot_nt(jb_ref[g * rows : (g + 1) * rows, :], w_ref[...])
            out_ref[g, :rows, :] = part.astype(BF)
            low = keep_ref[0, g] + got_ref[0, g].astype(F32) + far_ref[g].astype(F32)
            out_ref[g, rows:, :] = low.astype(BF)

    return call(
        body,
        "tokens_parts",
        [back, weight, keep, got, far],
        [((GROUPS, rows + more, width), BF)],
        in_specs=[vmem(back.shape), vmem(weight.shape), first, first, vmem(far.shape)],
        flops=2 * count * width * cols,
    )[0]


def finish_tokens(got, attn_back):
    rows, width = attn_back.shape
    more = got.shape[1] - rows

    def body(got_ref, attn_ref, out_ref, sum_ref):
        total = attn_ref[...]
        rest = jnp.zeros((more, width), F32)
        for g in range(GROUPS):
            total = total + got_ref[g, :rows, :].astype(F32)
            rest = rest + got_ref[g, rows:, :].astype(F32)
        out_ref[...] = total
        sum_ref[...] = rest.astype(BF)

    return call(
        body,
        "finish_tokens",
        [got, attn_back],
        [((rows, width), F32), ((more, width), BF)],
    )


def joined_grads(ids, x_four, query_back, keep, got, small, kb):
    count, width = x_four.shape
    cols = query_back.shape[1]
    wide = 3 * cols

    def body(ids_ref, x_ref, q_ref, kv_ref, got_ref, small_ref, keep_ref, give_ref, back_ref, full_ref):
        back_ref[:, :cols] = q_ref[...]
        back_ref[:, cols:] = (kv_ref[...] + got_ref[...].astype(F32)).astype(BF)
        full_ref[...] = dot_tn(x_ref[...], back_ref[...])
        split_rows(ids_ref, full_ref, keep_ref, give_ref, kb)
        g_own = ids_ref[0]
        sums = jnp.sum(back_ref[...].astype(F32), axis=0, keepdims=True)
        pair = jnp.concatenate([jnp.zeros((14, cols), F32), sums[:, :cols], sums[:, 2 * cols :]], axis=0)
        blocks = []
        for row in range(2):
            blocks.append([])
            for g in range(GROUPS):
                blocks[-1].append([])
                for member in range(2):
                    b = row * 8 + g * 2 + member
                    part = pair[:, (b % GROUPS) * kb : (b % GROUPS + 1) * kb]
                    blocks[-1][-1].append(small_ref[b] + jnp.where(g_own == b // GROUPS, part, 0.0))
        place_small(ids_ref, blocks, keep_ref, give_ref, kb)

    shape = (2, GROUPS, kb + 16, wide)
    return call(
        body,
        "joined_grads",
        [ids, x_four, query_back, keep, got, small],
        [(shape, F32), (shape, BF), ((count, wide), BF)],
        scratch=[pltpu.VMEM((width, wide), F32)],
        flops=2 * count * width * wide,
    )


def cut_wide(ids, total, kb):
    cols = total.shape[1] - 16 * kb
    width = 16 * kb

    def body(ids_ref, all_ref, side_ref, far_ref):
        y = ids_ref[2]
        side_ref[:, :cols] = all_ref[pl.ds(pl.multiple_of(y * kb, 16), kb), :cols]
        for half in range(2):
            side_ref[:, cols + half * width : cols + (half + 1) * width] = all_ref[half * kb : (half + 1) * kb, cols:]
        far_ref[...] = all_ref[pl.ds(pl.multiple_of((1 - y) * kb, 16), kb), :cols]

    return call(body, "cut_wide", [ids, total], [((kb, cols + 2 * width), BF), ((kb, cols), BF)])


def finish_widen(ids, pieces):
    kb, cols = pieces[2].shape
    width = 16 * kb
    half = 2 * kb
    quarter = cols // 2
    count = quarter // half

    def body(ids_ref, *refs):
        out_ref, narrow_ref, all_ref = refs[4:]
        y, x = ids_ref[2], ids_ref[3]
        for k in range(4):
            row = y if k < 2 else 1 - y
            col = x if k % 2 == 0 else 1 - x
            all_ref[row * 2 + col] = refs[k][:, :cols].astype(F32)
        for part in range(2):
            for row in range(2):
                picks = []
                for c in range(count):
                    for col in range(2):
                        at = part * quarter + c * half
                        picks.append(all_ref[row * 2 + col, :, at : at + half])
                at = (part * 2 + row) * 2 * quarter
                out_ref[:, at : at + 2 * quarter] = jnp.concatenate(picks, axis=1)
        for k in range(2):
            for line in range(2):
                at = (x if k == 0 else 1 - x) * half + line * kb
                rows = pl.ds(pl.multiple_of(at, 16), kb)
                narrow_ref[rows, :] = refs[k][:, cols + line * width : cols + (line + 1) * width].astype(F32)

    return call(
        body,
        "finish_widen",
        [ids] + list(pieces),
        [((kb, 8 * quarter), F32), ((2 * half, width), F32)],
        scratch=[pltpu.VMEM((4, kb, cols), F32)],
    )


def cut_joined(ids, own, got):
    shape = own.shape[1:]

    def body(ids_ref, own_ref, got_ref, *outs):
        for k, ref in enumerate(outs):
            turn = (ids_ref[0] + k) % GROUPS
            ref[...] = (own_ref[turn].astype(F32) + got_ref[turn].astype(F32)).astype(BF)

    return call(body, "cut_joined", [ids, own, got], [(shape, BF)] * GROUPS)


def finish_joined(ids, pieces, kb):
    lines, wide = pieces[0].shape
    cols = wide // 3

    def body(ids_ref, *refs):
        out_ref, small_ref, got_ref = refs[GROUPS:]
        for k in range(GROUPS):
            got_ref[(ids_ref[0] + GROUPS - k) % GROUPS] = refs[k][...]
        for g in range(GROUPS):
            for part in range(3):
                at = (part * GROUPS + g) * cols
                out_ref[:, at : at + cols] = got_ref[g, :kb, part * cols : (part + 1) * cols].astype(F32)
        small = jnp.zeros((16, wide), F32)
        for g in range(GROUPS):
            small = small + got_ref[g, kb:, :].astype(F32)
        small_ref[...] = small

    return call(
        body,
        "finish_joined",
        [ids] + list(pieces),
        [((kb, GROUPS * wide), F32), ((16, wide), F32)],
        scratch=[pltpu.VMEM((GROUPS, lines, wide), BF)],
    )


def fast_device(
    tokens,
    segments,
    joined_weight,
    query_bias,
    value_bias,
    output_weight,
    output_bias,
    first_gain,
    first_shift,
    widen_weight,
    widen_bias,
    narrow_weight,
    narrow_bias,
    final_gain,
    final_shift,
    cotangent,
):
    at = Layout()
    n, r = at.size, at.members
    rows, width = tokens.shape[1:]
    heads = width // HEAD_DIM
    near_heads = heads // GROUPS
    cols = near_heads * HEAD_DIM
    kb = joined_weight.shape[0]
    ff_own = narrow_weight.shape[0]
    quarter = 4 * ff_own
    span = 2 * ff_own
    seg_row = segments[0]
    length = seg_row.shape[0]
    scale = 1.0 / math.sqrt(HEAD_DIM)
    inputs = tokens[0]
    columns = [[g * r + m for g in range(GROUPS)] for m in range(r)]
    ids = jnp.stack([at.group, at.member, at.seq, at.rep]).astype(jnp.int32)

    def across(value):
        return lax.all_to_all(value, "ctx", 0, 0, axis_index_groups=columns, tiled=True)

    def spread_out(value):
        far = at.swap(value, "seq")
        return (value, far, at.partner(value), at.partner(far))

    packed = pack_joined(
        ids,
        joined_weight,
        [
            query_bias,
            value_bias,
            output_bias,
            first_gain,
            first_shift,
            narrow_bias,
            final_gain,
            final_shift,
        ],
        widen_bias,
        inputs,
        cols,
    )
    output_far = after(at.swap(output_weight, "seq"), packed[0])
    output_pair = jnp.where(
        at.seq == 0,
        jnp.concatenate([output_weight, output_far], axis=0),
        jnp.concatenate([output_far, output_weight], axis=0),
    )
    output_got = lax.all_gather(output_pair, "ctx", tiled=True)
    joined_rel = [packed[0]] + [at.shift(packed[k], k) for k in range(1, GROUPS)]
    x_cut = after(packed[4], *joined_rel)
    x_four = across(x_cut).reshape(-1, width)
    joined_got = jnp.stack(joined_rel)
    joined_parts = spread_out(joined_got)
    w_joined, vec, near, wide = assemble_joined(ids, joined_parts, kb)
    widen_near, widen_far, narrow_low = pick_widen(after(ids, packed[3]), widen_weight, narrow_weight)
    widen_got = at.swap(after(widen_far, *joined_rel), "seq")
    widen_all = pack_widen(ids, after(widen_near, w_joined), widen_got, narrow_low)
    w_wide = lax.all_gather(widen_all, "ctx", tiled=True)

    queries, kv_own = split_joined(x_four, w_joined, near, scale)
    kv_other = at.partner(kv_own)
    lanes = jnp.arange(rows, dtype=jnp.int32)

    def places(member):
        return ((jnp.arange(GROUPS, dtype=jnp.int32) * r + member)[:, None] * rows + lanes).reshape(-1)

    by_member = jnp.transpose(seg_row.reshape(GROUPS, r, rows), (1, 0, 2)).reshape(r, -1)

    def documents(member):
        return lax.dynamic_index_in_dim(by_member, member, 0, keepdims=False)

    q_row = jnp.stack([places(at.member), documents(at.member)]).astype(F32)
    o_row = jnp.stack([places(1 - at.member), documents(1 - at.member)]).astype(F32)
    k_row = jnp.concatenate([q_row, o_row], axis=1)
    q_col = jnp.transpose(q_row)
    k_col = jnp.transpose(k_row)
    order_heads = at.group * near_heads + jnp.arange(near_heads, dtype=jnp.int32)
    slopes = jnp.power(2.0, -8.0 * (order_heads.astype(F32) + 1.0) / heads) * (512.0 / length)
    attended = attend(ids, slopes, queries, kv_own, kv_other, q_col, k_row)
    mixed_near, inv = attended[:2]
    mixed_send = attended[2:]
    mixed_rel = [mixed_send[0]] + [at.shift(mixed_send[k], k) for k in range(1, GROUPS)]
    w_output = assemble_output(output_got, kb)

    first, first_low, first_unit, first_root = close_attention(
        ids, inputs, mixed_rel, w_output, vec, kb
    )
    first_rel = [first_low] + [at.plane(first_low, k) for k in (1, 2, 3)]
    own, s1, s2, s3, hidden, gate, up = widen_narrow(first_rel, w_wide, wide)
    received = [at.plane(s1, 1), at.plane(s2, 2), at.plane(s3, 3)]
    gate_factor, up_factor = gate_slopes(gate, up)
    result, final_back, narrow_back, final_sums = turn_final(own, received, first, cotangent[0], vec)

    back_rel = [narrow_back] + [at.plane(narrow_back, k) for k in (1, 2, 3)]
    own, s1, s2, s3, gate_back, up_back = widen_narrow_back(back_rel, w_wide, gate_factor, up_factor)
    received = [at.plane(s1, 1), at.plane(s2, 2), at.plane(s3, 3)]
    wide_grad, gate_sum, up_sum = wide_grads(
        first_rel, gate_back, up_back, hidden, back_rel
    )
    wide_sum = lax.psum_scatter(wide_grad, "ctx", tiled=True)
    turned = turn_first(ids, own, received, final_back, first_unit, first_root, w_output, vec, kb)
    attn_back, output_back, first_sums = turned[:3]
    back_send = turned[3:]
    back_near = [back_send[0]] + [at.shift(back_send[k], k) for k in range(1, GROUPS)]

    output_keep, output_give, small = output_grads(
        ids, mixed_rel, output_back, first_sums, final_sums, gate_sum, up_sum, kb
    )

    def seq_send(keep, got):
        return (keep + got.astype(F32)).astype(BF)

    output_got = at.partner(output_give)

    query_back, kv_keep, kv_give = attend_back(
        ids, slopes, queries, back_near, mixed_near, inv, kv_own, kv_other, q_row, k_col, scale
    )
    output_far = at.swap(seq_send(output_keep[1], after(output_got, query_back)[1]), "seq")
    kv_got = at.partner(kv_give)

    joined_keep, joined_give, joined_back = joined_grads(ids, x_four, query_back, kv_keep, kv_got, small, kb)
    joined_got = at.partner(joined_give)
    parts = tokens_parts(ids, joined_back, w_joined, output_keep, output_got, output_far)
    tokens_got = across(parts)
    joined_far = at.swap(seq_send(joined_keep[1], after(joined_got, parts)[1]), "seq")
    joined_sum = (joined_keep[0] + joined_got[0].astype(F32) + joined_far.astype(F32)).astype(BF)
    wide_sum = after(wide_sum, joined_got)
    side, far = cut_wide(ids, wide_sum, kb)
    widen_pieces = [side, at.plane(side, 1), at.plane(far, 2), at.plane(far, 3)]
    joined_mine = cut_joined(after(ids, *widen_pieces[1:]), joined_sum, at.swap(joined_sum, "rep"))
    widen_total, narrow_total = finish_widen(ids, widen_pieces)
    joined_total, pair = finish_joined(
        ids,
        [joined_mine[0]] + [at.shift(joined_mine[k], k) for k in range(1, GROUPS)],
        kb,
    )
    tokens_grad, output_mine = finish_tokens(tokens_got, after(attn_back, joined_mine[0]))
    output_total = output_mine.astype(F32) + at.swap(output_mine, "rep").astype(F32)
    last = pair[:, :kb]
    return (
        result[None],
        tokens_grad[None],
        joined_total,
        last[14],
        last[15],
        output_total,
        last[0],
        last[1],
        last[2],
        widen_total,
        last[6:14].reshape(-1),
        narrow_total,
        last[3],
        last[4],
        last[5],
    )


def solution(mesh):
    tokens = P(("rep", "seq"), "ctx", None)
    matrix = P(("seq", "ctx"), None)
    vector = P(("seq", "ctx"))
    near = mesh.shape["ctx"] == 2 * GROUPS and mesh.shape["rep"] == 2
    return jax.shard_map(
        fast_device if near else on_device,
        mesh=mesh,
        in_specs=(
            tokens,
            P(("rep", "seq"), None),
            matrix,
            vector,
            vector,
            matrix,
            vector,
            vector,
            vector,
            matrix,
            vector,
            matrix,
            vector,
            vector,
            vector,
            tokens,
        ),
        out_specs=(
            tokens,
            tokens,
            matrix,
            vector,
            vector,
            matrix,
            vector,
            vector,
            vector,
            matrix,
            vector,
            matrix,
            vector,
            vector,
            vector,
        ),
        check_vma=False,
    )
```
